32 devices in a mesh: dp: 16 (over z, x, core), mp: 2 (over y).
Axes of the slice: x: 2, y: 2, z: 4, core: 2. Of those that a mesh axis runs over, the one named last changes fastest.
Arguments:
- tokens: bfloat16 [16, 4096, 1024], P('dp', 'mp'), may hold values from -6 to 6
- prefix: int32 [16], P('dp'), may hold values from 0 to 4096, as said below
- init_state: float32 [16, 512, 1024], P('dp', 'mp'), may hold values from -6 to 6
- cotangent: bfloat16 [16, 4096, 1024], P('dp', 'mp'), may hold values from -6 to 6
- norm_gains: bfloat16 [3, 1024], P(None, 'dp'), may hold values from 0.25 to 1.75
- gate_bias: bfloat16 [1024], P('dp'), may hold values from -2 to 4
- rel_table: bfloat16 [32, 8], P('dp', 'mp'), may hold values from -5 to 5
- tok_in_proj: bfloat16 [1024, 4, 1024], P('dp', None, 'mp'), may hold values from -0.1875 to 0.1875
- tok_out_proj: bfloat16 [2, 1024, 1024], P(None, 'mp', 'dp'), may hold values from -2 to 2
- st_in_proj: bfloat16 [1024, 4, 1024], P('dp', None, 'mp'), may hold values from -0.1875 to 0.1875
- st_out_proj: bfloat16 [2, 1024, 1024], P(None, 'mp', 'dp'), may hold values from -2 to 2
- mlp_up: bfloat16 [1024, 4096], P('dp', 'mp'), may hold values from -0.1875 to 0.1875
- mlp_down: bfloat16 [4096, 1024], P('mp', 'dp'), may hold values from -0.09375 to 0.09375
Outputs:
- mixed: bfloat16 [16, 4096, 1024], P('dp', 'mp')
- final_state: float32 [16, 512, 1024], P('dp', 'mp')
- input_grad: float32 [16, 4096, 1024], P('dp', 'mp')
- grad_norm_gains: float32 [3, 1024], P(None, 'dp')
- grad_gate_bias: float32 [1024], P('dp')
- grad_rel_table: float32 [32, 8], P('dp', 'mp')
- grad_tok_in: float32 [1024, 4, 1024], P('dp', None, 'mp')
- grad_tok_out: float32 [2, 1024, 1024], P(None, 'mp', 'dp')
- grad_st_in: float32 [1024, 4, 1024], P('dp', None, 'mp')
- grad_st_out: float32 [2, 1024, 1024], P(None, 'mp', 'dp')
- grad_mlp_up: float32 [1024, 4096], P('dp', 'mp')
- grad_mlp_down: float32 [4096, 1024], P('mp', 'dp')
The draws below stay inside these ranges and needn't reach their ends.
Inputs may be any that keep to these rules, and one draw needn't show every extreme that they name: Some sequence has prefix 4096 and some has 0.
All inputs are finite; a program needn't handle non-finite values.
Results may differ from the reference program's by a relative error of at most 0.022.
Values may be sent and summed in bfloat16 or wider, within the bound.
A program may use at most 704 MiB of HBM per device.

```python
import jax
import jax.numpy as jnp
from jax import lax

D = 1024
H = 8
HD = 128
FF = 4096
S = 512
W = 512
BUCKETS = 32
SEQ = 4096
SEQS = 16


def draw_prefix(key, part):
    lengths = jax.random.randint(jax.random.fold_in(key, 11), (SEQS,), 0, SEQ + 1)
    order = jax.random.permutation(jax.random.fold_in(key, 12), SEQS)
    lengths = jnp.where(order == 0, SEQ, lengths)
    lengths = jnp.where(order == 1, 0, lengths)
    return lengths.astype(jnp.int32)


def block_levels(rng, dims, shards, low, largest):
    def one(axis_at, blocks):
        draws = jax.random.uniform(jax.random.fold_in(jax.random.fold_in(rng, 6), axis_at), (blocks,), jnp.float32, low / len(shards), largest / len(shards))
        return jnp.repeat(jnp.exp(draws), dims[axis_at] // blocks).reshape((-1,) + (1,) * (len(dims) - axis_at - 1))

    level = one(*shards[0])
    for cut in shards[1:]:
        level = level * one(*cut)
    return level


def bell_draw(key, dims, scale, reach, split=(), held_as=jnp.bfloat16):
    factor_of = block_levels(key, dims, split, -0.22, 0.18) if split else 1.0
    entries = jax.random.normal(key, dims, jnp.float32) * scale * factor_of
    return jnp.minimum(jnp.maximum(entries, -reach), reach).astype(held_as)


def setup_inputs(seed: int = 0) -> dict:
    streams_of = jax.random.split(jax.random.key(seed), 14)
    tokens = bell_draw(streams_of[0], (SEQS, SEQ, D), 1.0, 6.0, ((0, 16), (1, 2)))
    prefix = draw_prefix(jax.random.fold_in(streams_of[13], 71), 0)
    init_state = bell_draw(streams_of[2], (SEQS, S, D), 1.0, 6.0, ((0, 16), (1, 2)), jnp.float32)
    cotangent = bell_draw(streams_of[3], (SEQS, SEQ, D), 1.0, 6.0, ((0, 16), (1, 2)))
    norm_gains = jnp.clip(1.0 + 0.15 * jax.random.normal(streams_of[4], (3, D), jnp.float32), 0.25, 1.75).astype(jnp.bfloat16)
    gate_bias = jnp.clip(-2.0 + 6.0 * jax.random.uniform(streams_of[5], (D,), jnp.float32) ** block_levels(streams_of[5], (D,), ((0, 16),), -0.2, 0.2), -2.0, 4.0).astype(jnp.bfloat16)
    rel_table = bell_draw(streams_of[6], (BUCKETS, H), 1.0, 5.0, ((0, 16), (1, 2)))
    tok_in_proj = bell_draw(streams_of[7], (D, 4, D), D ** -0.5, 0.1875, ((0, 16), (2, 2)))
    tok_out_proj = bell_draw(streams_of[8], (2, D, D), 8 ** -0.5, 2.0, ((1, 2), (2, 16)))
    st_in_proj = bell_draw(streams_of[9], (D, 4, D), D ** -0.5, 0.1875, ((0, 16), (2, 2)))
    st_out_proj = bell_draw(streams_of[10], (2, D, D), 8 ** -0.5, 2.0, ((1, 2), (2, 16)))
    mlp_up = bell_draw(streams_of[11], (D, FF), D ** -0.5, 0.1875, ((0, 16), (1, 2)))
    mlp_down = bell_draw(streams_of[12], (FF, D), FF ** -0.5, 0.09375, ((0, 2), (1, 16)))
    return {"tokens": tokens, "prefix": prefix, "init_state": init_state, "cotangent": cotangent, "norm_gains": norm_gains, "gate_bias": gate_bias, "rel_table": rel_table, "tok_in_proj": tok_in_proj, "tok_out_proj": tok_out_proj, "st_in_proj": st_in_proj, "st_out_proj": st_out_proj, "mlp_up": mlp_up, "mlp_down": mlp_down}


EPS = 1e-06
NEG = -1e+30
THRESH = (12, 16, 23, 32, 46, 64, 91)
HIGH = lax.Precision.HIGHEST

@jax.custom_vjp
def low(v):
    return lax.optimization_barrier(v.astype(jnp.bfloat16)).astype(jnp.float32)

@jax.custom_vjp
def low_back(v):
    return v

def low_keep(v):
    return (low(v), None)

def low_pass(kept, grad):
    return (grad,)

def back_keep(v):
    return (v, None)

def back_low(kept, grad):
    return (low(grad),)
low.defvjp(low_keep, low_pass)
low_back.defvjp(back_keep, back_low)

def layer_norm(values, gain):
    center = values - lax.optimization_barrier(jnp.mean(values, -1, keepdims=True))
    spread = lax.optimization_barrier(jnp.mean(center * center, -1, keepdims=True))
    return center * lax.rsqrt(spread + EPS) * gain

def bucket_ids(width, half):
    query_pos = lax.broadcasted_iota(jnp.int32, (width, 2 * width), 0) + width
    key_pos = lax.broadcasted_iota(jnp.int32, (width, 2 * width), 1)
    offset = key_pos - query_pos
    distance = jnp.abs(offset)
    far_part = jnp.full((width, 2 * width), 8, jnp.int32)
    for limit in THRESH:
        far_part = far_part + (distance >= limit).astype(jnp.int32)
    magnitude = jnp.where(distance < 8, distance, far_part)
    return magnitude + half * (offset > 0).astype(jnp.int32)

def rel_bias(table, width):
    bucket_of = bucket_ids(width, table.shape[0] // 2)
    bias_all = jnp.zeros((table.shape[1], width, 2 * width), table.dtype)
    for entry in range(table.shape[0]):
        picked = jnp.where(bucket_of == entry, 1.0, 0.0).astype(table.dtype)
        bias_all = bias_all + picked[None] * table[entry][:, None, None]
    return bias_all

def window_mask(block_idx, prefix_len, width):
    query_pos = block_idx * width + lax.broadcasted_iota(jnp.int32, (width, 2 * width), 0)
    key_pos = (block_idx - 1) * width + lax.broadcasted_iota(jnp.int32, (width, 2 * width), 1)
    both_prefix = (query_pos < prefix_len) & (key_pos < prefix_len)
    return (key_pos >= 0) & ((key_pos <= query_pos) | both_prefix)

def attend_ref(queries, keys, values, bias, allowed):
    logits = jnp.einsum('nhe,mhe->hnm', queries, keys, precision=HIGH) * HD ** (-0.5)
    if bias is not None:
        logits = logits + bias
    logits = low_back(logits)
    if allowed is not None:
        logits = jnp.where(allowed[None], logits, NEG)
    probs = jax.nn.softmax(logits, axis=-1)
    result = jnp.einsum('hnm,mhe->nhe', low(probs), values, precision=HIGH)
    return low(low_back(result))

def sequence_forward(tok_rows, state_start, prefix_len, params):
    gains, gate_bias, table, tin, tout, sin, sout, w_up, w_down = params
    seq_len = tok_rows.shape[0]
    blocks = seq_len // W
    normed = low(layer_norm(tok_rows, gains[0]))
    proj = low(low_back(jnp.einsum('td,dke->tke', normed, tin, precision=HIGH)))
    proj = proj.reshape(seq_len, 4, H, HD)
    tok_q = proj[:, 0].reshape(blocks, W, H, HD)
    tok_cq = proj[:, 1].reshape(blocks, W, H, HD)
    key_blocks = proj[:, 2].reshape(blocks, W, H, HD)
    val_blocks = proj[:, 3].reshape(blocks, W, H, HD)
    zero_block = jnp.zeros((1, W, H, HD), proj.dtype)
    key_win = jnp.concatenate([jnp.concatenate([zero_block, key_blocks[:-1]], 0), key_blocks], 1)
    val_win = jnp.concatenate([jnp.concatenate([zero_block, val_blocks[:-1]], 0), val_blocks], 1)
    rel = rel_bias(table, W)
    gate = jax.nn.sigmoid(gate_bias)

    def step(state, inputs):
        q_blk, cq_blk, key_w, val_w, key_c, val_c, block_idx = inputs
        norm_s = low(layer_norm(state, gains[2]))
        st_proj = low(low_back(jnp.einsum('sd,dke->ske', norm_s, sin, precision=HIGH))).reshape(S, 4, H, HD)
        allowed = window_mask(block_idx, prefix_len, W)
        self_out = attend_ref(q_blk, key_w, val_w, rel, allowed)
        cross_out = attend_ref(cq_blk, st_proj[:, 2], st_proj[:, 3], None, None)
        st_self = attend_ref(st_proj[:, 0], st_proj[:, 2], st_proj[:, 3], None, None)
        st_cross = attend_ref(st_proj[:, 1], key_c, val_c, None, None)
        update = low_back(jnp.dot(st_self.reshape(S, D), sout[0], precision=HIGH) + jnp.dot(st_cross.reshape(S, D), sout[1], precision=HIGH))
        return (gate * state + (1.0 - gate) * update, (self_out.reshape(W, D), cross_out.reshape(W, D)))
    block_ids = jnp.arange(blocks, dtype=jnp.int32)
    final, (self_all, cross_all) = lax.scan(jax.checkpoint(step), state_start, (tok_q, tok_cq, key_win, val_win, key_blocks, val_blocks, block_ids))
    self_all = self_all.reshape(seq_len, D)
    cross_all = cross_all.reshape(seq_len, D)
    resid = tok_rows + low_back(jnp.dot(self_all, tout[0], precision=HIGH) + jnp.dot(cross_all, tout[1], precision=HIGH))
    normed2 = low(layer_norm(resid, gains[1]))
    pre_act = low_back(jnp.dot(normed2, w_up, precision=HIGH))
    act = low(jax.nn.gelu(pre_act))
    mixed = resid + low_back(jnp.dot(act, w_down, precision=HIGH))
    return (mixed, final)

def reference(tokens, prefix, init_state, cotangent, norm_gains, gate_bias, rel_table, tok_in_proj, tok_out_proj, st_in_proj, st_out_proj, mlp_up, mlp_down):
    params = tuple((w.astype(jnp.float32) for w in (norm_gains, gate_bias, rel_table, tok_in_proj, tok_out_proj, st_in_proj, st_out_proj, mlp_up, mlp_down)))

    def per_sequence(acc, inputs):
        tok_rows, state_start, prefix_len, cot_rows = inputs

        def forward(tok_f, weights):
            return sequence_forward(tok_f, state_start, prefix_len, weights)
        (mixed, final), pull = jax.vjp(forward, tok_rows.astype(jnp.float32), params)
        input_grad, grads = pull((cot_rows.astype(jnp.float32), jnp.zeros_like(final)))
        acc = jax.tree.map(lambda left, right: left + right, acc, grads)
        return (acc, (mixed.astype(jnp.bfloat16), final, input_grad))
    start_acc = jax.tree.map(jnp.zeros_like, params)
    grads, (mixed, finals, input_grads) = lax.scan(per_sequence, start_acc, (tokens, init_state, prefix, cotangent))
    return (mixed, finals, input_grads, grads[0], grads[1], grads[2], grads[3], grads[4], grads[5], grads[6], grads[7], grads[8])
```

```python
import functools

import jax
import jax.numpy as jnp
from jax import lax
from jax.experimental import pallas as pl
from jax.experimental.pallas import tpu as pltpu
from jax.sharding import PartitionSpec as P

HD = 128
S = 512
W = 512
TILE = 128

EPS = 1e-06
NEG = -1e30
THRESH = (12, 16, 23, 32, 46, 64, 91)
LOG2E = 1.4426950408889634
SCALE = HD ** (-0.5)
SCALE2 = SCALE * LOG2E
VMEM_BYTES = 60 * 1024 * 1024

GRP = ("mpl", "core")
ORIG_DP = ("dph", "core")
EVERY = ("dph", "core", "mph", "mpl")
SWAP = ("core", "mph", "mpl")

F32 = jnp.float32
BF16 = jnp.bfloat16


def regroup(arr, forward):
    ranks = lax.axis_size(("mph", "mpl"))
    half = ranks // 2
    pairs = []
    for seq in range(2):
        for rank in range(ranks):
            here = seq * ranks + rank
            there = (rank % 2) * ranks + seq * half + rank // 2
            pairs.append((here, there) if forward else (there, here))
    return lax.ppermute(arr, SWAP, pairs)


def shift(arr, step):
    half = lax.axis_size("mpl")
    size = 2 * half

    def place(rank):
        return (rank % 2) * half + rank // 2

    pairs = [(place(i), place((i + step) % size)) for i in range(size)]
    return lax.ppermute(arr, ("core", "mpl"), pairs)


def gather_rot(rows):
    size = lax.axis_size(GRP)
    return jnp.concatenate([rows] + [shift(rows, -k) for k in range(1, size)], 0)


def sum_rot(term, count):
    size = lax.axis_size(GRP)
    sent = [shift(term(k * count, count).astype(BF16), k) for k in range(1, size)]
    total = term(0, count)
    for piece in sent:
        total = total + piece.astype(F32)
    return total


def dot_nn(left, right):
    return lax.dot_general(left, right, (((1,), (0,)), ((), ())), preferred_element_type=F32)


def dot_tn(left, right):
    return lax.dot_general(left, right, (((0,), (0,)), ((), ())), preferred_element_type=F32)


def dot_nt(left, right):
    return lax.dot_general(left, right, (((1,), (1,)), ((), ())), preferred_element_type=F32)


def normalize(values):
    center = values - jnp.mean(values, -1, keepdims=True)
    spread = jnp.mean(center * center, -1, keepdims=True)
    inv = lax.rsqrt(spread + EPS)
    return center * inv, inv


def norm_back(grad, gain, unit, inv):
    scaled = grad * gain
    mean_g = jnp.mean(scaled, -1, keepdims=True)
    mean_x = jnp.mean(scaled * unit, -1, keepdims=True)
    return inv * (scaled - mean_g - unit * mean_x)


def bucket_of(offset, half):
    distance = jnp.abs(offset)
    far_part = jnp.full(offset.shape, 8, jnp.int32)
    for limit in THRESH:
        far_part = far_part + (distance >= limit).astype(jnp.int32)
    magnitude = jnp.where(distance < 8, distance, far_part)
    return magnitude + half * (offset > 0).astype(jnp.int32)


def window_bias(table):
    key_pos = lax.broadcasted_iota(jnp.int32, (2 * W, W), 0) - W
    query_pos = lax.broadcasted_iota(jnp.int32, (2 * W, W), 1)
    which = bucket_of(key_pos - query_pos, table.shape[0] // 2)
    bias = jnp.zeros((table.shape[1], 2 * W, W), F32)
    for entry in range(table.shape[0]):
        bias = jnp.where((which == entry)[None], table[entry][:, None, None], bias)
    return bias


def table_grad(cells, entries):
    heads = cells.shape[0]
    diag = lax.broadcasted_iota(jnp.int32, (3, TILE, TILE), 0) - 1
    key_pos = lax.broadcasted_iota(jnp.int32, (3, TILE, TILE), 1)
    query_pos = lax.broadcasted_iota(jnp.int32, (3, TILE, TILE), 2)
    which = bucket_of(diag * TILE + key_pos - query_pos, entries // 2)
    rows = lax.broadcasted_iota(jnp.int32, (entries, 1, 1, 1), 0)
    hot = (which[None] == rows).astype(F32)
    near = jnp.stack(
        [jnp.sum(hot * cells[h, :3][None], (1, 2, 3)) for h in range(heads)], 1
    )
    far = jnp.sum(cells[:, 3:], (2, 3))
    entry = lax.broadcasted_iota(jnp.int32, (entries, heads), 0)
    left = jnp.where(entry == entries // 2 - 1, far[:, 0][None], 0.0)
    right = jnp.where(entry == entries - 1, far[:, 1][None], 0.0)
    return near + left + right


def reach_of(block, prefix):
    query = block * W + lax.broadcasted_iota(jnp.int32, (1, W), 1)
    return jnp.where(query < prefix, jnp.maximum(query, prefix - 1), query)


def allowed_keys(block, prefix):
    key = block * W + lax.broadcasted_iota(jnp.int32, (W, W), 0)
    return key <= reach_of(block, prefix)


def soft_unit(logits, values):
    top = jnp.max(logits[0], 0, keepdims=True)
    for part in logits[1:]:
        top = jnp.maximum(top, jnp.max(part, 0, keepdims=True))
    total = None
    acc = None
    for part, vals in zip(logits, values):
        expo = jnp.exp2(part - top)
        summed = jnp.sum(expo, 0, keepdims=True)
        mixed = dot_tn(vals, expo.astype(BF16))
        total = summed if total is None else total + summed
        acc = mixed if acc is None else acc + mixed
    return jnp.transpose(acc / total).astype(BF16), top + jnp.log2(total)


def row_dot(grad_out, out):
    prod = grad_out.astype(F32) * out.astype(F32)
    return jnp.sum(jnp.transpose(prod), 0, keepdims=True)


def back_unit(logits, queries, keys, values, grad_out, lse, delta):
    probs = jnp.exp2(logits - lse)
    grad_probs = dot_nt(values, grad_out)
    grad_values = dot_nn(probs.astype(BF16), grad_out)
    grad_scores = probs * (grad_probs - delta)
    low = grad_scores.astype(BF16)
    grad_keys = dot_nn(low, queries) * SCALE
    grad_queries = dot_tn(keys, low)
    return grad_queries, grad_keys, grad_values, grad_scores


def self_forward_kernel(where, q, kp, kc, vp, vc, bias, out, lse):
    block = pl.program_id(0)
    edge = jnp.where(block == 0, NEG, 0.0)
    allowed = allowed_keys(block, where[1])
    for h in range(bias.shape[0]):
        cols = slice(h * HD, (h + 1) * HD)
        before = dot_nt(kp[:, cols], q[:, cols]) * SCALE2 + (bias[h, :W] + edge)
        here = jnp.where(allowed, dot_nt(kc[:, cols], q[:, cols]) * SCALE2 + bias[h, W:], NEG)
        out[:, cols], lse[0, h : h + 1] = soft_unit(
            (before, here), (vp[:, cols], vc[:, cols])
        )


def self_specs(blocks, local_w, order):
    def at(part, delta):
        def index(i, where):
            block = jnp.maximum(order(i) + delta, 0)
            return ((block + blocks - where[0]) % blocks, part)

        return pl.BlockSpec((W, local_w), index)

    return at


def self_forward(where, proj, bias):
    seq_len, width = proj.shape
    local_w = width // 4
    heads = bias.shape[0]
    blocks = seq_len // W
    at = self_specs(blocks, local_w, lambda i: i)
    return pl.pallas_call(
        self_forward_kernel,
        grid_spec=pltpu.PrefetchScalarGridSpec(
            num_scalar_prefetch=1,
            grid=(blocks,),
            in_specs=[
                at(0, 0),
                at(2, -1),
                at(2, 0),
                at(3, -1),
                at(3, 0),
                pl.BlockSpec(bias.shape, lambda i, where: (0, 0, 0)),
            ],
            out_specs=[
                at(0, 0),
                pl.BlockSpec((1, heads, W), lambda i, where: (i, 0, 0)),
            ],
        ),
        out_shape=[
            jax.ShapeDtypeStruct((seq_len, 2 * local_w), BF16),
            jax.ShapeDtypeStruct((blocks, heads, W), F32),
        ],
        compiler_params=pltpu.CompilerParams(vmem_limit_bytes=VMEM_BYTES),
        cost_estimate=pl.CostEstimate(
            flops=seq_len * 2 * W * local_w * 4,
            bytes_accessed=seq_len * local_w * 12 + bias.size * 4,
            transcendentals=seq_len * 2 * W * heads,
        ),
        name="self_forward",
    )(where, proj, proj, proj, proj, proj, bias)


def self_backward_kernel(
    where, q, kp, kc, vp, vc, bias, dout, out, lse, aux, grad_proj, cells, carry
):
    step = pl.program_id(0)
    block = pl.num_programs(0) - 1 - step
    edge = jnp.where(block == 0, NEG, 0.0)
    allowed = allowed_keys(block, where[1])
    heads = bias.shape[0]
    local_w = heads * HD
    tiles = W // TILE

    @pl.when(step == 0)
    def _():
        carry[...] = jnp.zeros_like(carry)
        cells[...] = jnp.zeros_like(cells)

    for h in range(heads):
        cols = slice(h * HD, (h + 1) * HD)
        vcols = slice(local_w + h * HD, local_w + (h + 1) * HD)
        delta = row_dot(dout[:, cols], out[:, cols])
        row_lse = lse[0, h : h + 1]
        before = dot_nt(kp[:, cols], q[:, cols]) * SCALE2 + (bias[h, :W] + edge)
        dq0, dk0, dv0, ds0 = back_unit(
            before, q[:, cols], kp[:, cols], vp[:, cols], dout[:, cols], row_lse, delta
        )
        here = jnp.where(allowed, dot_nt(kc[:, cols], q[:, cols]) * SCALE2 + bias[h, W:], NEG)
        dq1, dk1, dv1, ds1 = back_unit(
            here, q[:, cols], kc[:, cols], vc[:, cols], dout[:, cols], row_lse, delta
        )
        parts = {0: [], 1: [], 2: [], 3: [], 4: []}
        for kt in range(2 * tiles):
            for qt in range(tiles):
                source, row = (ds0, kt) if kt < tiles else (ds1, kt - tiles)
                cell = source[row * TILE : (row + 1) * TILE, qt * TILE : (qt + 1) * TILE]
                diag = kt - tiles - qt
                slot = diag + 1 if -1 <= diag <= 1 else (3 if diag < 0 else 4)
                parts[slot].append(cell)
        for slot, group in parts.items():
            cells[h, slot] += functools.reduce(jnp.add, group)
        grad_proj[:, cols] = (jnp.transpose(dq0 + dq1) * SCALE).astype(BF16)
        grad_proj[:, local_w + h * HD : local_w + (h + 1) * HD] = aux[:, cols]
        grad_proj[:, 2 * local_w + h * HD : 2 * local_w + (h + 1) * HD] = (
            dk1 + carry[:, cols] + aux[:, vcols].astype(F32)
        ).astype(BF16)
        grad_proj[:, 3 * local_w + h * HD : 3 * local_w + (h + 1) * HD] = (
            dv1
            + carry[:, vcols]
            + aux[:, 2 * local_w + h * HD : 2 * local_w + (h + 1) * HD].astype(F32)
        ).astype(BF16)
        carry[:, cols] = dk0
        carry[:, vcols] = dv0


def self_backward(where, proj, bias, grad_att, att, lse, aux):
    seq_len, width = proj.shape
    local_w = width // 4
    heads = bias.shape[0]
    blocks = seq_len // W

    def order(i):
        return blocks - 1 - i

    at = self_specs(blocks, local_w, order)

    def whole(i, where):
        return ((order(i) + blocks - where[0]) % blocks, 0)

    return pl.pallas_call(
        self_backward_kernel,
        grid_spec=pltpu.PrefetchScalarGridSpec(
            num_scalar_prefetch=1,
            grid=(blocks,),
            in_specs=[
                at(0, 0),
                at(2, -1),
                at(2, 0),
                at(3, -1),
                at(3, 0),
                pl.BlockSpec(
                    bias.shape, lambda i, where: (0, 0, 0), pipeline_mode=pl.Buffered(1)
                ),
                at(0, 0),
                at(0, 0),
                pl.BlockSpec((1, heads, W), lambda i, where: (order(i), 0, 0)),
                pl.BlockSpec((W, 3 * local_w), whole),
            ],
            out_specs=[
                pl.BlockSpec((W, width), whole),
                pl.BlockSpec((heads, 5, TILE, TILE), lambda i, where: (0, 0, 0, 0)),
            ],
            scratch_shapes=[pltpu.VMEM((W, 2 * local_w), F32)],
        ),
        out_shape=[
            jax.ShapeDtypeStruct((seq_len, width), BF16),
            jax.ShapeDtypeStruct((heads, 5, TILE, TILE), F32),
        ],
        compiler_params=pltpu.CompilerParams(vmem_limit_bytes=VMEM_BYTES),
        cost_estimate=pl.CostEstimate(
            flops=seq_len * 2 * W * local_w * 10,
            bytes_accessed=seq_len * local_w * 30 + bias.size * 4,
            transcendentals=seq_len * 2 * W * heads,
        ),
        name="self_backward",
    )(where, proj, proj, proj, proj, proj, bias, grad_att, att, lse, aux)


def state_forward_kernel(first, where, *refs):
    refs = list(refs)
    prev = refs.pop(0)
    if not first:
        mine, theirs = refs.pop(0), refs.pop(0)
    gain, gate, w_in, w_out, cq, kc, vc = refs[:7]
    state, norm, sproj, satt, att, lse, part = refs[-7:]
    local_w = cq.shape[1]
    heads = local_w // HD
    if first:
        fresh = prev[...]
    else:
        update = mine[...].astype(F32) + theirs[...].astype(F32)
        fresh = gate[...] * prev[...] + (1.0 - gate[...]) * update
    state[...] = fresh
    unit, _ = normalize(fresh)
    normed = (unit * gain[...]).astype(BF16)
    norm[...] = normed
    for p in range(4):
        cols = slice(p * local_w, (p + 1) * local_w)
        sproj[:, cols] = dot_nn(normed, w_in[:, cols]).astype(BF16)
    for h in range(heads):
        cols = [slice(p * local_w + h * HD, p * local_w + (h + 1) * HD) for p in range(4)]
        sk, sv = sproj[:, cols[2]], sproj[:, cols[3]]
        satt[:, cols[0]], lse[0, h : h + 1] = soft_unit(
            (dot_nt(sk, sproj[:, cols[0]]) * SCALE2,), (sv,)
        )
        satt[:, cols[1]], lse[0, heads + h : heads + h + 1] = soft_unit(
            (dot_nt(kc[:, cols[0]], sproj[:, cols[1]]) * SCALE2,), (vc[:, cols[0]],)
        )
        att[:, cols[0]], lse[0, 2 * heads + h : 2 * heads + h + 1] = soft_unit(
            (dot_nt(sk, cq[:, cols[0]]) * SCALE2,), (sv,)
        )
    part[...] = dot_nt(satt[...], w_out[...]).astype(BF16)


def state_forward(where, block, prev, mine, theirs, gain, gate, w_in, w_out, proj, kept, att):
    first = block == 0
    seq_len, width = proj.shape
    local_w = width // 4
    heads = local_w // HD
    blocks = seq_len // W
    model = prev.shape[1]

    def phys(part):
        return pl.BlockSpec(
            (W, local_w), lambda i, where: ((where[2] + blocks - where[0]) % blocks, part)
        )

    def full(arr):
        return pl.BlockSpec(arr.shape, lambda i, where: (0,) * arr.ndim)

    def row_block(cols):
        return pl.BlockSpec((S, cols), lambda i, where: (where[2], 0))

    anywhere = pl.BlockSpec(memory_space=pl.ANY)
    operands = [prev] + ([] if first else [mine, theirs]) + [gain, gate, w_in, w_out]
    in_specs = [full(arr) for arr in operands] + [phys(1), phys(2), phys(3)]
    operands += [proj, proj, proj]
    aliases = {}
    held = [] if first else list(kept[:3])
    for slot, arr in enumerate(held):
        aliases[1 + len(operands)] = 1 + slot
        operands.append(arr)
        in_specs.append(anywhere)
    aliases[1 + len(operands)] = 4
    operands.append(att)
    in_specs.append(anywhere)
    if not first:
        aliases[1 + len(operands)] = 5
        operands.append(kept[3])
        in_specs.append(anywhere)
    return pl.pallas_call(
        functools.partial(state_forward_kernel, first),
        grid_spec=pltpu.PrefetchScalarGridSpec(
            num_scalar_prefetch=1,
            grid=(1,),
            in_specs=in_specs,
            out_specs=[
                full(prev),
                row_block(model),
                row_block(width),
                row_block(2 * local_w),
                phys(1),
                pl.BlockSpec((1, 3 * heads, S), lambda i, where: (where[2], 0, 0)),
                full(prev),
            ],
        ),
        out_shape=[
            jax.ShapeDtypeStruct(prev.shape, F32),
            jax.ShapeDtypeStruct((blocks * S, model), BF16),
            jax.ShapeDtypeStruct((blocks * S, width), BF16),
            jax.ShapeDtypeStruct((blocks * S, 2 * local_w), BF16),
            jax.ShapeDtypeStruct(att.shape, BF16),
            jax.ShapeDtypeStruct((blocks, 3 * heads, S), F32),
            jax.ShapeDtypeStruct(prev.shape, BF16),
        ],
        input_output_aliases=aliases,
        compiler_params=pltpu.CompilerParams(vmem_limit_bytes=VMEM_BYTES),
        cost_estimate=pl.CostEstimate(
            flops=S * model * local_w * 12 + 3 * S * W * local_w * 4,
            bytes_accessed=(w_in.size + w_out.size) * 2 + S * model * 20,
            transcendentals=3 * S * W * heads,
        ),
        name="state_forward",
    )(where, *operands)


def state_backward_kernel(last, where, *refs):
    refs = list(refs)
    if not last:
        later, mine, theirs, state_next, upd_mine, upd_theirs = refs[:6]
        refs = refs[6:]
    state, gain, gate, w_in, w_out, cq, kc, vc, dcross, cross, sproj, satt, lse = refs[:13]
    dstate, dupd, dsproj, aux, sums, part = refs[-6:]
    local_w = cq.shape[1]
    heads = local_w // HD
    model = state.shape[1]
    gate_f = gate[...]
    if last:
        dstate[...] = jnp.zeros_like(dstate)
        dupd[...] = jnp.zeros_like(dupd)
        gate_sum = jnp.zeros((1, model), F32)
    else:
        unit, inv = normalize(state_next[...])
        grad_norm = mine[...].astype(F32) + theirs[...].astype(F32)
        grad_state = gate_f * later[...] + norm_back(grad_norm, gain[...], unit, inv)
        dstate[...] = grad_state
        update = upd_mine[...].astype(F32) + upd_theirs[...].astype(F32)
        gate_sum = jnp.sum(grad_state * (state[...] - update), 0, keepdims=True)
        gate_sum = gate_sum * gate_f * (1.0 - gate_f)
        dupd[...] = ((1.0 - gate_f) * grad_state).astype(BF16)
    for h in range(heads):
        cols = [slice(p * local_w + h * HD, p * local_w + (h + 1) * HD) for p in range(4)]
        head = cols[0]
        sk, sv = sproj[:, cols[2]], sproj[:, cols[3]]
        delta = row_dot(dcross[:, head], cross[:, head])
        dq, dk, dv, _ = back_unit(
            dot_nt(sk, cq[:, head]) * SCALE2,
            cq[:, head],
            sk,
            sv,
            dcross[:, head],
            lse[0, 2 * heads + h : 2 * heads + h + 1],
            delta,
        )
        aux[:, cols[0]] = (jnp.transpose(dq) * SCALE).astype(BF16)
        if last:
            aux[:, cols[1]] = jnp.zeros((S, HD), BF16)
            aux[:, cols[2]] = jnp.zeros((S, HD), BF16)
            dsproj[:, cols[0]] = jnp.zeros((S, HD), BF16)
            dsproj[:, cols[1]] = jnp.zeros((S, HD), BF16)
        else:
            dself = dot_nn(dupd[...], w_out[:, cols[0]]).astype(BF16)
            dext = dot_nn(dupd[...], w_out[:, cols[1]]).astype(BF16)
            sq = sproj[:, cols[0]]
            dq, dk_s, dv_s, _ = back_unit(
                dot_nt(sk, sq) * SCALE2,
                sq,
                sk,
                sv,
                dself,
                lse[0, h : h + 1],
                row_dot(dself, satt[:, cols[0]]),
            )
            dsproj[:, cols[0]] = (jnp.transpose(dq) * SCALE).astype(BF16)
            dk = dk + dk_s
            dv = dv + dv_s
            sx = sproj[:, cols[1]]
            dq, dk_x, dv_x, _ = back_unit(
                dot_nt(kc[:, head], sx) * SCALE2,
                sx,
                kc[:, head],
                vc[:, head],
                dext,
                lse[0, heads + h : heads + h + 1],
                row_dot(dext, satt[:, cols[1]]),
            )
            dsproj[:, cols[1]] = (jnp.transpose(dq) * SCALE).astype(BF16)
            aux[:, cols[1]] = dk_x.astype(BF16)
            aux[:, cols[2]] = dv_x.astype(BF16)
        dsproj[:, cols[2]] = dk.astype(BF16)
        dsproj[:, cols[3]] = dv.astype(BF16)
    grad_norm = dot_nt(dsproj[...], w_in[...])
    part[...] = grad_norm.astype(BF16)
    unit, _ = normalize(state[...])
    sums[0:1] = jnp.sum(grad_norm * unit, 0, keepdims=True)
    sums[1:2] = gate_sum
    sums[2:] = jnp.zeros((sums.shape[0] - 2, model), F32)


def state_backward(
    where, block, chain, state, gain, gate, w_in, w_out, proj, grad_att, att, sproj, satt, lse, kept
):
    seq_len, width = proj.shape
    local_w = width // 4
    heads = local_w // HD
    blocks = seq_len // W
    last = block == blocks - 1
    model = state.shape[1]

    def phys(part):
        return pl.BlockSpec(
            (W, local_w), lambda i, where: ((where[2] + blocks - where[0]) % blocks, part)
        )

    def full(arr):
        return pl.BlockSpec(arr.shape, lambda i, where: (0,) * arr.ndim)

    def row_block(cols):
        return pl.BlockSpec((S, cols), lambda i, where: (where[2], 0))

    anywhere = pl.BlockSpec(memory_space=pl.ANY)
    operands = ([] if last else list(chain)) + [state, gain, gate, w_in, w_out]
    in_specs = [full(arr) for arr in operands]
    operands += [proj, proj, proj, grad_att, att, sproj, satt, lse]
    in_specs += [phys(1), phys(2), phys(3), phys(1), phys(1)]
    in_specs += [row_block(width), row_block(2 * local_w)]
    in_specs += [pl.BlockSpec((1, 3 * heads, S), lambda i, where: (where[2], 0, 0))]
    aliases = {}
    if not last:
        for slot, arr in enumerate(kept):
            aliases[1 + len(operands)] = 1 + slot
            operands.append(arr)
            in_specs.append(anywhere)
    return pl.pallas_call(
        functools.partial(state_backward_kernel, last),
        grid_spec=pltpu.PrefetchScalarGridSpec(
            num_scalar_prefetch=1,
            grid=(1,),
            in_specs=in_specs,
            out_specs=[
                full(state),
                row_block(model),
                row_block(width),
                pl.BlockSpec(
                    (W, 3 * local_w),
                    lambda i, where: ((where[2] + blocks - where[0]) % blocks, 0),
                ),
                pl.BlockSpec((8, model), lambda i, where: (0, 0)),
                full(state),
            ],
        ),
        out_shape=[
            jax.ShapeDtypeStruct(state.shape, F32),
            jax.ShapeDtypeStruct((blocks * S, model), BF16),
            jax.ShapeDtypeStruct((blocks * S, width), BF16),
            jax.ShapeDtypeStruct((seq_len, 3 * local_w), BF16),
            jax.ShapeDtypeStruct((8, model), F32),
            jax.ShapeDtypeStruct(state.shape, BF16),
        ],
        input_output_aliases=aliases,
        compiler_params=pltpu.CompilerParams(vmem_limit_bytes=VMEM_BYTES),
        cost_estimate=pl.CostEstimate(
            flops=S * model * local_w * 12 + 3 * S * W * local_w * 10,
            bytes_accessed=(w_in.size + w_out.size) * 2 + S * model * 40,
            transcendentals=3 * S * W * heads,
        ),
        name="state_backward",
    )(where, *operands)


def up_kernel(rows, weight, act, slope):
    step = min(512, weight.shape[1])
    root = 0.7978845608028654
    for start in range(0, weight.shape[1], step):
        cols = slice(start, start + step)
        pre = dot_nn(rows[...], weight[:, cols])
        square = pre * pre
        half = 0.5 * jnp.tanh(pre * (root + (root * 0.044715) * square)) + 0.5
        value = pre * half
        act[:, cols] = value.astype(BF16)
        rise = 2.0 * root + (6.0 * root * 0.044715) * square
        slope[:, cols] = (half + value * (1.0 - half) * rise).astype(BF16)


def up_project(rows, weight):
    count, model = rows.shape
    units = weight.shape[1]
    out = jax.ShapeDtypeStruct((count, units), BF16)
    return pl.pallas_call(
        up_kernel,
        grid=(count // W,),
        in_specs=[
            pl.BlockSpec((W, model), lambda i: (i, 0)),
            pl.BlockSpec((model, units), lambda i: (0, 0)),
        ],
        out_specs=[pl.BlockSpec((W, units), lambda i: (i, 0))] * 2,
        out_shape=[out, out],
        compiler_params=pltpu.CompilerParams(vmem_limit_bytes=VMEM_BYTES),
        cost_estimate=pl.CostEstimate(
            flops=2 * count * model * units,
            bytes_accessed=count * (model + 2 * units) * 2 + model * units * 2,
            transcendentals=count * units,
        ),
        name="up_project",
    )(rows, weight)


def gather_weight(shard):
    whole = lax.all_gather(shard.astype(BF16), ORIG_DP, axis=0, tiled=True)
    return regroup(whole, True)


def scatter_grad(grad):
    moved = regroup(grad.astype(BF16), False)
    return lax.psum_scatter(moved, ORIG_DP, scatter_dimension=0, tiled=True)


def local(
    tokens,
    prefix,
    init_state,
    cotangent,
    norm_gains,
    gate_bias,
    rel_table,
    tok_in_proj,
    tok_out_proj,
    st_in_proj,
    st_out_proj,
    mlp_up,
    mlp_down,
):
    rows = tokens.shape[1]
    model = tokens.shape[2]
    size = lax.axis_size(GRP)
    rank = lax.axis_index(GRP)
    seq_len = rows * size
    blocks = seq_len // W
    shard = tok_in_proj.shape[0]
    local_w = tok_in_proj.shape[2]
    heads = rel_table.shape[1]
    units = mlp_up.shape[1]

    tok_rows = regroup(tokens[0], True)
    w_tin = gather_weight(tok_in_proj.reshape(shard, 4 * local_w))
    start = regroup(init_state[0], True)
    state0 = lax.all_gather(start, GRP, axis=0, tiled=True)
    small = lax.all_gather(
        jnp.concatenate([norm_gains, gate_bias[None]], 0), ORIG_DP, axis=1, tiled=True
    ).astype(F32)
    table = regroup(lax.all_gather(rel_table, ORIG_DP, axis=0, tiled=True), True).astype(F32)
    prefix_len = regroup(prefix, True)
    w_sin = gather_weight(st_in_proj.reshape(shard, 4 * local_w))
    w_sout = gather_weight(st_out_proj.reshape(2 * local_w, shard).T)
    w_tout = gather_weight(tok_out_proj.reshape(2 * local_w, shard).T)
    w_up = gather_weight(mlp_up)
    w_down = gather_weight(mlp_down.T)
    cot_rows = regroup(cotangent[0], True)

    gain1, gain2, gain3 = small[0:1], small[1:2], small[2:3]
    gate = jax.nn.sigmoid(small[3:4])
    bias = window_bias(table * LOG2E)
    base = jnp.stack([rank.astype(jnp.int32) * (rows // W), prefix_len[0]])

    def where_at(block):
        return jnp.concatenate([base, jnp.full((1,), block, jnp.int32)])

    tok_f = tok_rows.astype(F32)
    unit1, inv1 = normalize(tok_f)
    normed = gather_rot((unit1 * gain1).astype(BF16))
    proj = dot_nn(normed, w_tin).astype(BF16)

    att, lse_tok = self_forward(where_at(0), proj, bias)
    states, ups = [], []
    prev, mine, theirs, kept = state0, None, None, None
    for block in range(blocks):
        outs = state_forward(
            where_at(block), block, prev, mine, theirs, gain3, gate, w_sin, w_sout, proj, kept, att
        )
        prev, norm_st, sproj, satt, att, lse_st, mine = outs
        kept = (norm_st, sproj, satt, lse_st)
        if size == 2:
            theirs = shift(mine, 1)
        else:
            theirs = lax.psum(mine.astype(F32), GRP) - mine.astype(F32)
            theirs = theirs.astype(BF16)
        states.append(prev)
        ups.append((mine, theirs))
    final = gate * prev + (1.0 - gate) * (mine.astype(F32) + theirs.astype(F32))
    final_rows = lax.dynamic_slice_in_dim(final, rank * (S // size), S // size, 0)

    def attn_term(first, count):
        return dot_nt(lax.slice_in_dim(att, first, first + count, axis=0), w_tout)

    resid = tok_f + sum_rot(attn_term, rows)
    unit2, inv2 = normalize(resid)
    normed2 = gather_rot((unit2 * gain2).astype(BF16))
    act, slope = up_project(normed2, w_up)

    def mlp_term(first, count):
        return dot_nt(lax.slice_in_dim(act, first, first + count, axis=0), w_down)

    mixed = (resid + sum_rot(mlp_term, rows)).astype(BF16)

    cot_all = gather_rot(cot_rows)
    grad_pre = (dot_nn(cot_all, w_down) * slope.astype(F32)).astype(BF16)
    grad_down = scatter_grad(dot_tn(cot_all, act))

    def up_term(first, count):
        return dot_nt(lax.slice_in_dim(grad_pre, first, first + count, axis=0), w_up)

    grad_norm2 = sum_rot(up_term, rows)
    grad_up = scatter_grad(dot_tn(normed2, grad_pre))
    grad_gain2 = jnp.sum(grad_norm2 * unit2, 0)
    grad_resid = cot_rows.astype(F32) + norm_back(grad_norm2, gain2, unit2, inv2)
    grad_attn = gather_rot(grad_resid.astype(BF16))
    grad_att = dot_nn(grad_attn, w_tout).astype(BF16)
    grad_tout = scatter_grad(dot_tn(grad_attn, att))

    chain, kept_b, sums = None, None, []
    for block in reversed(range(blocks)):
        outs = state_backward(
            where_at(block),
            block,
            chain,
            states[block],
            gain3,
            gate,
            w_sin,
            w_sout,
            proj,
            grad_att,
            att,
            sproj,
            satt,
            lse_st,
            kept_b,
        )
        later, dupd, dsproj, aux, sum_b, part = outs
        kept_b = (dupd, dsproj, aux)
        sums.append(sum_b)
        if block > 0:
            if size == 2:
                other = shift(part, 1)
            else:
                other = (lax.psum(part.astype(F32), GRP) - part.astype(F32)).astype(BF16)
            chain = (later, part, other, states[block]) + ups[block - 1]
    small_sum = functools.reduce(jnp.add, sums)
    grad_sin = scatter_grad(dot_tn(norm_st, dsproj))
    grad_sout = scatter_grad(dot_tn(dupd, satt))

    grad_proj, cells = self_backward(where_at(0), proj, bias, grad_att, att, lse_tok, aux)

    def tok_term(first, count):
        return dot_nt(lax.slice_in_dim(grad_proj, first, first + count, axis=0), w_tin)

    grad_norm1 = sum_rot(tok_term, rows)
    grad_tin = scatter_grad(dot_tn(normed, grad_proj))
    grad_gain1 = jnp.sum(grad_norm1 * unit1, 0)
    input_grad = grad_resid + norm_back(grad_norm1, gain1, unit1, inv1)

    gate_grad = small_sum[1] / size
    gains = jnp.stack([grad_gain1, grad_gain2, small_sum[0], gate_grad])
    grad_table = table_grad(cells, table.shape[0])
    placed = lax.dynamic_update_slice(
        jnp.zeros((table.shape[0], heads * size), F32), grad_table, (0, rank * heads)
    )
    packed = lax.psum(jnp.concatenate([gains.reshape(-1), placed.reshape(-1)]), EVERY)
    gains = packed[: 4 * model].reshape(4, model)
    placed = packed[4 * model :].reshape(placed.shape)
    dp_at = lax.axis_index(ORIG_DP)
    mp_at = lax.axis_index(("mph", "mpl"))
    cols = norm_gains.shape[1]
    gains = lax.dynamic_slice_in_dim(gains, dp_at * cols, cols, 1)
    entries = rel_table.shape[0]
    grad_table = lax.dynamic_slice(placed, (dp_at * entries, mp_at * heads), (entries, heads))

    return (
        regroup(mixed, False)[None],
        regroup(final_rows, False)[None],
        regroup(input_grad.astype(BF16), False).astype(F32)[None],
        gains[:3],
        gains[3],
        grad_table,
        grad_tin.astype(F32).reshape(shard, 4, local_w),
        grad_tout.T.astype(F32).reshape(2, local_w, shard),
        grad_sin.astype(F32).reshape(shard, 4, local_w),
        grad_sout.T.astype(F32).reshape(2, local_w, shard),
        grad_up.astype(F32),
        grad_down.T.astype(F32),
    )


def solution(mesh):
    devs = mesh.devices
    dp_n, mp_n = devs.shape
    fine = jax.sharding.Mesh(
        devs.reshape(dp_n // 2, 2, 2, mp_n // 2), ("dph", "core", "mph", "mpl")
    )
    dp, mp = ("dph", "core"), ("mph", "mpl")
    weights = (
        P(None, dp),
        P(dp),
        P(dp, mp),
        P(dp, None, mp),
        P(None, mp, dp),
        P(dp, None, mp),
        P(None, mp, dp),
        P(dp, mp),
        P(mp, dp),
    )
    rows = P(dp, mp, None)
    return jax.shard_map(
        local,
        mesh=fine,
        in_specs=(rows, P(dp), rows, rows) + weights,
        out_specs=(rows, rows, rows) + weights,
        check_vma=False,
    )
```

```python
import functools

import jax
import jax.numpy as jnp
from jax import lax
from jax.experimental import pallas as pl
from jax.experimental.pallas import tpu as pltpu
from jax.sharding import PartitionSpec as P

HD = 128
S = 512
W = 512
TILE = 128
EXTRA = 128

EPS = 1e-06
NEG = -1e30
THRESH = (12, 16, 23, 32, 46, 64, 91)
LOG2E = 1.4426950408889634
SCALE = HD ** (-0.5)
SCALE2 = SCALE * LOG2E
VMEM_BYTES = 60 * 1024 * 1024

GRP = ("mpl", "core")
ORIG_DP = ("dph", "core")
SWAP = ("core", "mph", "mpl")

F32 = jnp.float32
BF16 = jnp.bfloat16


def regroup(arr, forward):
    ranks = lax.axis_size(("mph", "mpl"))
    half = ranks // 2
    pairs = []
    for seq in range(2):
        for rank in range(ranks):
            here = seq * ranks + rank
            there = (rank % 2) * ranks + seq * half + rank // 2
            if here != there:
                pairs.append((here, there) if forward else (there, here))
    moved = lax.ppermute(arr, SWAP, pairs)
    seq, rank = lax.axis_index("core"), lax.axis_index(("mph", "mpl"))
    stays = (rank % 2 == seq) & (rank == seq * half + rank // 2)
    return jnp.where(stays, arr, moved)


def shift(arr, step):
    half = lax.axis_size("mpl")
    size = 2 * half

    def place(rank):
        return (rank % 2) * half + rank // 2

    pairs = [(place(i), place((i + step) % size)) for i in range(size)]
    return lax.ppermute(arr, ("core", "mpl"), pairs)


def gather_rot(rows):
    size = lax.axis_size(GRP)
    return jnp.concatenate([rows] + [shift(rows, -k) for k in range(1, size)], 0)


def sum_rot(term, count):
    size = lax.axis_size(GRP)
    sent = [shift(term(k * count, count).astype(BF16), k) for k in range(1, size)]
    total = term(0, count)
    for piece in sent:
        total = total + piece.astype(F32)
    return total


def dot_nn(left, right):
    return lax.dot_general(left, right, (((1,), (0,)), ((), ())), preferred_element_type=F32)


def dot_tn(left, right):
    return lax.dot_general(left, right, (((0,), (0,)), ((), ())), preferred_element_type=F32)


def dot_nt(left, right):
    return lax.dot_general(left, right, (((1,), (1,)), ((), ())), preferred_element_type=F32)


def normalize(values):
    center = values - jnp.mean(values, -1, keepdims=True)
    spread = jnp.mean(center * center, -1, keepdims=True)
    inv = lax.rsqrt(spread + EPS)
    return center * inv, inv


def norm_back(grad, gain, unit, inv):
    scaled = grad * gain
    mean_g = jnp.mean(scaled, -1, keepdims=True)
    mean_x = jnp.mean(scaled * unit, -1, keepdims=True)
    return inv * (scaled - mean_g - unit * mean_x)


def bucket_of(offset, half):
    distance = jnp.abs(offset)
    far_part = jnp.full(offset.shape, 8, jnp.int32)
    for limit in THRESH:
        far_part = far_part + (distance >= limit).astype(jnp.int32)
    magnitude = jnp.where(distance < 8, distance, far_part)
    return magnitude + half * (offset > 0).astype(jnp.int32)


def window_bias(table):
    key_pos = lax.broadcasted_iota(jnp.int32, (2 * W, W), 0) - W
    query_pos = lax.broadcasted_iota(jnp.int32, (2 * W, W), 1)
    which = bucket_of(key_pos - query_pos, table.shape[0] // 2)
    bias = jnp.zeros((table.shape[1], 2 * W, W), F32)
    for entry in range(table.shape[0]):
        bias = jnp.where((which == entry)[None], table[entry][:, None, None], bias)
    return bias


def table_grad(cells, entries):
    heads = cells.shape[0]
    diag = lax.broadcasted_iota(jnp.int32, (3, TILE, TILE), 0) - 1
    key_pos = lax.broadcasted_iota(jnp.int32, (3, TILE, TILE), 1)
    query_pos = lax.broadcasted_iota(jnp.int32, (3, TILE, TILE), 2)
    which = bucket_of(diag * TILE + key_pos - query_pos, entries // 2)
    rows = lax.broadcasted_iota(jnp.int32, (entries, 1, 1, 1), 0)
    hot = (which[None] == rows).astype(F32)
    near = jnp.stack(
        [jnp.sum(hot * cells[h, :3][None], (1, 2, 3)) for h in range(heads)], 1
    )
    far = jnp.sum(cells[:, 3:], (2, 3))
    entry = lax.broadcasted_iota(jnp.int32, (entries, heads), 0)
    left = jnp.where(entry == entries // 2 - 1, far[:, 0][None], 0.0)
    right = jnp.where(entry == entries - 1, far[:, 1][None], 0.0)
    return near + left + right


def reach_of(block, prefix):
    query = block * W + lax.broadcasted_iota(jnp.int32, (1, W), 1)
    return jnp.where(query < prefix, jnp.maximum(query, prefix - 1), query)


def allowed_keys(block, prefix):
    key = block * W + lax.broadcasted_iota(jnp.int32, (W, W), 0)
    return key <= reach_of(block, prefix)


def soft_unit(logits, values):
    top = jnp.max(logits[0], 0, keepdims=True)
    for part in logits[1:]:
        top = jnp.maximum(top, jnp.max(part, 0, keepdims=True))
    total = None
    acc = None
    for part, vals in zip(logits, values):
        expo = jnp.exp2(part - top)
        summed = jnp.sum(expo, 0, keepdims=True)
        mixed = dot_tn(vals, expo.astype(BF16))
        total = summed if total is None else total + summed
        acc = mixed if acc is None else acc + mixed
    return jnp.transpose(acc / total).astype(BF16), top + jnp.log2(total)


def row_dot(grad_out, out):
    prod = grad_out.astype(F32) * out.astype(F32)
    return jnp.sum(jnp.transpose(prod), 0, keepdims=True)


def back_unit(logits, queries, keys, values, grad_out, lse, delta):
    probs = jnp.exp2(logits - lse)
    grad_probs = dot_nt(values, grad_out)
    grad_values = dot_nn(probs.astype(BF16), grad_out)
    grad_scores = probs * (grad_probs - delta)
    low = grad_scores.astype(BF16)
    grad_keys = dot_nn(low, queries) * SCALE
    grad_queries = dot_tn(keys, low)
    return grad_queries, grad_keys, grad_values, grad_scores


def self_forward_kernel(where, q, kp, kc, vp, vc, bias, out, lse):
    block = pl.program_id(0)
    edge = jnp.where(block == 0, NEG, 0.0)
    allowed = allowed_keys(block, where[1])
    for h in range(bias.shape[0]):
        cols = slice(h * HD, (h + 1) * HD)
        before = dot_nt(kp[:, cols], q[:, cols]) * SCALE2 + (bias[h, :W] + edge)
        here = jnp.where(allowed, dot_nt(kc[:, cols], q[:, cols]) * SCALE2 + bias[h, W:], NEG)
        out[:, cols], lse[0, h : h + 1] = soft_unit(
            (before, here), (vp[:, cols], vc[:, cols])
        )


def self_specs(blocks, local_w, order):
    def at(part, delta):
        def index(i, where):
            block = jnp.maximum(order(i) + delta, 0)
            return ((block + blocks - where[0]) % blocks, part)

        return pl.BlockSpec((W, local_w), index)

    return at


def self_forward(where, proj, bias):
    seq_len, width = proj.shape
    local_w = width // 4
    heads = bias.shape[0]
    blocks = seq_len // W
    at = self_specs(blocks, local_w, lambda i: i)
    return pl.pallas_call(
        self_forward_kernel,
        grid_spec=pltpu.PrefetchScalarGridSpec(
            num_scalar_prefetch=1,
            grid=(blocks,),
            in_specs=[
                at(0, 0),
                at(2, -1),
                at(2, 0),
                at(3, -1),
                at(3, 0),
                pl.BlockSpec(bias.shape, lambda i, where: (0, 0, 0)),
            ],
            out_specs=[
                at(0, 0),
                pl.BlockSpec((1, heads, W), lambda i, where: (i, 0, 0)),
            ],
        ),
        out_shape=[
            jax.ShapeDtypeStruct((seq_len, 2 * local_w), BF16),
            jax.ShapeDtypeStruct((blocks, heads, W), F32),
        ],
        compiler_params=pltpu.CompilerParams(vmem_limit_bytes=VMEM_BYTES),
        cost_estimate=pl.CostEstimate(
            flops=seq_len * 2 * W * local_w * 4,
            bytes_accessed=seq_len * local_w * 12 + bias.size * 4,
            transcendentals=seq_len * 2 * W * heads,
        ),
        name="self_forward",
    )(where, proj, proj, proj, proj, proj, bias)


def self_backward_kernel(
    where, q, kp, kc, vp, vc, bias, dout, out, lse, aux, grad_proj, cells, carry
):
    step = pl.program_id(0)
    block = pl.num_programs(0) - 1 - step
    edge = jnp.where(block == 0, NEG, 0.0)
    allowed = allowed_keys(block, where[1])
    heads = bias.shape[0]
    local_w = heads * HD
    tiles = W // TILE

    @pl.when(step == 0)
    def _():
        carry[...] = jnp.zeros_like(carry)
        cells[...] = jnp.zeros_like(cells)

    for h in range(heads):
        cols = slice(h * HD, (h + 1) * HD)
        vcols = slice(local_w + h * HD, local_w + (h + 1) * HD)
        delta = row_dot(dout[:, cols], out[:, cols])
        row_lse = lse[0, h : h + 1]
        before = dot_nt(kp[:, cols], q[:, cols]) * SCALE2 + (bias[h, :W] + edge)
        dq0, dk0, dv0, ds0 = back_unit(
            before, q[:, cols], kp[:, cols], vp[:, cols], dout[:, cols], row_lse, delta
        )
        here = jnp.where(allowed, dot_nt(kc[:, cols], q[:, cols]) * SCALE2 + bias[h, W:], NEG)
        dq1, dk1, dv1, ds1 = back_unit(
            here, q[:, cols], kc[:, cols], vc[:, cols], dout[:, cols], row_lse, delta
        )
        parts = {0: [], 1: [], 2: [], 3: [], 4: []}
        for kt in range(2 * tiles):
            for qt in range(tiles):
                source, row = (ds0, kt) if kt < tiles else (ds1, kt - tiles)
                cell = source[row * TILE : (row + 1) * TILE, qt * TILE : (qt + 1) * TILE]
                diag = kt - tiles - qt
                slot = diag + 1 if -1 <= diag <= 1 else (3 if diag < 0 else 4)
                parts[slot].append(cell)
        for slot, group in parts.items():
            cells[h, slot] += functools.reduce(jnp.add, group)
        grad_proj[:, cols] = (jnp.transpose(dq0 + dq1) * SCALE).astype(BF16)
        grad_proj[:, local_w + h * HD : local_w + (h + 1) * HD] = aux[:, cols]
        grad_proj[:, 2 * local_w + h * HD : 2 * local_w + (h + 1) * HD] = (
            dk1 + carry[:, cols] + aux[:, vcols].astype(F32)
        ).astype(BF16)
        grad_proj[:, 3 * local_w + h * HD : 3 * local_w + (h + 1) * HD] = (
            dv1
            + carry[:, vcols]
            + aux[:, 2 * local_w + h * HD : 2 * local_w + (h + 1) * HD].astype(F32)
        ).astype(BF16)
        carry[:, cols] = dk0
        carry[:, vcols] = dv0


def self_backward(where, proj, bias, grad_att, att, lse, aux):
    seq_len, width = proj.shape
    local_w = width // 4
    heads = bias.shape[0]
    blocks = seq_len // W

    def order(i):
        return blocks - 1 - i

    at = self_specs(blocks, local_w, order)

    def whole(i, where):
        return ((order(i) + blocks - where[0]) % blocks, 0)

    return pl.pallas_call(
        self_backward_kernel,
        grid_spec=pltpu.PrefetchScalarGridSpec(
            num_scalar_prefetch=1,
            grid=(blocks,),
            in_specs=[
                at(0, 0),
                at(2, -1),
                at(2, 0),
                at(3, -1),
                at(3, 0),
                pl.BlockSpec(
                    bias.shape, lambda i, where: (0, 0, 0), pipeline_mode=pl.Buffered(1)
                ),
                at(0, 0),
                at(0, 0),
                pl.BlockSpec((1, heads, W), lambda i, where: (order(i), 0, 0)),
                pl.BlockSpec((W, 3 * local_w), whole),
            ],
            out_specs=[
                pl.BlockSpec((W, width), whole),
                pl.BlockSpec((heads, 5, TILE, TILE), lambda i, where: (0, 0, 0, 0)),
            ],
            scratch_shapes=[pltpu.VMEM((W, 2 * local_w), F32)],
        ),
        out_shape=[
            jax.ShapeDtypeStruct((seq_len, width), BF16),
            jax.ShapeDtypeStruct((heads, 5, TILE, TILE), F32),
        ],
        compiler_params=pltpu.CompilerParams(vmem_limit_bytes=VMEM_BYTES),
        cost_estimate=pl.CostEstimate(
            flops=seq_len * 2 * W * local_w * 10,
            bytes_accessed=seq_len * local_w * 30 + bias.size * 4,
            transcendentals=seq_len * 2 * W * heads,
        ),
        name="self_backward",
    )(where, proj, proj, proj, proj, proj, bias, grad_att, att, lse, aux)


def state_forward_kernel(first, where, *refs):
    refs = list(refs)
    prev = refs.pop(0)
    if not first:
        mine, theirs = refs.pop(0), refs.pop(0)
    gain, gate, w_in, w_out, cq, kc, vc = refs[:7]
    state, norm, sproj, satt, att, lse, part = refs[-7:]
    local_w = cq.shape[1]
    heads = local_w // HD
    if first:
        fresh = prev[...]
    else:
        update = mine[...].astype(F32) + theirs[...].astype(F32)
        fresh = gate[...] * prev[...] + (1.0 - gate[...]) * update
    state[...] = fresh
    unit, _ = normalize(fresh)
    normed = (unit * gain[...]).astype(BF16)
    norm[...] = normed
    for p in range(4):
        cols = slice(p * local_w, (p + 1) * local_w)
        sproj[:, cols] = dot_nn(normed, w_in[:, cols]).astype(BF16)
    for h in range(heads):
        cols = [slice(p * local_w + h * HD, p * local_w + (h + 1) * HD) for p in range(4)]
        sk, sv = sproj[:, cols[2]], sproj[:, cols[3]]
        satt[:, cols[0]], lse[0, h : h + 1] = soft_unit(
            (dot_nt(sk, sproj[:, cols[0]]) * SCALE2,), (sv,)
        )
        satt[:, cols[1]], lse[0, heads + h : heads + h + 1] = soft_unit(
            (dot_nt(kc[:, cols[0]], sproj[:, cols[1]]) * SCALE2,), (vc[:, cols[0]],)
        )
        att[:, cols[0]], lse[0, 2 * heads + h : 2 * heads + h + 1] = soft_unit(
            (dot_nt(sk, cq[:, cols[0]]) * SCALE2,), (sv,)
        )
    part[...] = dot_nt(satt[...], w_out[...]).astype(BF16)


def state_forward(where, block, prev, mine, theirs, gain, gate, w_in, w_out, proj, kept, att):
    first = block == 0
    seq_len, width = proj.shape
    local_w = width // 4
    heads = local_w // HD
    blocks = seq_len // W
    model = prev.shape[1]

    def phys(part):
        return pl.BlockSpec(
            (W, local_w), lambda i, where: ((where[2] + blocks - where[0]) % blocks, part)
        )

    def full(arr):
        return pl.BlockSpec(arr.shape, lambda i, where: (0,) * arr.ndim)

    def row_block(cols):
        return pl.BlockSpec((S, cols), lambda i, where: (where[2], 0))

    anywhere = pl.BlockSpec(memory_space=pl.ANY)
    operands = [prev] + ([] if first else [mine, theirs]) + [gain, gate, w_in, w_out]
    in_specs = [full(arr) for arr in operands] + [phys(1), phys(2), phys(3)]
    operands += [proj, proj, proj]
    aliases = {}
    held = [] if first else list(kept[:3])
    for slot, arr in enumerate(held):
        aliases[1 + len(operands)] = 1 + slot
        operands.append(arr)
        in_specs.append(anywhere)
    aliases[1 + len(operands)] = 4
    operands.append(att)
    in_specs.append(anywhere)
    if not first:
        aliases[1 + len(operands)] = 5
        operands.append(kept[3])
        in_specs.append(anywhere)
    return pl.pallas_call(
        functools.partial(state_forward_kernel, first),
        grid_spec=pltpu.PrefetchScalarGridSpec(
            num_scalar_prefetch=1,
            grid=(1,),
            in_specs=in_specs,
            out_specs=[
                full(prev),
                row_block(model),
                row_block(width),
                row_block(2 * local_w),
                phys(1),
                pl.BlockSpec((1, 3 * heads, S), lambda i, where: (where[2], 0, 0)),
                full(prev),
            ],
        ),
        out_shape=[
            jax.ShapeDtypeStruct(prev.shape, F32),
            jax.ShapeDtypeStruct((blocks * S, model), BF16),
            jax.ShapeDtypeStruct((blocks * S, width), BF16),
            jax.ShapeDtypeStruct((blocks * S, 2 * local_w), BF16),
            jax.ShapeDtypeStruct(att.shape, BF16),
            jax.ShapeDtypeStruct((blocks, 3 * heads, S), F32),
            jax.ShapeDtypeStruct(prev.shape, BF16),
        ],
        input_output_aliases=aliases,
        compiler_params=pltpu.CompilerParams(vmem_limit_bytes=VMEM_BYTES),
        cost_estimate=pl.CostEstimate(
            flops=S * model * local_w * 12 + 3 * S * W * local_w * 4,
            bytes_accessed=(w_in.size + w_out.size) * 2 + S * model * 20,
            transcendentals=3 * S * W * heads,
        ),
        name="state_forward",
    )(where, *operands)


def state_backward_kernel(last, where, *refs):
    refs = list(refs)
    if not last:
        later, mine, theirs, state_next, upd_mine, upd_theirs = refs[:6]
        refs = refs[6:]
    state, gain, gate, w_in, w_out, cq, kc, vc, dcross, cross, sproj, satt, lse = refs[:13]
    dstate, dupd, dsproj, aux, sums, part = refs[-6:]
    local_w = cq.shape[1]
    heads = local_w // HD
    model = state.shape[1]
    gate_f = gate[...]
    if last:
        dstate[...] = jnp.zeros_like(dstate)
        dupd[...] = jnp.zeros_like(dupd)
        gate_sum = jnp.zeros((1, model), F32)
    else:
        unit, inv = normalize(state_next[...])
        grad_norm = mine[...].astype(F32) + theirs[...].astype(F32)
        grad_state = gate_f * later[...] + norm_back(grad_norm, gain[...], unit, inv)
        dstate[...] = grad_state
        update = upd_mine[...].astype(F32) + upd_theirs[...].astype(F32)
        gate_sum = jnp.sum(grad_state * (state[...] - update), 0, keepdims=True)
        gate_sum = gate_sum * gate_f * (1.0 - gate_f)
        dupd[...] = ((1.0 - gate_f) * grad_state).astype(BF16)
    for h in range(heads):
        cols = [slice(p * local_w + h * HD, p * local_w + (h + 1) * HD) for p in range(4)]
        head = cols[0]
        sk, sv = sproj[:, cols[2]], sproj[:, cols[3]]
        delta = row_dot(dcross[:, head], cross[:, head])
        dq, dk, dv, _ = back_unit(
            dot_nt(sk, cq[:, head]) * SCALE2,
            cq[:, head],
            sk,
            sv,
            dcross[:, head],
            lse[0, 2 * heads + h : 2 * heads + h + 1],
            delta,
        )
        aux[:, cols[0]] = (jnp.transpose(dq) * SCALE).astype(BF16)
        if last:
            aux[:, cols[1]] = jnp.zeros((S, HD), BF16)
            aux[:, cols[2]] = jnp.zeros((S, HD), BF16)
            dsproj[:, cols[0]] = jnp.zeros((S, HD), BF16)
            dsproj[:, cols[1]] = jnp.zeros((S, HD), BF16)
        else:
            dself = dot_nn(dupd[...], w_out[:, cols[0]]).astype(BF16)
            dext = dot_nn(dupd[...], w_out[:, cols[1]]).astype(BF16)
            sq = sproj[:, cols[0]]
            dq, dk_s, dv_s, _ = back_unit(
                dot_nt(sk, sq) * SCALE2,
                sq,
                sk,
                sv,
                dself,
                lse[0, h : h + 1],
                row_dot(dself, satt[:, cols[0]]),
            )
            dsproj[:, cols[0]] = (jnp.transpose(dq) * SCALE).astype(BF16)
            dk = dk + dk_s
            dv = dv + dv_s
            sx = sproj[:, cols[1]]
            dq, dk_x, dv_x, _ = back_unit(
                dot_nt(kc[:, head], sx) * SCALE2,
                sx,
                kc[:, head],
                vc[:, head],
                dext,
                lse[0, heads + h : heads + h + 1],
                row_dot(dext, satt[:, cols[1]]),
            )
            dsproj[:, cols[1]] = (jnp.transpose(dq) * SCALE).astype(BF16)
            aux[:, cols[1]] = dk_x.astype(BF16)
            aux[:, cols[2]] = dv_x.astype(BF16)
        dsproj[:, cols[2]] = dk.astype(BF16)
        dsproj[:, cols[3]] = dv.astype(BF16)
    part[...] = dot_nt(dsproj[...], w_in[...]).astype(BF16)
    sums[...] = jnp.broadcast_to(gate_sum, sums.shape)


def state_backward(
    where, block, chain, state, gain, gate, w_in, w_out, proj, grad_att, att, sproj, satt, lse, kept
):
    seq_len, width = proj.shape
    local_w = width // 4
    heads = local_w // HD
    blocks = seq_len // W
    last = block == blocks - 1
    model = state.shape[1]

    def phys(part):
        return pl.BlockSpec(
            (W, local_w), lambda i, where: ((where[2] + blocks - where[0]) % blocks, part)
        )

    def full(arr):
        return pl.BlockSpec(arr.shape, lambda i, where: (0,) * arr.ndim)

    def row_block(cols):
        return pl.BlockSpec((S, cols), lambda i, where: (where[2], 0))

    anywhere = pl.BlockSpec(memory_space=pl.ANY)
    operands = ([] if last else list(chain)) + [state, gain, gate, w_in, w_out]
    in_specs = [full(arr) for arr in operands]
    operands += [proj, proj, proj, grad_att, att, sproj, satt, lse]
    in_specs += [phys(1), phys(2), phys(3), phys(1), phys(1)]
    in_specs += [row_block(width), row_block(2 * local_w)]
    in_specs += [pl.BlockSpec((1, 3 * heads, S), lambda i, where: (where[2], 0, 0))]
    aliases = {}
    if not last:
        for slot, arr in enumerate(kept):
            aliases[1 + len(operands)] = 1 + slot
            operands.append(arr)
            in_specs.append(anywhere)
    return pl.pallas_call(
        functools.partial(state_backward_kernel, last),
        grid_spec=pltpu.PrefetchScalarGridSpec(
            num_scalar_prefetch=1,
            grid=(1,),
            in_specs=in_specs,
            out_specs=[
                full(state),
                row_block(model),
                row_block(width),
                pl.BlockSpec(
                    (W, 3 * local_w),
                    lambda i, where: ((where[2] + blocks - where[0]) % blocks, 0),
                ),
                pl.BlockSpec((8, model), lambda i, where: (0, 0)),
                full(state),
            ],
        ),
        out_shape=[
            jax.ShapeDtypeStruct(state.shape, F32),
            jax.ShapeDtypeStruct((blocks * S, model), BF16),
            jax.ShapeDtypeStruct((blocks * S, width), BF16),
            jax.ShapeDtypeStruct((seq_len, 3 * local_w), BF16),
            jax.ShapeDtypeStruct((8, model), F32),
            jax.ShapeDtypeStruct(state.shape, BF16),
        ],
        input_output_aliases=aliases,
        compiler_params=pltpu.CompilerParams(vmem_limit_bytes=VMEM_BYTES),
        cost_estimate=pl.CostEstimate(
            flops=S * model * local_w * 12 + 3 * S * W * local_w * 10,
            bytes_accessed=(w_in.size + w_out.size) * 2 + S * model * 40,
            transcendentals=3 * S * W * heads,
        ),
        name="state_backward",
    )(where, *operands)


def up_kernel(rows, weight, act, slope):
    step = min(512, weight.shape[1])
    root = 0.7978845608028654
    for start in range(0, weight.shape[1], step):
        cols = slice(start, start + step)
        pre = dot_nn(rows[...], weight[:, cols])
        square = pre * pre
        half = 0.5 * jnp.tanh(pre * (root + (root * 0.044715) * square)) + 0.5
        value = pre * half
        act[:, cols] = value.astype(BF16)
        rise = 2.0 * root + (6.0 * root * 0.044715) * square
        slope[:, cols] = (half + value * (1.0 - half) * rise).astype(BF16)


def up_project(rows, weight):
    count, model = rows.shape
    units = weight.shape[1]
    out = jax.ShapeDtypeStruct((count, units), BF16)
    return pl.pallas_call(
        up_kernel,
        grid=(count // W,),
        in_specs=[
            pl.BlockSpec((W, model), lambda i: (i, 0)),
            pl.BlockSpec((model, units), lambda i: (0, 0)),
        ],
        out_specs=[pl.BlockSpec((W, units), lambda i: (i, 0))] * 2,
        out_shape=[out, out],
        compiler_params=pltpu.CompilerParams(vmem_limit_bytes=VMEM_BYTES),
        cost_estimate=pl.CostEstimate(
            flops=2 * count * model * units,
            bytes_accessed=count * (model + 2 * units) * 2 + model * units * 2,
            transcendentals=count * units,
        ),
        name="up_project",
    )(rows, weight)


def gather_weight(shard):
    return lax.all_gather(shard, ORIG_DP, axis=0, tiled=True)


def scatter_moved(moved):
    return lax.psum_scatter(moved, ORIG_DP, scatter_dimension=0, tiled=True)


def scatter_grad(grad):
    return scatter_moved(regroup(grad.astype(BF16), False))


def local(
    tokens,
    prefix,
    init_state,
    cotangent,
    norm_gains,
    gate_bias,
    rel_table,
    tok_in_proj,
    tok_out_proj,
    st_in_proj,
    st_out_proj,
    mlp_up,
    mlp_down,
):
    rows = tokens.shape[1]
    model = tokens.shape[2]
    size = lax.axis_size(GRP)
    rank = lax.axis_index(GRP)
    seq_len = rows * size
    blocks = seq_len // W
    shard = tok_in_proj.shape[0]
    local_w = tok_in_proj.shape[2]
    heads = rel_table.shape[1]
    units = mlp_up.shape[1]

    small = jnp.concatenate([norm_gains, gate_bias[None]], 0).T
    entries = rel_table.shape[0]
    extra = jnp.zeros((shard, EXTRA), BF16)
    extra = lax.dynamic_update_slice(extra, small, (0, 0))
    extra = lax.dynamic_update_slice(extra, rel_table, (0, 4))
    tok_rows = regroup(tokens[0], True)
    wide = 4 * local_w
    shard_tin = tok_in_proj.reshape(shard, wide)
    shard_sin = st_in_proj.reshape(shard, wide)
    first = gather_weight(jnp.concatenate([shard_tin, extra], 1))
    second = jnp.concatenate([shard_sin, st_out_proj.reshape(2 * local_w, shard).T], 1)
    third = jnp.concatenate(
        [tok_out_proj.reshape(2 * local_w, shard).T, mlp_up, mlp_down.T], 1
    )
    first, tok_rows, second = lax.optimization_barrier((first, tok_rows, second))
    first = regroup(first, True)
    second = gather_weight(second)
    w_tin, extra = first[:, :wide], first[:, wide:]
    small = extra[:, :4].T.astype(F32)
    table = extra.reshape(-1, shard, EXTRA)[:, :entries, 4 : 4 + heads]
    table = table.reshape(-1, heads).astype(F32)
    start = regroup(init_state[0], True)
    if size == 2:
        other = shift(start, 1)
        state0 = jnp.where(
            rank == 0,
            jnp.concatenate([start, other], 0),
            jnp.concatenate([other, start], 0),
        )
    else:
        state0 = lax.all_gather(start, GRP, axis=0, tiled=True)
    prefix_len = regroup(prefix, True)
    gain1, gain2, gain3 = small[0:1], small[1:2], small[2:3]
    gate = jax.nn.sigmoid(small[3:4])
    bias = window_bias(table * LOG2E)
    base = jnp.stack([rank.astype(jnp.int32) * (rows // W), prefix_len[0]])

    def where_at(block):
        return jnp.concatenate([base, jnp.full((1,), block, jnp.int32)])

    tok_f = tok_rows.astype(F32)
    unit1, inv1 = normalize(tok_f)
    normed = gather_rot((unit1 * gain1).astype(BF16))
    proj = dot_nn(normed, w_tin).astype(BF16)
    proj, cotangent, second, third = lax.optimization_barrier((proj, cotangent, second, third))
    third = gather_weight(third)
    second = regroup(second, True)
    w_sin, w_sout = second[:, :wide], second[:, wide:]
    cot_rows = regroup(cotangent[0], True)

    att, lse_tok = self_forward(where_at(0), proj, bias)
    states, ups = [], []
    prev, mine, theirs, kept = state0, None, None, None
    for block in range(blocks):
        outs = state_forward(
            where_at(block), block, prev, mine, theirs, gain3, gate, w_sin, w_sout, proj, kept, att
        )
        prev, norm_st, sproj, satt, att, lse_st, mine = outs
        kept = (norm_st, sproj, satt, lse_st)
        if block == 1:
            mine, third = lax.optimization_barrier((mine, third))
        if size == 2:
            theirs = shift(mine, 1)
        else:
            theirs = lax.psum(mine.astype(F32), GRP) - mine.astype(F32)
            theirs = theirs.astype(BF16)
        states.append(prev)
        ups.append((mine, theirs))
    third = regroup(third, True)
    w_tout = third[:, : 2 * local_w]
    w_up = third[:, 2 * local_w : 2 * local_w + units]
    w_down = third[:, 2 * local_w + units :]
    final = gate * prev + (1.0 - gate) * (mine.astype(F32) + theirs.astype(F32))
    final_rows = lax.dynamic_slice_in_dim(final, rank * (S // size), S // size, 0)

    def attn_term(first, count):
        return dot_nt(lax.slice_in_dim(att, first, first + count, axis=0), w_tout)

    resid = tok_f + sum_rot(attn_term, rows)
    unit2, inv2 = normalize(resid)
    normed2 = gather_rot((unit2 * gain2).astype(BF16))
    act, slope = up_project(normed2, w_up)

    def mlp_term(first, count):
        return dot_nt(lax.slice_in_dim(act, first, first + count, axis=0), w_down)

    mixed = (resid + sum_rot(mlp_term, rows)).astype(BF16)

    cot_all = gather_rot(cot_rows)
    grad_pre = (dot_nn(cot_all, w_down) * slope.astype(F32)).astype(BF16)
    grad_down = scatter_grad(dot_tn(cot_all, act))

    def up_term(first, count):
        return dot_nt(lax.slice_in_dim(grad_pre, first, first + count, axis=0), w_up)

    grad_norm2 = sum_rot(up_term, rows)
    grad_up = scatter_grad(dot_tn(normed2, grad_pre))
    grad_resid = cot_rows.astype(F32) + norm_back(grad_norm2, gain2, unit2, inv2)
    grad_attn = gather_rot(grad_resid.astype(BF16))
    grad_att = dot_nn(grad_attn, w_tout).astype(BF16)
    grad_tout = scatter_grad(dot_tn(grad_attn, att))

    chain, kept_b, sums = None, None, []
    for block in reversed(range(blocks)):
        outs = state_backward(
            where_at(block),
            block,
            chain,
            states[block],
            gain3,
            gate,
            w_sin,
            w_sout,
            proj,
            grad_att,
            att,
            sproj,
            satt,
            lse_st,
            kept_b,
        )
        later, dupd, dsproj, aux, sum_b, part = outs
        kept_b = (dupd, dsproj, aux)
        sums.append(sum_b)
        if block > 0:
            if size == 2:
                other = shift(part, 1)
            else:
                other = (lax.psum(part.astype(F32), GRP) - part.astype(F32)).astype(BF16)
            chain = (later, part, other, states[block]) + ups[block - 1]
    gate_grad = functools.reduce(jnp.add, sums)[0]
    mixed = regroup(mixed, False)
    final_rows = regroup(final_rows, False)
    grad_st = jnp.concatenate(
        [dot_tn(norm_st, dsproj).astype(BF16), dot_tn(dupd, satt).astype(BF16)], 1
    )
    aux, grad_st, mixed, final_rows = lax.optimization_barrier(
        (aux, grad_st, mixed, final_rows)
    )
    grad_st = regroup(grad_st, False)

    grad_proj, cells = self_backward(where_at(0), proj, bias, grad_att, att, lse_tok, aux)

    def tok_term(first, count):
        return dot_nt(lax.slice_in_dim(grad_proj, first, first + count, axis=0), w_tin)

    grad_tin = dot_tn(normed, grad_proj).astype(BF16)
    grad_tin, grad_st = lax.optimization_barrier((grad_tin, grad_st))
    grad_st = scatter_moved(grad_st)
    grad_sin, grad_sout = grad_st[:, :wide], grad_st[:, wide:]
    grad_norm1 = sum_rot(tok_term, rows)
    input_grad = grad_resid + norm_back(grad_norm1, gain1, unit1, inv1)

    grad_table = table_grad(cells, table.shape[0])
    packed = jnp.zeros((model // shard, shard, EXTRA), F32)
    packed = packed.at[:, :, 0].set(gate_grad.reshape(-1, shard))
    packed = packed.at[:, :entries, 1 : 1 + heads].set(grad_table.reshape(-1, entries, heads))
    packed = scatter_grad(packed.reshape(model, EXTRA)).astype(F32)
    grad_tin = scatter_grad(grad_tin)

    def gain_sum(shard_in, grad):
        return jnp.sum(shard_in.astype(F32) * grad.astype(F32), 1)

    ranks = lax.axis_size(("mph", "mpl"))
    vectors = jnp.stack(
        [
            gain_sum(shard_tin, grad_tin),
            gain_sum(mlp_up, grad_up),
            gain_sum(shard_sin, grad_sin),
            packed[:, 0] / ranks,
        ]
    )
    if ranks == 2:
        vectors = vectors + lax.ppermute(vectors, ("mph", "mpl"), [(0, 1), (1, 0)])
    else:
        vectors = lax.psum(vectors, ("mph", "mpl"))
    gains = vectors[:3] / norm_gains.astype(F32)
    grad_table = packed[:entries, 1 : 1 + heads]

    return (
        mixed[None],
        final_rows[None],
        regroup(input_grad.astype(BF16), False).astype(F32)[None],
        gains,
        vectors[3],
        grad_table,
        grad_tin.astype(F32).reshape(shard, 4, local_w),
        grad_tout.T.astype(F32).reshape(2, local_w, shard),
        grad_sin.astype(F32).reshape(shard, 4, local_w),
        grad_sout.T.astype(F32).reshape(2, local_w, shard),
        grad_up.astype(F32),
        grad_down.T.astype(F32),
    )


def solution(mesh):
    devs = mesh.devices
    dp_n, mp_n = devs.shape
    fine = jax.sharding.Mesh(
        devs.reshape(dp_n // 2, 2, 2, mp_n // 2), ("dph", "core", "mph", "mpl")
    )
    dp, mp = ("dph", "core"), ("mph", "mpl")
    weights = (
        P(None, dp),
        P(dp),
        P(dp, mp),
        P(dp, None, mp),
        P(None, mp, dp),
        P(dp, None, mp),
        P(None, mp, dp),
        P(dp, mp),
        P(mp, dp),
    )
    rows = P(dp, mp, None)
    return jax.shard_map(
        local,
        mesh=fine,
        in_specs=(rows, P(dp), rows, rows) + weights,
        out_specs=(rows, rows, rows) + weights,
        check_vma=False,
    )
```

```python
import functools

import jax
import jax.numpy as jnp
from jax import lax
from jax.experimental import pallas as pl
from jax.experimental.pallas import tpu as pltpu
from jax.sharding import PartitionSpec as P

HD = 128
S = 512
W = 512
TILE = 128
EXTRA = 128

EPS = 1e-06
NEG = -1e30
THRESH = (12, 16, 23, 32, 46, 64, 91)
LOG2E = 1.4426950408889634
SCALE = HD ** (-0.5)
SCALE2 = SCALE * LOG2E
VMEM_BYTES = 60 * 1024 * 1024

GRP = ("mpl", "core")
ORIG_DP = ("dph", "core")
SWAP = ("core", "mph", "mpl")

F32 = jnp.float32
BF16 = jnp.bfloat16


def regroup(arr, forward):
    ranks = lax.axis_size(("mph", "mpl"))
    half = ranks // 2
    pairs = []
    for seq in range(2):
        for rank in range(ranks):
            here = seq * ranks + rank
            there = (rank % 2) * ranks + seq * half + rank // 2
            if here != there:
                pairs.append((here, there) if forward else (there, here))
    moved = lax.ppermute(arr, SWAP, pairs)
    seq, rank = lax.axis_index("core"), lax.axis_index(("mph", "mpl"))
    stays = (rank % 2 == seq) & (rank == seq * half + rank // 2)
    return jnp.where(stays, arr, moved)


def shift(arr, step):
    half = lax.axis_size("mpl")
    size = 2 * half

    def place(rank):
        return (rank % 2) * half + rank // 2

    pairs = [(place(i), place((i + step) % size)) for i in range(size)]
    return lax.ppermute(arr, ("core", "mpl"), pairs)


def gather_rot(rows):
    size = lax.axis_size(GRP)
    return jnp.concatenate([rows] + [shift(rows, -k) for k in range(1, size)], 0)


def sum_rot(term, count):
    size = lax.axis_size(GRP)
    sent = [shift(term(k * count, count).astype(BF16), k) for k in range(1, size)]
    total = term(0, count)
    for piece in sent:
        total = total + piece.astype(F32)
    return total


def dot_nn(left, right):
    return lax.dot_general(left, right, (((1,), (0,)), ((), ())), preferred_element_type=F32)


def dot_tn(left, right):
    return lax.dot_general(left, right, (((0,), (0,)), ((), ())), preferred_element_type=F32)


def dot_nt(left, right):
    return lax.dot_general(left, right, (((1,), (1,)), ((), ())), preferred_element_type=F32)


def normalize(values):
    center = values - jnp.mean(values, -1, keepdims=True)
    spread = jnp.mean(center * center, -1, keepdims=True)
    inv = lax.rsqrt(spread + EPS)
    return center * inv, inv


def norm_back(grad, gain, unit, inv):
    scaled = grad * gain
    mean_g = jnp.mean(scaled, -1, keepdims=True)
    mean_x = jnp.mean(scaled * unit, -1, keepdims=True)
    return inv * (scaled - mean_g - unit * mean_x)


def bucket_of(offset, half):
    distance = jnp.abs(offset)
    far_part = jnp.full(offset.shape, 8, jnp.int32)
    for limit in THRESH:
        far_part = far_part + (distance >= limit).astype(jnp.int32)
    magnitude = jnp.where(distance < 8, distance, far_part)
    return magnitude + half * (offset > 0).astype(jnp.int32)


def window_bias(table):
    key_pos = lax.broadcasted_iota(jnp.int32, (2 * W, W), 0) - W
    query_pos = lax.broadcasted_iota(jnp.int32, (2 * W, W), 1)
    which = bucket_of(key_pos - query_pos, table.shape[0] // 2)
    bias = jnp.zeros((table.shape[1], 2 * W, W), F32)
    for entry in range(table.shape[0]):
        bias = jnp.where((which == entry)[None], table[entry][:, None, None], bias)
    return bias


def table_grad(cells, entries):
    heads = cells.shape[0]
    diag = lax.broadcasted_iota(jnp.int32, (3, TILE, TILE), 0) - 1
    key_pos = lax.broadcasted_iota(jnp.int32, (3, TILE, TILE), 1)
    query_pos = lax.broadcasted_iota(jnp.int32, (3, TILE, TILE), 2)
    which = bucket_of(diag * TILE + key_pos - query_pos, entries // 2)
    rows = lax.broadcasted_iota(jnp.int32, (entries, 1, 1, 1), 0)
    hot = (which[None] == rows).astype(F32)
    near = jnp.stack(
        [jnp.sum(hot * cells[h, :3][None], (1, 2, 3)) for h in range(heads)], 1
    )
    far = jnp.sum(cells[:, 3:], (2, 3))
    entry = lax.broadcasted_iota(jnp.int32, (entries, heads), 0)
    left = jnp.where(entry == entries // 2 - 1, far[:, 0][None], 0.0)
    right = jnp.where(entry == entries - 1, far[:, 1][None], 0.0)
    return near + left + right


def reach_of(block, prefix):
    query = block * W + lax.broadcasted_iota(jnp.int32, (1, W), 1)
    return jnp.where(query < prefix, jnp.maximum(query, prefix - 1), query)


def allowed_keys(block, prefix):
    key = block * W + lax.broadcasted_iota(jnp.int32, (W, W), 0)
    return key <= reach_of(block, prefix)


def soft_unit(logits, values):
    top = jnp.max(logits[0], 0, keepdims=True)
    for part in logits[1:]:
        top = jnp.maximum(top, jnp.max(part, 0, keepdims=True))
    total = None
    acc = None
    for part, vals in zip(logits, values):
        expo = jnp.exp2(part - top)
        summed = jnp.sum(expo, 0, keepdims=True)
        mixed = dot_tn(vals, expo.astype(BF16))
        total = summed if total is None else total + summed
        acc = mixed if acc is None else acc + mixed
    return jnp.transpose(acc / total).astype(BF16), top + jnp.log2(total)


def row_dot(grad_out, out):
    prod = grad_out.astype(F32) * out.astype(F32)
    return jnp.sum(jnp.transpose(prod), 0, keepdims=True)


def back_unit(logits, queries, keys, values, grad_out, lse, delta):
    probs = jnp.exp2(logits - lse)
    grad_probs = dot_nt(values, grad_out)
    grad_values = dot_nn(probs.astype(BF16), grad_out)
    grad_scores = probs * (grad_probs - delta)
    low = grad_scores.astype(BF16)
    grad_keys = dot_nn(low, queries) * SCALE
    grad_queries = dot_tn(keys, low)
    return grad_queries, grad_keys, grad_values, grad_scores


def self_forward_kernel(where, q, kp, kc, vp, vc, bias, out, lse):
    block = pl.program_id(0)
    edge = jnp.where(block == 0, NEG, 0.0)
    allowed = allowed_keys(block, where[1])
    for h in range(bias.shape[0]):
        cols = slice(h * HD, (h + 1) * HD)
        before = dot_nt(kp[:, cols], q[:, cols]) * SCALE2 + (bias[h, :W] + edge)
        here = jnp.where(allowed, dot_nt(kc[:, cols], q[:, cols]) * SCALE2 + bias[h, W:], NEG)
        out[:, cols], lse[0, h : h + 1] = soft_unit(
            (before, here), (vp[:, cols], vc[:, cols])
        )


def self_specs(blocks, local_w, order):
    def at(part, delta):
        def index(i, where):
            block = jnp.maximum(order(i) + delta, 0)
            return ((block + blocks - where[0]) % blocks, part)

        return pl.BlockSpec((W, local_w), index)

    return at


def self_forward(where, proj, bias):
    seq_len, width = proj.shape
    local_w = width // 4
    heads = bias.shape[0]
    blocks = seq_len // W
    at = self_specs(blocks, local_w, lambda i: i)
    return pl.pallas_call(
        self_forward_kernel,
        grid_spec=pltpu.PrefetchScalarGridSpec(
            num_scalar_prefetch=1,
            grid=(blocks,),
            in_specs=[
                at(0, 0),
                at(2, -1),
                at(2, 0),
                at(3, -1),
                at(3, 0),
                pl.BlockSpec(bias.shape, lambda i, where: (0, 0, 0)),
            ],
            out_specs=[
                at(0, 0),
                pl.BlockSpec((1, heads, W), lambda i, where: (i, 0, 0)),
            ],
        ),
        out_shape=[
            jax.ShapeDtypeStruct((seq_len, 2 * local_w), BF16),
            jax.ShapeDtypeStruct((blocks, heads, W), F32),
        ],
        compiler_params=pltpu.CompilerParams(vmem_limit_bytes=VMEM_BYTES),
        cost_estimate=pl.CostEstimate(
            flops=seq_len * 2 * W * local_w * 4,
            bytes_accessed=seq_len * local_w * 12 + bias.size * 4,
            transcendentals=seq_len * 2 * W * heads,
        ),
        name="self_forward",
    )(where, proj, proj, proj, proj, proj, bias)


def self_backward_kernel(
    where, q, kp, kc, vp, vc, bias, dout, out, lse, aux, grad_proj, cells, carry
):
    step = pl.program_id(0)
    block = pl.num_programs(0) - 1 - step
    edge = jnp.where(block == 0, NEG, 0.0)
    allowed = allowed_keys(block, where[1])
    heads = bias.shape[0]
    local_w = heads * HD
    tiles = W // TILE

    @pl.when(step == 0)
    def _():
        carry[...] = jnp.zeros_like(carry)
        cells[...] = jnp.zeros_like(cells)

    for h in range(heads):
        cols = slice(h * HD, (h + 1) * HD)
        vcols = slice(local_w + h * HD, local_w + (h + 1) * HD)
        delta = row_dot(dout[:, cols], out[:, cols])
        row_lse = lse[0, h : h + 1]
        before = dot_nt(kp[:, cols], q[:, cols]) * SCALE2 + (bias[h, :W] + edge)
        dq0, dk0, dv0, ds0 = back_unit(
            before, q[:, cols], kp[:, cols], vp[:, cols], dout[:, cols], row_lse, delta
        )
        here = jnp.where(allowed, dot_nt(kc[:, cols], q[:, cols]) * SCALE2 + bias[h, W:], NEG)
        dq1, dk1, dv1, ds1 = back_unit(
            here, q[:, cols], kc[:, cols], vc[:, cols], dout[:, cols], row_lse, delta
        )
        parts = {0: [], 1: [], 2: [], 3: [], 4: []}
        for kt in range(2 * tiles):
            for qt in range(tiles):
                source, row = (ds0, kt) if kt < tiles else (ds1, kt - tiles)
                cell = source[row * TILE : (row + 1) * TILE, qt * TILE : (qt + 1) * TILE]
                diag = kt - tiles - qt
                slot = diag + 1 if -1 <= diag <= 1 else (3 if diag < 0 else 4)
                parts[slot].append(cell)
        for slot, group in parts.items():
            cells[h, slot] += functools.reduce(jnp.add, group)
        grad_proj[:, cols] = (jnp.transpose(dq0 + dq1) * SCALE).astype(BF16)
        grad_proj[:, local_w + h * HD : local_w + (h + 1) * HD] = aux[:, cols]
        grad_proj[:, 2 * local_w + h * HD : 2 * local_w + (h + 1) * HD] = (
            dk1 + carry[:, cols] + aux[:, vcols].astype(F32)
        ).astype(BF16)
        grad_proj[:, 3 * local_w + h * HD : 3 * local_w + (h + 1) * HD] = (
            dv1
            + carry[:, vcols]
            + aux[:, 2 * local_w + h * HD : 2 * local_w + (h + 1) * HD].astype(F32)
        ).astype(BF16)
        carry[:, cols] = dk0
        carry[:, vcols] = dv0


def self_backward(where, proj, bias, grad_att, att, lse, aux):
    seq_len, width = proj.shape
    local_w = width // 4
    heads = bias.shape[0]
    blocks = seq_len // W

    def order(i):
        return blocks - 1 - i

    at = self_specs(blocks, local_w, order)

    def whole(i, where):
        return ((order(i) + blocks - where[0]) % blocks, 0)

    return pl.pallas_call(
        self_backward_kernel,
        grid_spec=pltpu.PrefetchScalarGridSpec(
            num_scalar_prefetch=1,
            grid=(blocks,),
            in_specs=[
                at(0, 0),
                at(2, -1),
                at(2, 0),
                at(3, -1),
                at(3, 0),
                pl.BlockSpec(
                    bias.shape, lambda i, where: (0, 0, 0), pipeline_mode=pl.Buffered(1)
                ),
                at(0, 0),
                at(0, 0),
                pl.BlockSpec((1, heads, W), lambda i, where: (order(i), 0, 0)),
                pl.BlockSpec((W, 3 * local_w), whole),
            ],
            out_specs=[
                pl.BlockSpec((W, width), whole),
                pl.BlockSpec((heads, 5, TILE, TILE), lambda i, where: (0, 0, 0, 0)),
            ],
            scratch_shapes=[pltpu.VMEM((W, 2 * local_w), F32)],
        ),
        out_shape=[
            jax.ShapeDtypeStruct((seq_len, width), BF16),
            jax.ShapeDtypeStruct((heads, 5, TILE, TILE), F32),
        ],
        compiler_params=pltpu.CompilerParams(vmem_limit_bytes=VMEM_BYTES),
        cost_estimate=pl.CostEstimate(
            flops=seq_len * 2 * W * local_w * 10,
            bytes_accessed=seq_len * local_w * 30 + bias.size * 4,
            transcendentals=seq_len * 2 * W * heads,
        ),
        name="self_backward",
    )(where, proj, proj, proj, proj, proj, bias, grad_att, att, lse, aux)


def state_forward_kernel(first, where, *refs):
    refs = list(refs)
    prev = refs.pop(0)
    if not first:
        mine, theirs = refs.pop(0), refs.pop(0)
    gain, gate, w_in, w_out, cq, kc, vc = refs[:7]
    state, norm, sproj, satt, att, lse, part = refs[-7:]
    local_w = cq.shape[1]
    heads = local_w // HD
    if first:
        fresh = prev[...]
    else:
        update = mine[...].astype(F32) + theirs[...].astype(F32)
        fresh = gate[...] * prev[...] + (1.0 - gate[...]) * update
    state[...] = fresh
    unit, _ = normalize(fresh)
    normed = (unit * gain[...]).astype(BF16)
    norm[...] = normed
    for p in range(4):
        cols = slice(p * local_w, (p + 1) * local_w)
        sproj[:, cols] = dot_nn(normed, w_in[:, cols]).astype(BF16)
    for h in range(heads):
        cols = [slice(p * local_w + h * HD, p * local_w + (h + 1) * HD) for p in range(4)]
        sk, sv = sproj[:, cols[2]], sproj[:, cols[3]]
        satt[:, cols[0]], lse[0, h : h + 1] = soft_unit(
            (dot_nt(sk, sproj[:, cols[0]]) * SCALE2,), (sv,)
        )
        satt[:, cols[1]], lse[0, heads + h : heads + h + 1] = soft_unit(
            (dot_nt(kc[:, cols[0]], sproj[:, cols[1]]) * SCALE2,), (vc[:, cols[0]],)
        )
        att[:, cols[0]], lse[0, 2 * heads + h : 2 * heads + h + 1] = soft_unit(
            (dot_nt(sk, cq[:, cols[0]]) * SCALE2,), (sv,)
        )
    part[...] = dot_nt(satt[...], w_out[...]).astype(BF16)


def state_forward(where, block, prev, mine, theirs, gain, gate, w_in, w_out, proj, kept, att):
    first = block == 0
    seq_len, width = proj.shape
    local_w = width // 4
    heads = local_w // HD
    blocks = seq_len // W
    model = prev.shape[1]

    def phys(part):
        return pl.BlockSpec(
            (W, local_w), lambda i, where: ((where[2] + blocks - where[0]) % blocks, part)
        )

    def full(arr):
        return pl.BlockSpec(arr.shape, lambda i, where: (0,) * arr.ndim)

    def row_block(cols):
        return pl.BlockSpec((S, cols), lambda i, where: (where[2], 0))

    anywhere = pl.BlockSpec(memory_space=pl.ANY)
    operands = [prev] + ([] if first else [mine, theirs]) + [gain, gate, w_in, w_out]
    in_specs = [full(arr) for arr in operands] + [phys(1), phys(2), phys(3)]
    operands += [proj, proj, proj]
    aliases = {}
    held = [] if first else list(kept[:3])
    for slot, arr in enumerate(held):
        aliases[1 + len(operands)] = 1 + slot
        operands.append(arr)
        in_specs.append(anywhere)
    aliases[1 + len(operands)] = 4
    operands.append(att)
    in_specs.append(anywhere)
    if not first:
        aliases[1 + len(operands)] = 5
        operands.append(kept[3])
        in_specs.append(anywhere)
    return pl.pallas_call(
        functools.partial(state_forward_kernel, first),
        grid_spec=pltpu.PrefetchScalarGridSpec(
            num_scalar_prefetch=1,
            grid=(1,),
            in_specs=in_specs,
            out_specs=[
                full(prev),
                row_block(model),
                row_block(width),
                row_block(2 * local_w),
                phys(1),
                pl.BlockSpec((1, 3 * heads, S), lambda i, where: (where[2], 0, 0)),
                full(prev),
            ],
        ),
        out_shape=[
            jax.ShapeDtypeStruct(prev.shape, F32),
            jax.ShapeDtypeStruct((blocks * S, model), BF16),
            jax.ShapeDtypeStruct((blocks * S, width), BF16),
            jax.ShapeDtypeStruct((blocks * S, 2 * local_w), BF16),
            jax.ShapeDtypeStruct(att.shape, BF16),
            jax.ShapeDtypeStruct((blocks, 3 * heads, S), F32),
            jax.ShapeDtypeStruct(prev.shape, BF16),
        ],
        input_output_aliases=aliases,
        compiler_params=pltpu.CompilerParams(vmem_limit_bytes=VMEM_BYTES),
        cost_estimate=pl.CostEstimate(
            flops=S * model * local_w * 12 + 3 * S * W * local_w * 4,
            bytes_accessed=(w_in.size + w_out.size) * 2 + S * model * 20,
            transcendentals=3 * S * W * heads,
        ),
        name="state_forward",
    )(where, *operands)


def state_backward_kernel(last, where, *refs):
    refs = list(refs)
    if not last:
        later, mine, theirs, state_next, upd_mine, upd_theirs = refs[:6]
        refs = refs[6:]
    state, gain, gate, w_in, w_out, cq, kc, vc, dcross, cross, sproj, satt, lse = refs[:13]
    dstate, dupd, dsproj, aux, sums, part = refs[-6:]
    local_w = cq.shape[1]
    heads = local_w // HD
    model = state.shape[1]
    gate_f = gate[...]
    if last:
        dstate[...] = jnp.zeros_like(dstate)
        dupd[...] = jnp.zeros_like(dupd)
        gate_sum = jnp.zeros((1, model), F32)
    else:
        unit, inv = normalize(state_next[...])
        grad_norm = mine[...].astype(F32) + theirs[...].astype(F32)
        grad_state = gate_f * later[...] + norm_back(grad_norm, gain[...], unit, inv)
        dstate[...] = grad_state
        update = upd_mine[...].astype(F32) + upd_theirs[...].astype(F32)
        gate_sum = jnp.sum(grad_state * (state[...] - update), 0, keepdims=True)
        gate_sum = gate_sum * gate_f * (1.0 - gate_f)
        dupd[...] = ((1.0 - gate_f) * grad_state).astype(BF16)
    for h in range(heads):
        cols = [slice(p * local_w + h * HD, p * local_w + (h + 1) * HD) for p in range(4)]
        head = cols[0]
        sk, sv = sproj[:, cols[2]], sproj[:, cols[3]]
        delta = row_dot(dcross[:, head], cross[:, head])
        dq, dk, dv, _ = back_unit(
            dot_nt(sk, cq[:, head]) * SCALE2,
            cq[:, head],
            sk,
            sv,
            dcross[:, head],
            lse[0, 2 * heads + h : 2 * heads + h + 1],
            delta,
        )
        aux[:, cols[0]] = (jnp.transpose(dq) * SCALE).astype(BF16)
        if last:
            aux[:, cols[1]] = jnp.zeros((S, HD), BF16)
            aux[:, cols[2]] = jnp.zeros((S, HD), BF16)
            dsproj[:, cols[0]] = jnp.zeros((S, HD), BF16)
            dsproj[:, cols[1]] = jnp.zeros((S, HD), BF16)
        else:
            dself = dot_nn(dupd[...], w_out[:, cols[0]]).astype(BF16)
            dext = dot_nn(dupd[...], w_out[:, cols[1]]).astype(BF16)
            sq = sproj[:, cols[0]]
            dq, dk_s, dv_s, _ = back_unit(
                dot_nt(sk, sq) * SCALE2,
                sq,
                sk,
                sv,
                dself,
                lse[0, h : h + 1],
                row_dot(dself, satt[:, cols[0]]),
            )
            dsproj[:, cols[0]] = (jnp.transpose(dq) * SCALE).astype(BF16)
            dk = dk + dk_s
            dv = dv + dv_s
            sx = sproj[:, cols[1]]
            dq, dk_x, dv_x, _ = back_unit(
                dot_nt(kc[:, head], sx) * SCALE2,
                sx,
                kc[:, head],
                vc[:, head],
                dext,
                lse[0, heads + h : heads + h + 1],
                row_dot(dext, satt[:, cols[1]]),
            )
            dsproj[:, cols[1]] = (jnp.transpose(dq) * SCALE).astype(BF16)
            aux[:, cols[1]] = dk_x.astype(BF16)
            aux[:, cols[2]] = dv_x.astype(BF16)
        dsproj[:, cols[2]] = dk.astype(BF16)
        dsproj[:, cols[3]] = dv.astype(BF16)
    part[...] = dot_nt(dsproj[...], w_in[...]).astype(BF16)
    sums[...] = jnp.broadcast_to(gate_sum, sums.shape)


def state_backward(
    where, block, chain, state, gain, gate, w_in, w_out, proj, grad_att, att, sproj, satt, lse, kept
):
    seq_len, width = proj.shape
    local_w = width // 4
    heads = local_w // HD
    blocks = seq_len // W
    last = block == blocks - 1
    model = state.shape[1]

    def phys(part):
        return pl.BlockSpec(
            (W, local_w), lambda i, where: ((where[2] + blocks - where[0]) % blocks, part)
        )

    def full(arr):
        return pl.BlockSpec(arr.shape, lambda i, where: (0,) * arr.ndim)

    def row_block(cols):
        return pl.BlockSpec((S, cols), lambda i, where: (where[2], 0))

    anywhere = pl.BlockSpec(memory_space=pl.ANY)
    operands = ([] if last else list(chain)) + [state, gain, gate, w_in, w_out]
    in_specs = [full(arr) for arr in operands]
    operands += [proj, proj, proj, grad_att, att, sproj, satt, lse]
    in_specs += [phys(1), phys(2), phys(3), phys(1), phys(1)]
    in_specs += [row_block(width), row_block(2 * local_w)]
    in_specs += [pl.BlockSpec((1, 3 * heads, S), lambda i, where: (where[2], 0, 0))]
    aliases = {}
    if not last:
        for slot, arr in enumerate(kept):
            aliases[1 + len(operands)] = 1 + slot
            operands.append(arr)
            in_specs.append(anywhere)
    return pl.pallas_call(
        functools.partial(state_backward_kernel, last),
        grid_spec=pltpu.PrefetchScalarGridSpec(
            num_scalar_prefetch=1,
            grid=(1,),
            in_specs=in_specs,
            out_specs=[
                full(state),
                row_block(model),
                row_block(width),
                pl.BlockSpec(
                    (W, 3 * local_w),
                    lambda i, where: ((where[2] + blocks - where[0]) % blocks, 0),
                ),
                pl.BlockSpec((8, model), lambda i, where: (0, 0)),
                full(state),
            ],
        ),
        out_shape=[
            jax.ShapeDtypeStruct(state.shape, F32),
            jax.ShapeDtypeStruct((blocks * S, model), BF16),
            jax.ShapeDtypeStruct((blocks * S, width), BF16),
            jax.ShapeDtypeStruct((seq_len, 3 * local_w), BF16),
            jax.ShapeDtypeStruct((8, model), F32),
            jax.ShapeDtypeStruct(state.shape, BF16),
        ],
        input_output_aliases=aliases,
        compiler_params=pltpu.CompilerParams(vmem_limit_bytes=VMEM_BYTES),
        cost_estimate=pl.CostEstimate(
            flops=S * model * local_w * 12 + 3 * S * W * local_w * 10,
            bytes_accessed=(w_in.size + w_out.size) * 2 + S * model * 40,
            transcendentals=3 * S * W * heads,
        ),
        name="state_backward",
    )(where, *operands)


def up_kernel(rows, weight, act, slope):
    step = min(512, weight.shape[1])
    root = 0.7978845608028654
    for start in range(0, weight.shape[1], step):
        cols = slice(start, start + step)
        pre = dot_nn(rows[...], weight[:, cols])
        square = pre * pre
        half = 0.5 * jnp.tanh(pre * (root + (root * 0.044715) * square)) + 0.5
        value = pre * half
        act[:, cols] = value.astype(BF16)
        rise = 2.0 * root + (6.0 * root * 0.044715) * square
        slope[:, cols] = (half + value * (1.0 - half) * rise).astype(BF16)


def up_project(rows, weight, units):
    count, model = rows.shape
    out = jax.ShapeDtypeStruct((count, units), BF16)
    return pl.pallas_call(
        up_kernel,
        grid=(count // W,),
        in_specs=[
            pl.BlockSpec((W, model), lambda i: (i, 0)),
            pl.BlockSpec((model, units), lambda i: (0, 0)),
        ],
        out_specs=[pl.BlockSpec((W, units), lambda i: (i, 0))] * 2,
        out_shape=[out, out],
        compiler_params=pltpu.CompilerParams(vmem_limit_bytes=VMEM_BYTES),
        cost_estimate=pl.CostEstimate(
            flops=2 * count * model * units,
            bytes_accessed=count * (model + 2 * units) * 2 + model * units * 2,
            transcendentals=count * units,
        ),
        name="up_project",
    )(rows, weight)


def after(value, *others):
    return lax.optimization_barrier((value, *others))


def hold(value, *others):
    for arr in others:
        value = value + (arr[0, 0] * 0).astype(value.dtype)
    return value


def gather_weight(shard):
    return lax.all_gather(shard, ORIG_DP, axis=0, tiled=True)


def scatter_moved(moved):
    return lax.psum_scatter(moved, ORIG_DP, scatter_dimension=0, tiled=True)


def local(
    tokens,
    prefix,
    init_state,
    cotangent,
    norm_gains,
    gate_bias,
    rel_table,
    tok_in_proj,
    tok_out_proj,
    st_in_proj,
    st_out_proj,
    mlp_up,
    mlp_down,
):
    rows = tokens.shape[1]
    model = tokens.shape[2]
    size = lax.axis_size(GRP)
    rank = lax.axis_index(GRP)
    seq_len = rows * size
    blocks = seq_len // W
    shard = tok_in_proj.shape[0]
    local_w = tok_in_proj.shape[2]
    heads = rel_table.shape[1]
    units = mlp_up.shape[1]

    small = jnp.concatenate([norm_gains, gate_bias[None]], 0).T
    entries = rel_table.shape[0]
    extra = jnp.zeros((shard, EXTRA), BF16)
    extra = lax.dynamic_update_slice(extra, small, (0, 0))
    if lax.axis_size(("mph", "mpl")) == 2:
        other = lax.ppermute(rel_table, ("mph", "mpl"), [(0, 1), (1, 0)])
        table = jnp.where(
            lax.axis_index(("mph", "mpl")) == 0,
            jnp.concatenate([rel_table, other], 1),
            jnp.concatenate([other, rel_table], 1),
        )
    else:
        table = lax.all_gather(rel_table, ("mph", "mpl"), axis=1, tiled=True)
    extra = lax.dynamic_update_slice(extra, table, (0, 4))
    tok_rows = regroup(tokens[0], True)
    wide = 4 * local_w
    shard_tin = tok_in_proj.reshape(shard, wide)
    shard_sin = st_in_proj.reshape(shard, wide)
    first = gather_weight(jnp.concatenate([shard_tin, extra], 1))
    second = jnp.concatenate([shard_sin, st_out_proj.reshape(2 * local_w, shard).T], 1)
    third = jnp.concatenate(
        [mlp_up, mlp_down.T, tok_out_proj.reshape(2 * local_w, shard).T], 1
    )
    second = gather_weight(hold(second, first, tok_rows))
    extra = first[:, wide:]
    w_tin = regroup(first, True)[:, :wide]
    small = extra[:, :4].T.astype(F32)
    table = extra.reshape(-1, shard, EXTRA)[:, :entries, 4 : 4 + heads * size]
    table = table.reshape(-1, heads * size).astype(F32)
    table = lax.dynamic_slice_in_dim(table, rank * heads, heads, 1)
    start = regroup(hold(init_state[0], tok_rows), True)
    if size == 2:
        other = shift(start, 1)
        state0 = jnp.where(
            rank == 0,
            jnp.concatenate([start, other], 0),
            jnp.concatenate([other, start], 0),
        )
    else:
        state0 = lax.all_gather(start, GRP, axis=0, tiled=True)
    prefix_len = regroup(prefix, True)

    gain1, gain2, gain3 = small[0:1], small[1:2], small[2:3]
    gate = jax.nn.sigmoid(small[3:4])
    bias = window_bias(table * LOG2E)
    base = jnp.stack([rank.astype(jnp.int32) * (rows // W), prefix_len[0]])

    def where_at(block):
        return jnp.concatenate([base, jnp.full((1,), block, jnp.int32)])

    tok_f = tok_rows.astype(F32)
    unit1, inv1 = normalize(tok_f)
    normed = gather_rot((unit1 * gain1).astype(BF16))
    normed, bias, state0 = lax.optimization_barrier((normed, bias, state0))
    proj = dot_nn(normed, w_tin).astype(BF16)
    third, second, proj = after(third, second, proj)
    third = gather_weight(third)
    second = regroup(second, True)
    w_sin, w_sout = second[:, :wide], second[:, wide:]
    att, lse_tok = self_forward(where_at(0), proj, bias)
    states, ups = [], []
    prev, mine, theirs, kept = state0, None, None, None
    for block in range(blocks):
        outs = state_forward(
            where_at(block), block, prev, mine, theirs, gain3, gate, w_sin, w_sout, proj, kept, att
        )
        prev, norm_st, sproj, satt, att, lse_st, mine = outs
        kept = (norm_st, sproj, satt, lse_st)
        if block == 1:
            third, mine = after(third, mine)
        if block == blocks - 2:
            cot_rows, mine = after(cotangent[0], mine)
            cot_rows = regroup(cot_rows, True)
        if size == 2:
            theirs = shift(mine, 1)
        else:
            theirs = lax.psum(mine.astype(F32), GRP) - mine.astype(F32)
            theirs = theirs.astype(BF16)
        states.append(prev)
        ups.append((mine, theirs))
    third = regroup(third, True)
    w_up, w_down, w_tout = third[:, :units], third[:, units : 2 * units], third[:, 2 * units :]
    final = gate * prev + (1.0 - gate) * (mine.astype(F32) + theirs.astype(F32))
    final_rows = lax.dynamic_slice_in_dim(final, rank * (S // size), S // size, 0)

    def attn_term(first, count):
        return dot_nt(lax.slice_in_dim(att, first, first + count, axis=0), w_tout)

    resid = tok_f + sum_rot(attn_term, rows)
    unit2, inv2 = normalize(resid)
    normed2 = gather_rot((unit2 * gain2).astype(BF16))
    act, slope = up_project(normed2, third, units)

    def mlp_term(first, count):
        return dot_nt(lax.slice_in_dim(act, first, first + count, axis=0), w_down)

    mixed = (resid + sum_rot(mlp_term, rows)).astype(BF16)

    cot_all = gather_rot(cot_rows)
    grad_pre = (dot_nn(cot_all, w_down) * slope.astype(F32)).astype(BF16)
    grad_down = regroup(dot_tn(cot_all, act).astype(BF16), False)

    def up_term(first, count):
        return dot_nt(lax.slice_in_dim(grad_pre, first, first + count, axis=0), w_up)

    grad_norm2 = sum_rot(up_term, rows)
    grad_up = regroup(dot_tn(normed2, grad_pre).astype(BF16), False)
    grad_resid = cot_rows.astype(F32) + norm_back(grad_norm2, gain2, unit2, inv2)
    grad_attn = gather_rot(grad_resid.astype(BF16))
    grad_att = dot_nn(grad_attn, w_tout).astype(BF16)
    grad_tout = regroup(dot_tn(grad_attn, att).astype(BF16), False)
    grad_att, grad_down = after(grad_att, grad_down)
    grad_down = scatter_moved(grad_down)

    chain, kept_b, sums = None, None, []
    for block in reversed(range(blocks)):
        outs = state_backward(
            where_at(block),
            block,
            chain,
            states[block],
            gain3,
            gate,
            w_sin,
            w_sout,
            proj,
            grad_att,
            att,
            sproj,
            satt,
            lse_st,
            kept_b,
        )
        later, dupd, dsproj, aux, sum_b, part = outs
        kept_b = (dupd, dsproj, aux)
        sums.append(sum_b)
        if block == blocks - 3:
            part, grad_up = after(part, grad_up)
            grad_up = scatter_moved(grad_up)
        if block == blocks - 5:
            part, grad_tout, grad_down = after(part, grad_tout, grad_down)
            grad_tout = scatter_moved(grad_tout)
        if block == 1:
            part, grad_up = after(part, grad_up)
        if block > 0:
            if size == 2:
                other = shift(part, 1)
            else:
                other = (lax.psum(part.astype(F32), GRP) - part.astype(F32)).astype(BF16)
            chain = (later, part, other, states[block]) + ups[block - 1]
    gate_grad = functools.reduce(jnp.add, sums)[0]
    mixed = regroup(mixed, False)
    final_rows = regroup(final_rows, False)
    grad_st = jnp.concatenate(
        [dot_tn(norm_st, dsproj).astype(BF16), dot_tn(dupd, satt).astype(BF16)], 1
    )
    aux, grad_st, mixed, final_rows, grad_tout = after(
        aux, grad_st, mixed, final_rows, grad_tout
    )
    grad_st = regroup(grad_st, False)

    grad_proj, cells = self_backward(where_at(0), proj, bias, grad_att, att, lse_tok, aux)

    def tok_term(first, count):
        return dot_nt(lax.slice_in_dim(grad_proj, first, first + count, axis=0), w_tin)

    grad_table = table_grad(cells, table.shape[0]).reshape(-1, entries, heads)
    grad_table = jnp.pad(grad_table, ((0, 0), (0, shard - entries), (0, 0)))
    packed = jnp.concatenate([gate_grad[:, None], grad_table.reshape(model, heads)], 1)
    packed = jnp.pad(packed, ((0, 0), (0, EXTRA - 1 - heads))).astype(BF16)
    grad_tin = jnp.concatenate([dot_tn(normed, grad_proj).astype(BF16), packed], 1)
    grad_tin, grad_st = after(grad_tin, grad_st)
    grad_tin = regroup(grad_tin, False)
    grad_st = scatter_moved(grad_st)
    grad_sin, grad_sout = grad_st[:, :wide], grad_st[:, wide:]
    grad_tin = scatter_moved(grad_tin)
    grad_tin, packed = grad_tin[:, :wide], grad_tin[:, wide:].astype(F32)
    grad_norm1 = sum_rot(tok_term, rows)
    input_grad = grad_resid + norm_back(grad_norm1, gain1, unit1, inv1)

    def gain_sum(shard_in, grad):
        return jnp.sum(shard_in.astype(F32) * grad.astype(F32), 1)

    ranks = lax.axis_size(("mph", "mpl"))
    vectors = jnp.stack(
        [
            gain_sum(shard_tin, grad_tin),
            gain_sum(mlp_up, grad_up),
            gain_sum(shard_sin, grad_sin),
            packed[:, 0] / ranks,
        ]
    )
    if ranks == 2:
        vectors = vectors + lax.ppermute(vectors, ("mph", "mpl"), [(0, 1), (1, 0)])
    else:
        vectors = lax.psum(vectors, ("mph", "mpl"))
    gains = vectors[:3] / norm_gains.astype(F32)
    grad_table = packed[:entries, 1 : 1 + heads]

    return (
        mixed[None],
        final_rows[None],
        regroup(input_grad.astype(BF16), False).astype(F32)[None],
        gains,
        vectors[3],
        grad_table,
        grad_tin.astype(F32).reshape(shard, 4, local_w),
        grad_tout.T.astype(F32).reshape(2, local_w, shard),
        grad_sin.astype(F32).reshape(shard, 4, local_w),
        grad_sout.T.astype(F32).reshape(2, local_w, shard),
        grad_up.astype(F32),
        grad_down.T.astype(F32),
    )


def solution(mesh):
    devs = mesh.devices
    dp_n, mp_n = devs.shape
    fine = jax.sharding.Mesh(
        devs.reshape(dp_n // 2, 2, 2, mp_n // 2), ("dph", "core", "mph", "mpl")
    )
    dp, mp = ("dph", "core"), ("mph", "mpl")
    weights = (
        P(None, dp),
        P(dp),
        P(dp, mp),
        P(dp, None, mp),
        P(None, mp, dp),
        P(dp, None, mp),
        P(None, mp, dp),
        P(dp, mp),
        P(mp, dp),
    )
    rows = P(dp, mp, None)
    return jax.shard_map(
        local,
        mesh=fine,
        in_specs=(rows, P(dp), rows, rows) + weights,
        out_specs=(rows, rows, rows) + weights,
        check_vma=False,
    )
```

```python
import functools

import jax
import jax.numpy as jnp
from jax import lax
from jax.experimental import pallas as pl
from jax.experimental.pallas import tpu as pltpu
from jax.sharding import PartitionSpec as P

HD = 128
S = 512
W = 512
TILE = 128
EXTRA = 128

EPS = 1e-06
NEG = -1e30
THRESH = (12, 16, 23, 32, 46, 64, 91)
LOG2E = 1.4426950408889634
SCALE = HD ** (-0.5)
SCALE2 = SCALE * LOG2E
VMEM_BYTES = 60 * 1024 * 1024

GRP = ("mpl", "core")
ORIG_DP = ("dph", "core")
SWAP = ("core", "mph", "mpl")

F32 = jnp.float32
BF16 = jnp.bfloat16


def regroup(arr, forward):
    ranks = lax.axis_size(("mph", "mpl"))
    half = ranks // 2
    pairs = []
    for seq in range(2):
        for rank in range(ranks):
            here = seq * ranks + rank
            there = (rank % 2) * ranks + seq * half + rank // 2
            if here != there:
                pairs.append((here, there) if forward else (there, here))
    moved = lax.ppermute(arr, SWAP, pairs)
    seq, rank = lax.axis_index("core"), lax.axis_index(("mph", "mpl"))
    stays = (rank % 2 == seq) & (rank == seq * half + rank // 2)
    return jnp.where(stays, arr, moved)


def shift(arr, step):
    half = lax.axis_size("mpl")
    size = 2 * half

    def place(rank):
        return (rank % 2) * half + rank // 2

    pairs = [(place(i), place((i + step) % size)) for i in range(size)]
    return lax.ppermute(arr, ("core", "mpl"), pairs)


def gather_rot(rows):
    size = lax.axis_size(GRP)
    return jnp.concatenate([rows] + [shift(rows, -k) for k in range(1, size)], 0)


def sum_rot(term, count):
    size = lax.axis_size(GRP)
    sent = [shift(term(k * count, count).astype(BF16), k) for k in range(1, size)]
    total = term(0, count)
    for piece in sent:
        total = total + piece.astype(F32)
    return total


def dot_nn(left, right):
    return lax.dot_general(left, right, (((1,), (0,)), ((), ())), preferred_element_type=F32)


def dot_tn(left, right):
    return lax.dot_general(left, right, (((0,), (0,)), ((), ())), preferred_element_type=F32)


def dot_nt(left, right):
    return lax.dot_general(left, right, (((1,), (1,)), ((), ())), preferred_element_type=F32)


def normalize(values):
    center = values - jnp.mean(values, -1, keepdims=True)
    spread = jnp.mean(center * center, -1, keepdims=True)
    inv = lax.rsqrt(spread + EPS)
    return center * inv, inv


def norm_back(grad, gain, unit, inv):
    scaled = grad * gain
    mean_g = jnp.mean(scaled, -1, keepdims=True)
    mean_x = jnp.mean(scaled * unit, -1, keepdims=True)
    return inv * (scaled - mean_g - unit * mean_x)


def bucket_of(offset, half):
    distance = jnp.abs(offset)
    far_part = jnp.full(offset.shape, 8, jnp.int32)
    for limit in THRESH:
        far_part = far_part + (distance >= limit).astype(jnp.int32)
    magnitude = jnp.where(distance < 8, distance, far_part)
    return magnitude + half * (offset > 0).astype(jnp.int32)


def near_bias(table):
    entries, heads = table.shape
    diag = lax.broadcasted_iota(jnp.int32, (3, TILE, TILE), 0) - 1
    key_pos = lax.broadcasted_iota(jnp.int32, (3, TILE, TILE), 1)
    query_pos = lax.broadcasted_iota(jnp.int32, (3, TILE, TILE), 2)
    which = bucket_of(diag * TILE + key_pos - query_pos, entries // 2)
    near = jnp.zeros((heads, 3, TILE, TILE), F32)
    for entry in range(entries):
        near = jnp.where((which == entry)[None], table[entry][:, None, None, None], near)
    far = jnp.stack([table[entries // 2 - 1], table[entries - 1]], 1)
    far = jnp.broadcast_to(far[:, :, None, None], (heads, 2, TILE, TILE))
    return jnp.concatenate([near, far], 1)


def tile_slot(kt, qt):
    diag = kt - W // TILE - qt
    return diag + 1 if -1 <= diag <= 1 else (3 if diag < 0 else 4)


def fill_bias(near, bias):
    for h in range(near.shape[0]):
        for kt in range(2 * W // TILE):
            for qt in range(W // TILE):
                bias[h, kt * TILE : (kt + 1) * TILE, qt * TILE : (qt + 1) * TILE] = near[
                    h, tile_slot(kt, qt)
                ]


def table_grad(cells, entries):
    heads = cells.shape[0]
    diag = lax.broadcasted_iota(jnp.int32, (3, TILE, TILE), 0) - 1
    key_pos = lax.broadcasted_iota(jnp.int32, (3, TILE, TILE), 1)
    query_pos = lax.broadcasted_iota(jnp.int32, (3, TILE, TILE), 2)
    which = bucket_of(diag * TILE + key_pos - query_pos, entries // 2)
    rows = lax.broadcasted_iota(jnp.int32, (entries, 1, 1, 1), 0)
    hot = (which[None] == rows).astype(F32)
    near = jnp.stack(
        [jnp.sum(hot * cells[h, :3][None], (1, 2, 3)) for h in range(heads)], 1
    )
    far = jnp.sum(cells[:, 3:], (2, 3))
    entry = lax.broadcasted_iota(jnp.int32, (entries, heads), 0)
    left = jnp.where(entry == entries // 2 - 1, far[:, 0][None], 0.0)
    right = jnp.where(entry == entries - 1, far[:, 1][None], 0.0)
    return near + left + right


def reach_of(block, prefix):
    query = block * W + lax.broadcasted_iota(jnp.int32, (1, W), 1)
    return jnp.where(query < prefix, jnp.maximum(query, prefix - 1), query)


def allowed_keys(block, prefix):
    key = block * W + lax.broadcasted_iota(jnp.int32, (W, W), 0)
    return key <= reach_of(block, prefix)


def soft_unit(logits, values):
    top = jnp.max(logits[0], 0, keepdims=True)
    for part in logits[1:]:
        top = jnp.maximum(top, jnp.max(part, 0, keepdims=True))
    total = None
    acc = None
    for part, vals in zip(logits, values):
        expo = jnp.exp2(part - top)
        summed = jnp.sum(expo, 0, keepdims=True)
        mixed = dot_tn(vals, expo.astype(BF16))
        total = summed if total is None else total + summed
        acc = mixed if acc is None else acc + mixed
    return jnp.transpose(acc / total).astype(BF16), top + jnp.log2(total)


def row_dot(grad_out, out):
    prod = grad_out.astype(F32) * out.astype(F32)
    return jnp.sum(jnp.transpose(prod), 0, keepdims=True)


def back_unit(logits, queries, keys, values, grad_out, lse, delta):
    probs = jnp.exp2(logits - lse)
    grad_probs = dot_nt(values, grad_out)
    grad_values = dot_nn(probs.astype(BF16), grad_out)
    grad_scores = probs * (grad_probs - delta)
    low = grad_scores.astype(BF16)
    grad_keys = dot_nn(low, queries) * SCALE
    grad_queries = dot_tn(keys, low)
    return grad_queries, grad_keys, grad_values, grad_scores


def self_forward_kernel(where, q, kp, kc, vp, vc, near, out, lse, bias):
    block = pl.program_id(0)

    @pl.when(block == 0)
    def _():
        fill_bias(near, bias)

    edge = jnp.where(block == 0, NEG, 0.0)
    allowed = allowed_keys(block, where[1])
    for h in range(bias.shape[0]):
        cols = slice(h * HD, (h + 1) * HD)
        before = dot_nt(kp[:, cols], q[:, cols]) * SCALE2 + (bias[h, :W] + edge)
        here = jnp.where(allowed, dot_nt(kc[:, cols], q[:, cols]) * SCALE2 + bias[h, W:], NEG)
        out[:, cols], lse[0, h : h + 1] = soft_unit(
            (before, here), (vp[:, cols], vc[:, cols])
        )


def self_specs(blocks, local_w, order):
    def at(part, delta):
        def index(i, where):
            block = jnp.maximum(order(i) + delta, 0)
            return ((block + blocks - where[0]) % blocks, part)

        return pl.BlockSpec((W, local_w), index)

    return at


def self_forward(where, proj, near):
    seq_len, width = proj.shape
    local_w = width // 4
    heads = near.shape[0]
    blocks = seq_len // W
    at = self_specs(blocks, local_w, lambda i: i)
    return pl.pallas_call(
        self_forward_kernel,
        grid_spec=pltpu.PrefetchScalarGridSpec(
            num_scalar_prefetch=1,
            grid=(blocks,),
            in_specs=[
                at(0, 0),
                at(2, -1),
                at(2, 0),
                at(3, -1),
                at(3, 0),
                pl.BlockSpec(near.shape, lambda i, where: (0, 0, 0, 0)),
            ],
            out_specs=[
                at(0, 0),
                pl.BlockSpec((1, heads, W), lambda i, where: (i, 0, 0)),
            ],
            scratch_shapes=[pltpu.VMEM((heads, 2 * W, W), F32)],
        ),
        out_shape=[
            jax.ShapeDtypeStruct((seq_len, 2 * local_w), BF16),
            jax.ShapeDtypeStruct((blocks, heads, W), F32),
        ],
        compiler_params=pltpu.CompilerParams(vmem_limit_bytes=VMEM_BYTES),
        cost_estimate=pl.CostEstimate(
            flops=seq_len * 2 * W * local_w * 4,
            bytes_accessed=seq_len * local_w * 12,
            transcendentals=seq_len * 2 * W * heads,
        ),
        name="self_forward",
    )(where, proj, proj, proj, proj, proj, near)


def self_backward_kernel(
    where, q, kp, kc, vp, vc, near, dout, out, lse, aux, grad_proj, cells, carry, bias
):
    step = pl.program_id(0)
    block = pl.num_programs(0) - 1 - step
    edge = jnp.where(block == 0, NEG, 0.0)
    allowed = allowed_keys(block, where[1])
    heads = bias.shape[0]
    local_w = heads * HD
    tiles = W // TILE

    @pl.when(step == 0)
    def _():
        fill_bias(near, bias)
        carry[...] = jnp.zeros_like(carry)
        cells[...] = jnp.zeros_like(cells)

    for h in range(heads):
        cols = slice(h * HD, (h + 1) * HD)
        vcols = slice(local_w + h * HD, local_w + (h + 1) * HD)
        delta = row_dot(dout[:, cols], out[:, cols])
        row_lse = lse[0, h : h + 1]
        before = dot_nt(kp[:, cols], q[:, cols]) * SCALE2 + (bias[h, :W] + edge)
        dq0, dk0, dv0, ds0 = back_unit(
            before, q[:, cols], kp[:, cols], vp[:, cols], dout[:, cols], row_lse, delta
        )
        here = jnp.where(allowed, dot_nt(kc[:, cols], q[:, cols]) * SCALE2 + bias[h, W:], NEG)
        dq1, dk1, dv1, ds1 = back_unit(
            here, q[:, cols], kc[:, cols], vc[:, cols], dout[:, cols], row_lse, delta
        )
        parts = {0: [], 1: [], 2: [], 3: [], 4: []}
        for kt in range(2 * tiles):
            for qt in range(tiles):
                source, row = (ds0, kt) if kt < tiles else (ds1, kt - tiles)
                cell = source[row * TILE : (row + 1) * TILE, qt * TILE : (qt + 1) * TILE]
                parts[tile_slot(kt, qt)].append(cell)
        for slot, group in parts.items():
            cells[h, slot] += functools.reduce(jnp.add, group)
        grad_proj[:, cols] = (jnp.transpose(dq0 + dq1) * SCALE).astype(BF16)
        grad_proj[:, local_w + h * HD : local_w + (h + 1) * HD] = aux[:, cols]
        grad_proj[:, 2 * local_w + h * HD : 2 * local_w + (h + 1) * HD] = (
            dk1 + carry[:, cols] + aux[:, vcols].astype(F32)
        ).astype(BF16)
        grad_proj[:, 3 * local_w + h * HD : 3 * local_w + (h + 1) * HD] = (
            dv1
            + carry[:, vcols]
            + aux[:, 2 * local_w + h * HD : 2 * local_w + (h + 1) * HD].astype(F32)
        ).astype(BF16)
        carry[:, cols] = dk0
        carry[:, vcols] = dv0


def self_backward(where, proj, near, grad_att, att, lse, aux):
    seq_len, width = proj.shape
    local_w = width // 4
    heads = near.shape[0]
    blocks = seq_len // W

    def order(i):
        return blocks - 1 - i

    at = self_specs(blocks, local_w, order)

    def whole(i, where):
        return ((order(i) + blocks - where[0]) % blocks, 0)

    return pl.pallas_call(
        self_backward_kernel,
        grid_spec=pltpu.PrefetchScalarGridSpec(
            num_scalar_prefetch=1,
            grid=(blocks,),
            in_specs=[
                at(0, 0),
                at(2, -1),
                at(2, 0),
                at(3, -1),
                at(3, 0),
                pl.BlockSpec(near.shape, lambda i, where: (0, 0, 0, 0)),
                at(0, 0),
                at(0, 0),
                pl.BlockSpec((1, heads, W), lambda i, where: (order(i), 0, 0)),
                pl.BlockSpec((W, 3 * local_w), whole),
            ],
            out_specs=[
                pl.BlockSpec((W, width), whole),
                pl.BlockSpec((heads, 5, TILE, TILE), lambda i, where: (0, 0, 0, 0)),
            ],
            scratch_shapes=[
                pltpu.VMEM((W, 2 * local_w), F32),
                pltpu.VMEM((heads, 2 * W, W), F32),
            ],
        ),
        out_shape=[
            jax.ShapeDtypeStruct((seq_len, width), BF16),
            jax.ShapeDtypeStruct((heads, 5, TILE, TILE), F32),
        ],
        compiler_params=pltpu.CompilerParams(vmem_limit_bytes=VMEM_BYTES),
        cost_estimate=pl.CostEstimate(
            flops=seq_len * 2 * W * local_w * 10,
            bytes_accessed=seq_len * local_w * 30,
            transcendentals=seq_len * 2 * W * heads,
        ),
        name="self_backward",
    )(where, proj, proj, proj, proj, proj, near, grad_att, att, lse, aux)


def state_forward_kernel(first, where, *refs):
    refs = list(refs)
    prev = refs.pop(0)
    if not first:
        mine, theirs = refs.pop(0), refs.pop(0)
    gain, gate, w_in, w_out, cq, kc, vc = refs[:7]
    state, norm, sproj, satt, att, lse, part = refs[-7:]
    local_w = cq.shape[1]
    heads = local_w // HD
    if first:
        fresh = prev[...]
    else:
        update = mine[...].astype(F32) + theirs[...].astype(F32)
        fresh = gate[...] * prev[...] + (1.0 - gate[...]) * update
    state[...] = fresh
    unit, _ = normalize(fresh)
    normed = (unit * gain[...]).astype(BF16)
    norm[...] = normed
    for p in range(4):
        cols = slice(p * local_w, (p + 1) * local_w)
        sproj[:, cols] = dot_nn(normed, w_in[:, cols]).astype(BF16)
    for h in range(heads):
        cols = [slice(p * local_w + h * HD, p * local_w + (h + 1) * HD) for p in range(4)]
        sk, sv = sproj[:, cols[2]], sproj[:, cols[3]]
        satt[:, cols[0]], lse[0, h : h + 1] = soft_unit(
            (dot_nt(sk, sproj[:, cols[0]]) * SCALE2,), (sv,)
        )
        satt[:, cols[1]], lse[0, heads + h : heads + h + 1] = soft_unit(
            (dot_nt(kc[:, cols[0]], sproj[:, cols[1]]) * SCALE2,), (vc[:, cols[0]],)
        )
        att[:, cols[0]], lse[0, 2 * heads + h : 2 * heads + h + 1] = soft_unit(
            (dot_nt(sk, cq[:, cols[0]]) * SCALE2,), (sv,)
        )
    part[...] = dot_nt(satt[...], w_out[...]).astype(BF16)


def state_forward(where, block, prev, mine, theirs, gain, gate, w_in, w_out, proj, kept, att):
    first = block == 0
    seq_len, width = proj.shape
    local_w = width // 4
    heads = local_w // HD
    blocks = seq_len // W
    model = prev.shape[1]

    def phys(part):
        return pl.BlockSpec(
            (W, local_w), lambda i, where: ((where[2] + blocks - where[0]) % blocks, part)
        )

    def full(arr):
        return pl.BlockSpec(arr.shape, lambda i, where: (0,) * arr.ndim)

    def row_block(cols):
        return pl.BlockSpec((S, cols), lambda i, where: (where[2], 0))

    anywhere = pl.BlockSpec(memory_space=pl.ANY)
    operands = [prev] + ([] if first else [mine, theirs]) + [gain, gate, w_in, w_out]
    in_specs = [full(arr) for arr in operands] + [phys(1), phys(2), phys(3)]
    operands += [proj, proj, proj]
    aliases = {}
    held = [] if first else list(kept[:3])
    for slot, arr in enumerate(held):
        aliases[1 + len(operands)] = 1 + slot
        operands.append(arr)
        in_specs.append(anywhere)
    aliases[1 + len(operands)] = 4
    operands.append(att)
    in_specs.append(anywhere)
    if not first:
        aliases[1 + len(operands)] = 5
        operands.append(kept[3])
        in_specs.append(anywhere)
    return pl.pallas_call(
        functools.partial(state_forward_kernel, first),
        grid_spec=pltpu.PrefetchScalarGridSpec(
            num_scalar_prefetch=1,
            grid=(1,),
            in_specs=in_specs,
            out_specs=[
                full(prev),
                row_block(model),
                row_block(width),
                row_block(2 * local_w),
                phys(1),
                pl.BlockSpec((1, 3 * heads, S), lambda i, where: (where[2], 0, 0)),
                full(prev),
            ],
        ),
        out_shape=[
            jax.ShapeDtypeStruct(prev.shape, F32),
            jax.ShapeDtypeStruct((blocks * S, model), BF16),
            jax.ShapeDtypeStruct((blocks * S, width), BF16),
            jax.ShapeDtypeStruct((blocks * S, 2 * local_w), BF16),
            jax.ShapeDtypeStruct(att.shape, BF16),
            jax.ShapeDtypeStruct((blocks, 3 * heads, S), F32),
            jax.ShapeDtypeStruct(prev.shape, BF16),
        ],
        input_output_aliases=aliases,
        compiler_params=pltpu.CompilerParams(vmem_limit_bytes=VMEM_BYTES),
        cost_estimate=pl.CostEstimate(
            flops=S * model * local_w * 12 + 3 * S * W * local_w * 4,
            bytes_accessed=(w_in.size + w_out.size) * 2 + S * model * 20,
            transcendentals=3 * S * W * heads,
        ),
        name="state_forward",
    )(where, *operands)


def state_backward_kernel(last, where, *refs):
    refs = list(refs)
    if not last:
        later, mine, theirs, state_next, upd_mine, upd_theirs = refs[:6]
        refs = refs[6:]
    state, gain, gate, w_in, w_out, cq, kc, vc, dcross, cross, sproj, satt, lse = refs[:13]
    dstate, dupd, dsproj, aux, sums, part = refs[-6:]
    local_w = cq.shape[1]
    heads = local_w // HD
    model = state.shape[1]
    gate_f = gate[...]
    if last:
        dstate[...] = jnp.zeros_like(dstate)
        dupd[...] = jnp.zeros_like(dupd)
        gate_sum = jnp.zeros((1, model), F32)
    else:
        unit, inv = normalize(state_next[...])
        grad_norm = mine[...].astype(F32) + theirs[...].astype(F32)
        grad_state = gate_f * later[...] + norm_back(grad_norm, gain[...], unit, inv)
        dstate[...] = grad_state
        update = upd_mine[...].astype(F32) + upd_theirs[...].astype(F32)
        gate_sum = jnp.sum(grad_state * (state[...] - update), 0, keepdims=True)
        gate_sum = gate_sum * gate_f * (1.0 - gate_f)
        dupd[...] = ((1.0 - gate_f) * grad_state).astype(BF16)
    for h in range(heads):
        cols = [slice(p * local_w + h * HD, p * local_w + (h + 1) * HD) for p in range(4)]
        head = cols[0]
        sk, sv = sproj[:, cols[2]], sproj[:, cols[3]]
        delta = row_dot(dcross[:, head], cross[:, head])
        dq, dk, dv, _ = back_unit(
            dot_nt(sk, cq[:, head]) * SCALE2,
            cq[:, head],
            sk,
            sv,
            dcross[:, head],
            lse[0, 2 * heads + h : 2 * heads + h + 1],
            delta,
        )
        aux[:, cols[0]] = (jnp.transpose(dq) * SCALE).astype(BF16)
        if last:
            aux[:, cols[1]] = jnp.zeros((S, HD), BF16)
            aux[:, cols[2]] = jnp.zeros((S, HD), BF16)
            dsproj[:, cols[0]] = jnp.zeros((S, HD), BF16)
            dsproj[:, cols[1]] = jnp.zeros((S, HD), BF16)
        else:
            dself = dot_nn(dupd[...], w_out[:, cols[0]]).astype(BF16)
            dext = dot_nn(dupd[...], w_out[:, cols[1]]).astype(BF16)
            sq = sproj[:, cols[0]]
            dq, dk_s, dv_s, _ = back_unit(
                dot_nt(sk, sq) * SCALE2,
                sq,
                sk,
                sv,
                dself,
                lse[0, h : h + 1],
                row_dot(dself, satt[:, cols[0]]),
            )
            dsproj[:, cols[0]] = (jnp.transpose(dq) * SCALE).astype(BF16)
            dk = dk + dk_s
            dv = dv + dv_s
            sx = sproj[:, cols[1]]
            dq, dk_x, dv_x, _ = back_unit(
                dot_nt(kc[:, head], sx) * SCALE2,
                sx,
                kc[:, head],
                vc[:, head],
                dext,
                lse[0, heads + h : heads + h + 1],
                row_dot(dext, satt[:, cols[1]]),
            )
            dsproj[:, cols[1]] = (jnp.transpose(dq) * SCALE).astype(BF16)
            aux[:, cols[1]] = dk_x.astype(BF16)
            aux[:, cols[2]] = dv_x.astype(BF16)
        dsproj[:, cols[2]] = dk.astype(BF16)
        dsproj[:, cols[3]] = dv.astype(BF16)
    part[...] = dot_nt(dsproj[...], w_in[...]).astype(BF16)
    sums[...] = jnp.broadcast_to(gate_sum, sums.shape)


def state_backward(
    where, block, chain, state, gain, gate, w_in, w_out, proj, grad_att, att, sproj, satt, lse, kept
):
    seq_len, width = proj.shape
    local_w = width // 4
    heads = local_w // HD
    blocks = seq_len // W
    last = block == blocks - 1
    model = state.shape[1]

    def phys(part):
        return pl.BlockSpec(
            (W, local_w), lambda i, where: ((where[2] + blocks - where[0]) % blocks, part)
        )

    def full(arr):
        return pl.BlockSpec(arr.shape, lambda i, where: (0,) * arr.ndim)

    def row_block(cols):
        return pl.BlockSpec((S, cols), lambda i, where: (where[2], 0))

    anywhere = pl.BlockSpec(memory_space=pl.ANY)
    operands = ([] if last else list(chain)) + [state, gain, gate, w_in, w_out]
    in_specs = [full(arr) for arr in operands]
    operands += [proj, proj, proj, grad_att, att, sproj, satt, lse]
    in_specs += [phys(1), phys(2), phys(3), phys(1), phys(1)]
    in_specs += [row_block(width), row_block(2 * local_w)]
    in_specs += [pl.BlockSpec((1, 3 * heads, S), lambda i, where: (where[2], 0, 0))]
    aliases = {}
    if not last:
        for slot, arr in enumerate(kept):
            aliases[1 + len(operands)] = 1 + slot
            operands.append(arr)
            in_specs.append(anywhere)
    return pl.pallas_call(
        functools.partial(state_backward_kernel, last),
        grid_spec=pltpu.PrefetchScalarGridSpec(
            num_scalar_prefetch=1,
            grid=(1,),
            in_specs=in_specs,
            out_specs=[
                full(state),
                row_block(model),
                row_block(width),
                pl.BlockSpec(
                    (W, 3 * local_w),
                    lambda i, where: ((where[2] + blocks - where[0]) % blocks, 0),
                ),
                pl.BlockSpec((8, model), lambda i, where: (0, 0)),
                full(state),
            ],
        ),
        out_shape=[
            jax.ShapeDtypeStruct(state.shape, F32),
            jax.ShapeDtypeStruct((blocks * S, model), BF16),
            jax.ShapeDtypeStruct((blocks * S, width), BF16),
            jax.ShapeDtypeStruct((seq_len, 3 * local_w), BF16),
            jax.ShapeDtypeStruct((8, model), F32),
            jax.ShapeDtypeStruct(state.shape, BF16),
        ],
        input_output_aliases=aliases,
        compiler_params=pltpu.CompilerParams(vmem_limit_bytes=VMEM_BYTES),
        cost_estimate=pl.CostEstimate(
            flops=S * model * local_w * 12 + 3 * S * W * local_w * 10,
            bytes_accessed=(w_in.size + w_out.size) * 2 + S * model * 40,
            transcendentals=3 * S * W * heads,
        ),
        name="state_backward",
    )(where, *operands)


def up_kernel(rows, weight, act, slope):
    step = min(512, weight.shape[1])
    root = 0.7978845608028654
    for start in range(0, weight.shape[1], step):
        cols = slice(start, start + step)
        pre = dot_nn(rows[...], weight[:, cols])
        square = pre * pre
        half = 0.5 * jnp.tanh(pre * (root + (root * 0.044715) * square)) + 0.5
        value = pre * half
        act[:, cols] = value.astype(BF16)
        rise = 2.0 * root + (6.0 * root * 0.044715) * square
        slope[:, cols] = (half + value * (1.0 - half) * rise).astype(BF16)


def up_project(rows, weight, units):
    count, model = rows.shape
    out = jax.ShapeDtypeStruct((count, units), BF16)
    return pl.pallas_call(
        up_kernel,
        grid=(count // W,),
        in_specs=[
            pl.BlockSpec((W, model), lambda i: (i, 0)),
            pl.BlockSpec((model, units), lambda i: (0, 0)),
        ],
        out_specs=[pl.BlockSpec((W, units), lambda i: (i, 0))] * 2,
        out_shape=[out, out],
        compiler_params=pltpu.CompilerParams(vmem_limit_bytes=VMEM_BYTES),
        cost_estimate=pl.CostEstimate(
            flops=2 * count * model * units,
            bytes_accessed=count * (model + 2 * units) * 2 + model * units * 2,
            transcendentals=count * units,
        ),
        name="up_project",
    )(rows, weight)


def after(value, *others):
    return lax.optimization_barrier((value, *others))


def hold(value, *others):
    for arr in others:
        value = value + (arr[0, 0] * 0).astype(value.dtype)
    return value


def gather_weight(shard):
    if lax.axis_size(("mph", "mpl")) == 2:
        whole = lax.all_gather(shard, ("mph", "mpl") + ORIG_DP, axis=0, tiled=True)
        model = whole.shape[0] // 2
        first = lax.axis_index(GRP) * model
    else:
        whole = regroup(lax.all_gather(shard, ORIG_DP, axis=0, tiled=True), True)
        model, first = whole.shape[0], 0

    def take(start, stop):
        return lax.dynamic_slice(whole, (first, start), (model, stop - start))

    return whole, take


def scatter_moved(moved):
    return lax.psum_scatter(moved, ORIG_DP, scatter_dimension=0, tiled=True)


def local(
    tokens,
    prefix,
    init_state,
    cotangent,
    norm_gains,
    gate_bias,
    rel_table,
    tok_in_proj,
    tok_out_proj,
    st_in_proj,
    st_out_proj,
    mlp_up,
    mlp_down,
):
    rows = tokens.shape[1]
    model = tokens.shape[2]
    size = lax.axis_size(GRP)
    rank = lax.axis_index(GRP)
    seq_len = rows * size
    blocks = seq_len // W
    shard = tok_in_proj.shape[0]
    local_w = tok_in_proj.shape[2]
    heads = rel_table.shape[1]
    units = mlp_up.shape[1]

    small = jnp.concatenate([norm_gains, gate_bias[None]], 0).T
    entries = rel_table.shape[0]
    extra = jnp.zeros((shard, EXTRA), BF16)
    extra = lax.dynamic_update_slice(extra, small, (0, 0))
    extra = lax.dynamic_update_slice(extra, rel_table, (0, 4))
    digits = jnp.stack([prefix // 64, prefix % 64], 1).astype(BF16)
    extra = lax.dynamic_update_slice(extra, digits, (0, 4 + heads))
    tok_rows = regroup(tokens[0], True)
    wide = 4 * local_w
    shard_tin = tok_in_proj.reshape(shard, wide)
    shard_sin = st_in_proj.reshape(shard, wide)
    first, take_first = gather_weight(jnp.concatenate([shard_tin, extra], 1))
    second = jnp.concatenate([shard_sin, st_out_proj.reshape(2 * local_w, shard).T], 1)
    third = jnp.concatenate(
        [mlp_up, mlp_down.T, tok_out_proj.reshape(2 * local_w, shard).T], 1
    )
    second, take_second = gather_weight(hold(second, first, tok_rows))
    extra = take_first(wide, wide + EXTRA)
    w_tin = take_first(0, wide)
    small = extra[:, :4].T.astype(F32)
    by_seq = extra.reshape(-1, shard, EXTRA)
    table = by_seq[:, :entries, 4 : 4 + heads].reshape(-1, heads).astype(F32)
    seq = lax.axis_index(("dph", "mph"))
    digits = lax.dynamic_index_in_dim(by_seq[:, 0, 4 + heads : 6 + heads], seq, 0, False)
    digits = digits.astype(jnp.int32)
    prefix_len = digits[0] * 64 + digits[1]
    start = regroup(hold(init_state[0], tok_rows), True)
    if size == 2:
        other = shift(start, 1)
        state0 = jnp.where(
            rank == 0,
            jnp.concatenate([start, other], 0),
            jnp.concatenate([other, start], 0),
        )
    else:
        state0 = lax.all_gather(start, GRP, axis=0, tiled=True)

    gain1, gain2, gain3 = small[0:1], small[1:2], small[2:3]
    gate = jax.nn.sigmoid(small[3:4])
    near = near_bias(table * LOG2E)
    base = jnp.stack([rank.astype(jnp.int32) * (rows // W), prefix_len])

    def where_at(block):
        return jnp.concatenate([base, jnp.full((1,), block, jnp.int32)])

    tok_f = tok_rows.astype(F32)
    unit1, inv1 = normalize(tok_f)
    normed = gather_rot((unit1 * gain1).astype(BF16))
    normed, near, state0 = lax.optimization_barrier((normed, near, state0))
    proj = dot_nn(normed, w_tin).astype(BF16)
    att, lse_tok = self_forward(where_at(0), proj, near)
    third, take_third = gather_weight(hold(third, second, att))
    w_sin, w_sout = take_second(0, wide), take_second(wide, wide + 2 * local_w)
    states, ups = [], []
    prev, mine, theirs, kept = state0, None, None, None
    for block in range(blocks):
        outs = state_forward(
            where_at(block), block, prev, mine, theirs, gain3, gate, w_sin, w_sout, proj, kept, att
        )
        prev, norm_st, sproj, satt, att, lse_st, mine = outs
        kept = (norm_st, sproj, satt, lse_st)
        if block == 1:
            cot_rows, mine = after(cotangent[0], mine)
            cot_rows = regroup(cot_rows, True)
        if block == blocks - 2:
            cot_rows, mine = after(cot_rows, mine)
        if size == 2:
            theirs = shift(mine, 1)
        else:
            theirs = lax.psum(mine.astype(F32), GRP) - mine.astype(F32)
            theirs = theirs.astype(BF16)
        states.append(prev)
        ups.append((mine, theirs))
    w_up, w_down = take_third(0, units), take_third(units, 2 * units)
    w_tout = take_third(2 * units, 2 * units + 2 * local_w)
    final = gate * prev + (1.0 - gate) * (mine.astype(F32) + theirs.astype(F32))
    final_rows = lax.dynamic_slice_in_dim(final, rank * (S // size), S // size, 0)

    def attn_term(first, count):
        return dot_nt(lax.slice_in_dim(att, first, first + count, axis=0), w_tout)

    resid = tok_f + sum_rot(attn_term, rows)
    unit2, inv2 = normalize(resid)
    normed2 = gather_rot((unit2 * gain2).astype(BF16))
    act, slope = up_project(normed2, w_up, units)

    def mlp_term(first, count):
        return dot_nt(lax.slice_in_dim(act, first, first + count, axis=0), w_down)

    mixed = (resid + sum_rot(mlp_term, rows)).astype(BF16)

    cot_all = gather_rot(cot_rows)
    grad_pre = (dot_nn(cot_all, w_down) * slope.astype(F32)).astype(BF16)
    grad_down = regroup(dot_tn(cot_all, act).astype(BF16), False)

    def up_term(first, count):
        return dot_nt(lax.slice_in_dim(grad_pre, first, first + count, axis=0), w_up)

    grad_norm2 = sum_rot(up_term, rows)
    grad_up = regroup(dot_tn(normed2, grad_pre).astype(BF16), False)
    grad_resid = cot_rows.astype(F32) + norm_back(grad_norm2, gain2, unit2, inv2)
    grad_attn = gather_rot(grad_resid.astype(BF16))
    grad_att = dot_nn(grad_attn, w_tout).astype(BF16)
    grad_tout = regroup(dot_tn(grad_attn, att).astype(BF16), False)
    grad_att, grad_down = after(grad_att, grad_down)
    grad_down = scatter_moved(grad_down)

    chain, kept_b, sums = None, None, []
    for block in reversed(range(blocks)):
        outs = state_backward(
            where_at(block),
            block,
            chain,
            states[block],
            gain3,
            gate,
            w_sin,
            w_sout,
            proj,
            grad_att,
            att,
            sproj,
            satt,
            lse_st,
            kept_b,
        )
        later, dupd, dsproj, aux, sum_b, part = outs
        kept_b = (dupd, dsproj, aux)
        sums.append(sum_b)
        if block == blocks - 3:
            part, grad_up = after(part, grad_up)
            grad_up = scatter_moved(grad_up)
        if block == blocks - 5:
            part, grad_tout, grad_down = after(part, grad_tout, grad_down)
            grad_tout = scatter_moved(grad_tout)
        if block == 1:
            part, grad_up = after(part, grad_up)
        if block > 0:
            if size == 2:
                other = shift(part, 1)
            else:
                other = (lax.psum(part.astype(F32), GRP) - part.astype(F32)).astype(BF16)
            chain = (later, part, other, states[block]) + ups[block - 1]
    gate_grad = functools.reduce(jnp.add, sums)[0]
    mixed = regroup(mixed, False)
    final_rows = regroup(final_rows, False)
    grad_sout = dot_tn(dupd, satt).astype(BF16)
    aux, grad_sout, mixed, final_rows, grad_tout = after(
        aux, grad_sout, mixed, final_rows, grad_tout
    )
    grad_sout = regroup(grad_sout, False)
    grad_sin = dot_tn(norm_st, dsproj).astype(BF16)
    aux, grad_sin, grad_sout = after(aux, grad_sin, grad_sout)
    grad_sout = scatter_moved(grad_sout)
    grad_sin = regroup(grad_sin, False)

    grad_proj, cells = self_backward(where_at(0), proj, near, grad_att, att, lse_tok, aux)

    def tok_term(first, count):
        return dot_nt(lax.slice_in_dim(grad_proj, first, first + count, axis=0), w_tin)

    grad_table = table_grad(cells, table.shape[0]).reshape(-1, entries, heads)
    grad_table = jnp.pad(grad_table, ((0, 0), (0, shard - entries), (0, 0)))
    packed = jnp.concatenate([gate_grad[:, None], grad_table.reshape(model, heads)], 1)
    packed = jnp.pad(packed, ((0, 0), (0, EXTRA - 1 - heads))).astype(BF16)
    grad_tin = jnp.concatenate([dot_tn(normed, grad_proj).astype(BF16), packed], 1)
    grad_tin, grad_sin = after(grad_tin, grad_sin)
    grad_sin = scatter_moved(grad_sin)
    grad_proj, grad_tin = after(grad_proj, grad_tin)
    grad_tin = scatter_moved(regroup(grad_tin, False))
    grad_tin, packed = grad_tin[:, :wide], grad_tin[:, wide:].astype(F32)
    grad_norm1 = sum_rot(tok_term, rows)
    input_grad = grad_resid + norm_back(grad_norm1, gain1, unit1, inv1)

    def gain_sum(shard_in, grad):
        return jnp.sum(shard_in.astype(F32) * grad.astype(F32), 1)

    ranks = lax.axis_size(("mph", "mpl"))
    vectors = jnp.stack(
        [
            gain_sum(shard_tin, grad_tin),
            gain_sum(mlp_up, grad_up),
            gain_sum(shard_sin, grad_sin),
            packed[:, 0] / ranks,
        ]
    )
    if ranks == 2:
        vectors = vectors + lax.ppermute(vectors, ("mph", "mpl"), [(0, 1), (1, 0)])
    else:
        vectors = lax.psum(vectors, ("mph", "mpl"))
    gains = vectors[:3] / norm_gains.astype(F32)
    grad_table = packed[:entries, 1 : 1 + heads]

    return (
        mixed[None],
        final_rows[None],
        regroup(input_grad.astype(BF16), False).astype(F32)[None],
        gains,
        vectors[3],
        grad_table,
        grad_tin.astype(F32).reshape(shard, 4, local_w),
        grad_tout.T.astype(F32).reshape(2, local_w, shard),
        grad_sin.astype(F32).reshape(shard, 4, local_w),
        grad_sout.T.astype(F32).reshape(2, local_w, shard),
        grad_up.astype(F32),
        grad_down.T.astype(F32),
    )


def solution(mesh):
    devs = mesh.devices
    dp_n, mp_n = devs.shape
    fine = jax.sharding.Mesh(
        devs.reshape(dp_n // 2, 2, 2, mp_n // 2), ("dph", "core", "mph", "mpl")
    )
    dp, mp = ("dph", "core"), ("mph", "mpl")
    weights = (
        P(None, dp),
        P(dp),
        P(dp, mp),
        P(dp, None, mp),
        P(None, mp, dp),
        P(dp, None, mp),
        P(None, mp, dp),
        P(dp, mp),
        P(mp, dp),
    )
    rows = P(dp, mp, None)
    return jax.shard_map(
        local,
        mesh=fine,
        in_specs=(rows, P(dp), rows, rows) + weights,
        out_specs=(rows, rows, rows) + weights,
        check_vma=False,
    )
```

```python
import functools

import jax
import jax.numpy as jnp
from jax import lax
from jax.experimental import pallas as pl
from jax.experimental.pallas import tpu as pltpu
from jax.sharding import PartitionSpec as P

HD = 128
S = 512
W = 512
TILE = 128
EXTRA = 128

EPS = 1e-06
NEG = -1e30
THRESH = (12, 16, 23, 32, 46, 64, 91)
LOG2E = 1.4426950408889634
SCALE = HD ** (-0.5)
SCALE2 = SCALE * LOG2E
VMEM_BYTES = 60 * 1024 * 1024

GRP = ("mpl", "core")
ORIG_DP = ("dph", "core")
SWAP = ("core", "mph", "mpl")

F32 = jnp.float32
BF16 = jnp.bfloat16


def regroup(arr, forward):
    ranks = lax.axis_size(("mph", "mpl"))
    half = ranks // 2
    pairs = []
    for seq in range(2):
        for rank in range(ranks):
            here = seq * ranks + rank
            there = (rank % 2) * ranks + seq * half + rank // 2
            if here != there:
                pairs.append((here, there) if forward else (there, here))
    moved = lax.ppermute(arr, SWAP, pairs)
    seq, rank = lax.axis_index("core"), lax.axis_index(("mph", "mpl"))
    stays = (rank % 2 == seq) & (rank == seq * half + rank // 2)
    return jnp.where(stays, arr, moved)


def shift(arr, step):
    half = lax.axis_size("mpl")
    size = 2 * half

    def place(rank):
        return (rank % 2) * half + rank // 2

    pairs = [(place(i), place((i + step) % size)) for i in range(size)]
    return lax.ppermute(arr, ("core", "mpl"), pairs)


def gather_rot(rows):
    size = lax.axis_size(GRP)
    return jnp.concatenate([rows] + [shift(rows, -k) for k in range(1, size)], 0)


def sum_rot(term, count):
    size = lax.axis_size(GRP)
    sent = [shift(term(k * count, count).astype(BF16), k) for k in range(1, size)]
    total = term(0, count)
    for piece in sent:
        total = total + piece.astype(F32)
    return total


def dot_nn(left, right):
    return lax.dot_general(left, right, (((1,), (0,)), ((), ())), preferred_element_type=F32)


def dot_tn(left, right):
    return lax.dot_general(left, right, (((0,), (0,)), ((), ())), preferred_element_type=F32)


def dot_nt(left, right):
    return lax.dot_general(left, right, (((1,), (1,)), ((), ())), preferred_element_type=F32)


def normalize(values):
    center = values - jnp.mean(values, -1, keepdims=True)
    spread = jnp.mean(center * center, -1, keepdims=True)
    inv = lax.rsqrt(spread + EPS)
    return center * inv, inv


def norm_back(grad, gain, unit, inv):
    scaled = grad * gain
    mean_g = jnp.mean(scaled, -1, keepdims=True)
    mean_x = jnp.mean(scaled * unit, -1, keepdims=True)
    return inv * (scaled - mean_g - unit * mean_x)


def bucket_of(offset, half):
    distance = jnp.abs(offset)
    far_part = jnp.full(offset.shape, 8, jnp.int32)
    for limit in THRESH:
        far_part = far_part + (distance >= limit).astype(jnp.int32)
    magnitude = jnp.where(distance < 8, distance, far_part)
    return magnitude + half * (offset > 0).astype(jnp.int32)


def near_bias(table):
    entries, heads = table.shape
    diag = lax.broadcasted_iota(jnp.int32, (3, TILE, TILE), 0) - 1
    key_pos = lax.broadcasted_iota(jnp.int32, (3, TILE, TILE), 1)
    query_pos = lax.broadcasted_iota(jnp.int32, (3, TILE, TILE), 2)
    which = bucket_of(diag * TILE + key_pos - query_pos, entries // 2)
    near = jnp.zeros((heads, 3, TILE, TILE), F32)
    for entry in range(entries):
        near = jnp.where((which == entry)[None], table[entry][:, None, None, None], near)
    far = jnp.stack([table[entries // 2 - 1], table[entries - 1]], 1)
    far = jnp.broadcast_to(far[:, :, None, None], (heads, 2, TILE, TILE))
    return jnp.concatenate([near, far], 1)


def tile_slot(kt, qt):
    diag = kt - W // TILE - qt
    return diag + 1 if -1 <= diag <= 1 else (3 if diag < 0 else 4)


def fill_bias(near, bias):
    for h in range(near.shape[0]):
        for kt in range(2 * W // TILE):
            for qt in range(W // TILE):
                bias[h, kt * TILE : (kt + 1) * TILE, qt * TILE : (qt + 1) * TILE] = near[
                    h, tile_slot(kt, qt)
                ]


def table_grad(cells, entries):
    heads = cells.shape[0]
    diag = lax.broadcasted_iota(jnp.int32, (3, TILE, TILE), 0) - 1
    key_pos = lax.broadcasted_iota(jnp.int32, (3, TILE, TILE), 1)
    query_pos = lax.broadcasted_iota(jnp.int32, (3, TILE, TILE), 2)
    which = bucket_of(diag * TILE + key_pos - query_pos, entries // 2)
    rows = lax.broadcasted_iota(jnp.int32, (entries, 1, 1, 1), 0)
    hot = (which[None] == rows).astype(F32)
    near = jnp.stack(
        [jnp.sum(hot * cells[h, :3][None], (1, 2, 3)) for h in range(heads)], 1
    )
    far = jnp.sum(cells[:, 3:], (2, 3))
    entry = lax.broadcasted_iota(jnp.int32, (entries, heads), 0)
    left = jnp.where(entry == entries // 2 - 1, far[:, 0][None], 0.0)
    right = jnp.where(entry == entries - 1, far[:, 1][None], 0.0)
    return near + left + right


def reach_of(block, prefix):
    query = block * W + lax.broadcasted_iota(jnp.int32, (1, W), 1)
    return jnp.where(query < prefix, jnp.maximum(query, prefix - 1), query)


def allowed_keys(block, prefix):
    key = block * W + lax.broadcasted_iota(jnp.int32, (W, W), 0)
    return key <= reach_of(block, prefix)


def soft_unit(logits, values):
    top = jnp.max(logits[0], 0, keepdims=True)
    for part in logits[1:]:
        top = jnp.maximum(top, jnp.max(part, 0, keepdims=True))
    total = None
    acc = None
    for part, vals in zip(logits, values):
        expo = jnp.exp2(part - top)
        summed = jnp.sum(expo, 0, keepdims=True)
        mixed = dot_tn(vals, expo.astype(BF16))
        total = summed if total is None else total + summed
        acc = mixed if acc is None else acc + mixed
    return jnp.transpose(acc / total).astype(BF16), top + jnp.log2(total)


def row_dot(grad_out, out):
    prod = grad_out.astype(F32) * out.astype(F32)
    return jnp.sum(jnp.transpose(prod), 0, keepdims=True)


def back_unit(logits, queries, keys, values, grad_out, lse, delta):
    probs = jnp.exp2(logits - lse)
    grad_probs = dot_nt(values, grad_out)
    grad_values = dot_nn(probs.astype(BF16), grad_out)
    grad_scores = probs * (grad_probs - delta)
    low = grad_scores.astype(BF16)
    grad_keys = dot_nn(low, queries) * SCALE
    grad_queries = dot_tn(keys, low)
    return grad_queries, grad_keys, grad_values, grad_scores


def self_forward_kernel(where, q, kp, kc, vp, vc, near, out, lse, bias):
    block = pl.program_id(0)

    @pl.when(block == 0)
    def _():
        fill_bias(near, bias)

    edge = jnp.where(block == 0, NEG, 0.0)
    allowed = allowed_keys(block, where[1])
    for h in range(bias.shape[0]):
        cols = slice(h * HD, (h + 1) * HD)
        before = dot_nt(kp[:, cols], q[:, cols]) * SCALE2 + (bias[h, :W] + edge)
        here = jnp.where(allowed, dot_nt(kc[:, cols], q[:, cols]) * SCALE2 + bias[h, W:], NEG)
        out[:, cols], lse[0, h : h + 1] = soft_unit(
            (before, here), (vp[:, cols], vc[:, cols])
        )


def self_specs(blocks, local_w, order):
    def at(part, delta):
        def index(i, where):
            block = jnp.maximum(order(i) + delta, 0)
            return ((block + blocks - where[0]) % blocks, part)

        return pl.BlockSpec((W, local_w), index)

    return at


def self_forward(where, proj, near):
    seq_len, width = proj.shape
    local_w = width // 4
    heads = near.shape[0]
    blocks = seq_len // W
    at = self_specs(blocks, local_w, lambda i: i)
    return pl.pallas_call(
        self_forward_kernel,
        grid_spec=pltpu.PrefetchScalarGridSpec(
            num_scalar_prefetch=1,
            grid=(blocks,),
            in_specs=[
                at(0, 0),
                at(2, -1),
                at(2, 0),
                at(3, -1),
                at(3, 0),
                pl.BlockSpec(near.shape, lambda i, where: (0, 0, 0, 0)),
            ],
            out_specs=[
                at(0, 0),
                pl.BlockSpec((1, heads, W), lambda i, where: (i, 0, 0)),
            ],
            scratch_shapes=[pltpu.VMEM((heads, 2 * W, W), F32)],
        ),
        out_shape=[
            jax.ShapeDtypeStruct((seq_len, 2 * local_w), BF16),
            jax.ShapeDtypeStruct((blocks, heads, W), F32),
        ],
        compiler_params=pltpu.CompilerParams(vmem_limit_bytes=VMEM_BYTES),
        cost_estimate=pl.CostEstimate(
            flops=seq_len * 2 * W * local_w * 4,
            bytes_accessed=seq_len * local_w * 12,
            transcendentals=seq_len * 2 * W * heads,
        ),
        name="self_forward",
    )(where, proj, proj, proj, proj, proj, near)


def self_backward_kernel(top, where, q, kp, kc, vp, vc, near, dout, lse, aux, *refs):
    grad_proj, cells, carry, bias = refs[-4:]
    step = pl.program_id(0)
    block = top - step
    edge = jnp.where(block == 0, NEG, 0.0)
    allowed = allowed_keys(block, where[1])
    heads = bias.shape[0]
    local_w = heads * HD
    tiles = W // TILE

    @pl.when(step == 0)
    def _():
        fill_bias(near, bias)
        if len(refs) > 4:
            cells[...] = refs[1][...]
            carry[...] = refs[2][...]
        else:
            carry[...] = jnp.zeros_like(carry)
            cells[...] = jnp.zeros_like(cells)

    for h in range(heads):
        cols = slice(h * HD, (h + 1) * HD)
        vcols = slice(local_w + h * HD, local_w + (h + 1) * HD)
        row_lse = lse[0, h : h + 1]
        before = dot_nt(kp[:, cols], q[:, cols]) * SCALE2 + (bias[h, :W] + edge)
        here = jnp.where(allowed, dot_nt(kc[:, cols], q[:, cols]) * SCALE2 + bias[h, W:], NEG)
        probs0, probs1 = jnp.exp2(before - row_lse), jnp.exp2(here - row_lse)
        prod0 = probs0 * dot_nt(vp[:, cols], dout[:, cols])
        prod1 = probs1 * dot_nt(vc[:, cols], dout[:, cols])
        delta = jnp.sum(prod0, 0, keepdims=True) + jnp.sum(prod1, 0, keepdims=True)
        ds0 = (prod0 - probs0 * delta).astype(BF16)
        ds1 = (prod1 - probs1 * delta).astype(BF16)
        dv0 = dot_nn(probs0.astype(BF16), dout[:, cols])
        dv1 = dot_nn(probs1.astype(BF16), dout[:, cols])
        dk0 = dot_nn(ds0, q[:, cols]) * SCALE
        dk1 = dot_nn(ds1, q[:, cols]) * SCALE
        dq = dot_tn(kp[:, cols], ds0) + dot_tn(kc[:, cols], ds1)
        parts = {0: [], 1: [], 2: [], 3: [], 4: []}
        for kt in range(2 * tiles):
            for qt in range(tiles):
                source, row = (ds0, kt) if kt < tiles else (ds1, kt - tiles)
                cell = source[row * TILE : (row + 1) * TILE, qt * TILE : (qt + 1) * TILE]
                cell = cell.astype(F32)
                parts[tile_slot(kt, qt)].append(cell)
        for slot, group in parts.items():
            cells[h, slot] += functools.reduce(jnp.add, group)
        grad_proj[:, cols] = (jnp.transpose(dq) * SCALE).astype(BF16)
        grad_proj[:, local_w + h * HD : local_w + (h + 1) * HD] = aux[:, cols]
        grad_proj[:, 2 * local_w + h * HD : 2 * local_w + (h + 1) * HD] = (
            dk1 + carry[:, cols] + aux[:, vcols].astype(F32)
        ).astype(BF16)
        grad_proj[:, 3 * local_w + h * HD : 3 * local_w + (h + 1) * HD] = (
            dv1
            + carry[:, vcols]
            + aux[:, 2 * local_w + h * HD : 2 * local_w + (h + 1) * HD].astype(F32)
        ).astype(BF16)
        carry[:, cols] = dk0
        carry[:, vcols] = dv0


def self_backward(top, steps, where, proj, near, grad_att, lse, aux, *kept):
    seq_len, width = proj.shape
    local_w = width // 4
    heads = near.shape[0]
    blocks = seq_len // W

    def order(i):
        return top - i

    at = self_specs(blocks, local_w, order)

    def whole(i, where):
        return ((order(i) + blocks - where[0]) % blocks, 0)

    cell_spec = pl.BlockSpec((heads, 5, TILE, TILE), lambda i, where: (0, 0, 0, 0))
    carry_spec = pl.BlockSpec((W, 2 * local_w), lambda i, where: (0, 0))
    return pl.pallas_call(
        functools.partial(self_backward_kernel, top),
        grid_spec=pltpu.PrefetchScalarGridSpec(
            num_scalar_prefetch=1,
            grid=(steps,),
            in_specs=[
                at(0, 0),
                at(2, -1),
                at(2, 0),
                at(3, -1),
                at(3, 0),
                pl.BlockSpec(near.shape, lambda i, where: (0, 0, 0, 0)),
                at(0, 0),
                pl.BlockSpec((1, heads, W), lambda i, where: (order(i), 0, 0)),
                pl.BlockSpec((W, 3 * local_w), whole),
            ]
            + ([pl.BlockSpec(memory_space=pl.ANY), cell_spec, carry_spec] if kept else []),
            out_specs=[pl.BlockSpec((W, width), whole), cell_spec, carry_spec],
            scratch_shapes=[pltpu.VMEM((heads, 2 * W, W), F32)],
        ),
        out_shape=[
            jax.ShapeDtypeStruct((seq_len, width), BF16),
            jax.ShapeDtypeStruct((heads, 5, TILE, TILE), F32),
            jax.ShapeDtypeStruct((W, 2 * local_w), F32),
        ],
        input_output_aliases={10: 0} if kept else {},
        compiler_params=pltpu.CompilerParams(vmem_limit_bytes=VMEM_BYTES),
        cost_estimate=pl.CostEstimate(
            flops=steps * W * 2 * W * local_w * 20,
            bytes_accessed=steps * W * local_w * 30,
            transcendentals=steps * W * 2 * W * heads,
        ),
        name="self_backward_second" if kept else "self_backward_first",
    )(where, proj, proj, proj, proj, proj, near, grad_att, lse, aux, *kept)


def state_forward_kernel(first, where, *refs):
    refs = list(refs)
    prev = refs.pop(0)
    if not first:
        mine, theirs = refs.pop(0), refs.pop(0)
    gain, gate, w_in, w_out, cq, kc, vc = refs[:7]
    state, norm, sproj, satt, att, lse, part = refs[-7:]
    local_w = cq.shape[1]
    heads = local_w // HD
    if first:
        fresh = prev[...]
    else:
        update = mine[...].astype(F32) + theirs[...].astype(F32)
        fresh = gate[...] * prev[...] + (1.0 - gate[...]) * update
    state[...] = fresh
    unit, _ = normalize(fresh)
    normed = (unit * gain[...]).astype(BF16)
    norm[...] = normed
    for p in range(4):
        cols = slice(p * local_w, (p + 1) * local_w)
        sproj[:, cols] = dot_nn(normed, w_in[:, cols]).astype(BF16)
    for h in range(heads):
        cols = [slice(p * local_w + h * HD, p * local_w + (h + 1) * HD) for p in range(4)]
        sk, sv = sproj[:, cols[2]], sproj[:, cols[3]]
        satt[:, cols[0]], lse[0, h : h + 1] = soft_unit(
            (dot_nt(sk, sproj[:, cols[0]]) * SCALE2,), (sv,)
        )
        satt[:, cols[1]], lse[0, heads + h : heads + h + 1] = soft_unit(
            (dot_nt(kc[:, cols[0]], sproj[:, cols[1]]) * SCALE2,), (vc[:, cols[0]],)
        )
        att[:, cols[0]], lse[0, 2 * heads + h : 2 * heads + h + 1] = soft_unit(
            (dot_nt(sk, cq[:, cols[0]]) * SCALE2,), (sv,)
        )
    part[...] = dot_nt(satt[...], w_out[...]).astype(BF16)


def state_forward(where, block, prev, mine, theirs, gain, gate, w_in, w_out, proj, kept, att):
    first = block == 0
    seq_len, width = proj.shape
    local_w = width // 4
    heads = local_w // HD
    blocks = seq_len // W
    model = prev.shape[1]

    def phys(part):
        return pl.BlockSpec(
            (W, local_w), lambda i, where: ((where[2] + blocks - where[0]) % blocks, part)
        )

    def full(arr):
        return pl.BlockSpec(arr.shape, lambda i, where: (0,) * arr.ndim)

    def row_block(cols):
        return pl.BlockSpec((S, cols), lambda i, where: (where[2], 0))

    anywhere = pl.BlockSpec(memory_space=pl.ANY)
    operands = [prev] + ([] if first else [mine, theirs]) + [gain, gate, w_in, w_out]
    in_specs = [full(arr) for arr in operands] + [phys(1), phys(2), phys(3)]
    operands += [proj, proj, proj]
    aliases = {}
    held = [] if first else list(kept[:3])
    for slot, arr in enumerate(held):
        aliases[1 + len(operands)] = 1 + slot
        operands.append(arr)
        in_specs.append(anywhere)
    aliases[1 + len(operands)] = 4
    operands.append(att)
    in_specs.append(anywhere)
    if not first:
        aliases[1 + len(operands)] = 5
        operands.append(kept[3])
        in_specs.append(anywhere)
    return pl.pallas_call(
        functools.partial(state_forward_kernel, first),
        grid_spec=pltpu.PrefetchScalarGridSpec(
            num_scalar_prefetch=1,
            grid=(1,),
            in_specs=in_specs,
            out_specs=[
                full(prev),
                row_block(model),
                row_block(width),
                row_block(2 * local_w),
                phys(1),
                pl.BlockSpec((1, 3 * heads, S), lambda i, where: (where[2], 0, 0)),
                full(prev),
            ],
        ),
        out_shape=[
            jax.ShapeDtypeStruct(prev.shape, F32),
            jax.ShapeDtypeStruct((blocks * S, model), BF16),
            jax.ShapeDtypeStruct((blocks * S, width), BF16),
            jax.ShapeDtypeStruct((blocks * S, 2 * local_w), BF16),
            jax.ShapeDtypeStruct(att.shape, BF16),
            jax.ShapeDtypeStruct((blocks, 3 * heads, S), F32),
            jax.ShapeDtypeStruct(prev.shape, BF16),
        ],
        input_output_aliases=aliases,
        compiler_params=pltpu.CompilerParams(vmem_limit_bytes=VMEM_BYTES),
        cost_estimate=pl.CostEstimate(
            flops=S * model * local_w * 12 + 3 * S * W * local_w * 4,
            bytes_accessed=(w_in.size + w_out.size) * 2 + S * model * 20,
            transcendentals=3 * S * W * heads,
        ),
        name="state_forward",
    )(where, *operands)


def state_backward_kernel(last, where, *refs):
    refs = list(refs)
    if not last:
        later, mine, theirs, state_next, upd_mine, upd_theirs = refs[:6]
        refs = refs[6:]
    state, gain, gate, w_in, w_out, cq, kc, vc, dcross, cross, sproj, satt, lse = refs[:13]
    dstate, dupd, dsproj, aux, sums, part = refs[-6:]
    local_w = cq.shape[1]
    heads = local_w // HD
    model = state.shape[1]
    gate_f = gate[...]
    if last:
        dstate[...] = jnp.zeros_like(dstate)
        dupd[...] = jnp.zeros_like(dupd)
        gate_sum = jnp.zeros((1, model), F32)
    else:
        unit, inv = normalize(state_next[...])
        grad_norm = mine[...].astype(F32) + theirs[...].astype(F32)
        grad_state = gate_f * later[...] + norm_back(grad_norm, gain[...], unit, inv)
        dstate[...] = grad_state
        update = upd_mine[...].astype(F32) + upd_theirs[...].astype(F32)
        gate_sum = jnp.sum(grad_state * (state[...] - update), 0, keepdims=True)
        gate_sum = gate_sum * gate_f * (1.0 - gate_f)
        dupd[...] = ((1.0 - gate_f) * grad_state).astype(BF16)
    for h in range(heads):
        cols = [slice(p * local_w + h * HD, p * local_w + (h + 1) * HD) for p in range(4)]
        head = cols[0]
        sk, sv = sproj[:, cols[2]], sproj[:, cols[3]]
        delta = row_dot(dcross[:, head], cross[:, head])
        dq, dk, dv, _ = back_unit(
            dot_nt(sk, cq[:, head]) * SCALE2,
            cq[:, head],
            sk,
            sv,
            dcross[:, head],
            lse[0, 2 * heads + h : 2 * heads + h + 1],
            delta,
        )
        aux[:, cols[0]] = (jnp.transpose(dq) * SCALE).astype(BF16)
        if last:
            aux[:, cols[1]] = jnp.zeros((S, HD), BF16)
            aux[:, cols[2]] = jnp.zeros((S, HD), BF16)
            dsproj[:, cols[0]] = jnp.zeros((S, HD), BF16)
            dsproj[:, cols[1]] = jnp.zeros((S, HD), BF16)
        else:
            dself = dot_nn(dupd[...], w_out[:, cols[0]]).astype(BF16)
            dext = dot_nn(dupd[...], w_out[:, cols[1]]).astype(BF16)
            sq = sproj[:, cols[0]]
            dq, dk_s, dv_s, _ = back_unit(
                dot_nt(sk, sq) * SCALE2,
                sq,
                sk,
                sv,
                dself,
                lse[0, h : h + 1],
                row_dot(dself, satt[:, cols[0]]),
            )
            dsproj[:, cols[0]] = (jnp.transpose(dq) * SCALE).astype(BF16)
            dk = dk + dk_s
            dv = dv + dv_s
            sx = sproj[:, cols[1]]
            dq, dk_x, dv_x, _ = back_unit(
                dot_nt(kc[:, head], sx) * SCALE2,
                sx,
                kc[:, head],
                vc[:, head],
                dext,
                lse[0, heads + h : heads + h + 1],
                row_dot(dext, satt[:, cols[1]]),
            )
            dsproj[:, cols[1]] = (jnp.transpose(dq) * SCALE).astype(BF16)
            aux[:, cols[1]] = dk_x.astype(BF16)
            aux[:, cols[2]] = dv_x.astype(BF16)
        dsproj[:, cols[2]] = dk.astype(BF16)
        dsproj[:, cols[3]] = dv.astype(BF16)
    part[...] = dot_nt(dsproj[...], w_in[...]).astype(BF16)
    sums[...] = jnp.broadcast_to(gate_sum, sums.shape)


def state_backward(
    where, block, chain, state, gain, gate, w_in, w_out, proj, grad_att, att, sproj, satt, lse, kept
):
    seq_len, width = proj.shape
    local_w = width // 4
    heads = local_w // HD
    blocks = seq_len // W
    last = block == blocks - 1
    model = state.shape[1]

    def phys(part):
        return pl.BlockSpec(
            (W, local_w), lambda i, where: ((where[2] + blocks - where[0]) % blocks, part)
        )

    def full(arr):
        return pl.BlockSpec(arr.shape, lambda i, where: (0,) * arr.ndim)

    def row_block(cols):
        return pl.BlockSpec((S, cols), lambda i, where: (where[2], 0))

    anywhere = pl.BlockSpec(memory_space=pl.ANY)
    operands = ([] if last else list(chain)) + [state, gain, gate, w_in, w_out]
    in_specs = [full(arr) for arr in operands]
    operands += [proj, proj, proj, grad_att, att, sproj, satt, lse]
    in_specs += [phys(1), phys(2), phys(3), phys(1), phys(1)]
    in_specs += [row_block(width), row_block(2 * local_w)]
    in_specs += [pl.BlockSpec((1, 3 * heads, S), lambda i, where: (where[2], 0, 0))]
    aliases = {}
    if not last:
        for slot, arr in enumerate(kept):
            aliases[1 + len(operands)] = 1 + slot
            operands.append(arr)
            in_specs.append(anywhere)
    return pl.pallas_call(
        functools.partial(state_backward_kernel, last),
        grid_spec=pltpu.PrefetchScalarGridSpec(
            num_scalar_prefetch=1,
            grid=(1,),
            in_specs=in_specs,
            out_specs=[
                full(state),
                row_block(model),
                row_block(width),
                pl.BlockSpec(
                    (W, 3 * local_w),
                    lambda i, where: ((where[2] + blocks - where[0]) % blocks, 0),
                ),
                pl.BlockSpec((8, model), lambda i, where: (0, 0)),
                full(state),
            ],
        ),
        out_shape=[
            jax.ShapeDtypeStruct(state.shape, F32),
            jax.ShapeDtypeStruct((blocks * S, model), BF16),
            jax.ShapeDtypeStruct((blocks * S, width), BF16),
            jax.ShapeDtypeStruct((seq_len, 3 * local_w), BF16),
            jax.ShapeDtypeStruct((8, model), F32),
            jax.ShapeDtypeStruct(state.shape, BF16),
        ],
        input_output_aliases=aliases,
        compiler_params=pltpu.CompilerParams(vmem_limit_bytes=VMEM_BYTES),
        cost_estimate=pl.CostEstimate(
            flops=S * model * local_w * 12 + 3 * S * W * local_w * 10,
            bytes_accessed=(w_in.size + w_out.size) * 2 + S * model * 40,
            transcendentals=3 * S * W * heads,
        ),
        name="state_backward",
    )(where, *operands)


def partner_copy(send, recv, sems, slot):
    other = {"core": 1 - lax.axis_index("core")}
    return pltpu.make_async_remote_copy(
        src_ref=send.at[slot],
        dst_ref=recv.at[slot],
        send_sem=sems.at[0, slot],
        recv_sem=sems.at[1, slot],
        device_id=other,
        device_id_type=pl.DeviceIdType.MESH,
    )


def greet():
    barrier = pltpu.get_barrier_semaphore()
    other = {"core": 1 - lax.axis_index("core")}
    pl.semaphore_signal(barrier, inc=1, device_id=other, device_id_type=pl.DeviceIdType.MESH)
    pl.semaphore_wait(barrier, 1)


def chain_forward_kernel(
    state0,
    gain,
    gate,
    w_in,
    w_out,
    cq,
    kc,
    vc,
    held,
    states,
    norm,
    sproj,
    satt,
    att,
    lse,
    final,
    state,
    send,
    recv,
    sems,
):
    step = pl.program_id(0)
    steps = pl.num_programs(0)
    slot = lax.rem(step, 2)
    before = lax.rem(step + 1, 2)
    local_w = cq.shape[1]
    heads = local_w // HD

    @pl.when(step == 0)
    def _():
        greet()
        state[...] = state0[...]

    @pl.when(step > 0)
    def _():
        partner_copy(send, recv, sems, before).wait()
        update = send[before].astype(F32) + recv[before].astype(F32)
        state[...] = gate[...] * state[...] + (1.0 - gate[...]) * update

    fresh = state[...]
    states[...] = fresh
    unit, _ = normalize(fresh)
    normed = (unit * gain[...]).astype(BF16)
    norm[...] = normed
    for p in range(4):
        cols = slice(p * local_w, (p + 1) * local_w)
        sproj[:, cols] = dot_nn(normed, w_in[:, cols]).astype(BF16)
    for h in range(heads):
        cols = [slice(p * local_w + h * HD, p * local_w + (h + 1) * HD) for p in range(4)]
        sk, sv = sproj[:, cols[2]], sproj[:, cols[3]]
        satt[:, cols[0]], lse[0, h : h + 1] = soft_unit(
            (dot_nt(sk, sproj[:, cols[0]]) * SCALE2,), (sv,)
        )
        satt[:, cols[1]], lse[0, heads + h : heads + h + 1] = soft_unit(
            (dot_nt(kc[:, cols[0]], sproj[:, cols[1]]) * SCALE2,), (vc[:, cols[0]],)
        )
    send[slot] = dot_nt(satt[...], w_out[...]).astype(BF16)
    copy = partner_copy(send, recv, sems, slot)
    copy.start()
    for h in range(heads):
        cols = [slice(p * local_w + h * HD, p * local_w + (h + 1) * HD) for p in range(4)]
        sk, sv = sproj[:, cols[2]], sproj[:, cols[3]]
        att[:, cols[0]], lse[0, 2 * heads + h : 2 * heads + h + 1] = soft_unit(
            (dot_nt(sk, cq[:, cols[0]]) * SCALE2,), (sv,)
        )

    @pl.when(step == steps - 1)
    def _():
        copy.wait()
        update = send[slot].astype(F32) + recv[slot].astype(F32)
        final[...] = gate[...] * state[...] + (1.0 - gate[...]) * update


def rotated(block, blocks, local_blocks, part):
    return (lax.rem(block + blocks - lax.axis_index("core") * local_blocks, blocks), part)


def chain_forward(state0, gain, gate, w_in, w_out, proj, att):
    seq_len, width = proj.shape
    local_w = width // 4
    heads = local_w // HD
    blocks = seq_len // W
    local_blocks = blocks // 2
    model = state0.shape[1]

    def phys(part):
        return pl.BlockSpec((W, local_w), lambda i: rotated(i, blocks, local_blocks, part))

    def full(arr):
        return pl.BlockSpec(arr.shape, lambda i: (0,) * arr.ndim, pipeline_mode=pl.Buffered(1))

    def row_block(cols):
        return pl.BlockSpec((S, cols), lambda i: (i, 0))

    return pl.pallas_call(
        chain_forward_kernel,
        grid=(blocks,),
        in_specs=[full(arr) for arr in (state0, gain, gate, w_in, w_out)]
        + [phys(1), phys(2), phys(3), pl.BlockSpec(memory_space=pl.ANY)],
        out_specs=[
            row_block(model),
            row_block(model),
            row_block(width),
            row_block(2 * local_w),
            phys(1),
            pl.BlockSpec((1, 3 * heads, S), lambda i: (i, 0, 0)),
            pl.BlockSpec((S, model), lambda i: (0, 0)),
        ],
        out_shape=[
            jax.ShapeDtypeStruct((blocks * S, model), F32),
            jax.ShapeDtypeStruct((blocks * S, model), BF16),
            jax.ShapeDtypeStruct((blocks * S, width), BF16),
            jax.ShapeDtypeStruct((blocks * S, 2 * local_w), BF16),
            jax.ShapeDtypeStruct(att.shape, BF16),
            jax.ShapeDtypeStruct((blocks, 3 * heads, S), F32),
            jax.ShapeDtypeStruct((S, model), F32),
        ],
        scratch_shapes=[
            pltpu.VMEM((S, model), F32),
            pltpu.VMEM((2, S, model), BF16),
            pltpu.VMEM((2, S, model), BF16),
            pltpu.SemaphoreType.DMA((2, 2)),
        ],
        input_output_aliases={8: 4},
        compiler_params=pltpu.CompilerParams(
            vmem_limit_bytes=VMEM_BYTES, collective_id=0, has_side_effects=True
        ),
        cost_estimate=pl.CostEstimate(
            flops=blocks * (S * model * local_w * 12 + 3 * S * W * local_w * 8),
            bytes_accessed=blocks * S * model * 12,
            transcendentals=blocks * 3 * S * W * heads,
        ),
        name="chain_forward",
    )(state0, gain, gate, w_in, w_out, proj, proj, proj, att)


def chain_backward_kernel(top, steps, start, *refs):
    refs = list(refs)
    later = None if start else refs.pop(0)
    state, state_next, gain, gate, w_in, w_out, cq, kc, vc, dcross, cross, sproj, satt, lse = refs[
        :14
    ]
    refs = refs[14:] if start else refs[17:]
    dupd, dsproj, aux, sums, leave, dstate, dkv, send, recv, sems = refs
    step = pl.program_id(0)
    slot = lax.rem(step, 2)
    before = lax.rem(step + 1, 2)
    local_w = cq.shape[1]
    heads = local_w // HD
    gate_f = gate[...]
    finish = top - steps + 1 == 0

    def absorb(where, at):
        grad_norm = send[where].astype(F32) + recv[where].astype(F32)
        unit, inv = normalize(at[...])
        dstate[...] = gate_f * dstate[...] + norm_back(grad_norm, gain[...], unit, inv)

    @pl.when(step == 0)
    def _():
        greet()
        sums[...] = jnp.zeros_like(sums)
        dstate[...] = jnp.zeros_like(dstate) if start else later[...]

    for h in range(heads):
        cols = [slice(p * local_w + h * HD, p * local_w + (h + 1) * HD) for p in range(4)]
        head = cols[0]
        sk, sv = sproj[:, cols[2]], sproj[:, cols[3]]
        dq, dk, dv, _ = back_unit(
            dot_nt(sk, cq[:, head]) * SCALE2,
            cq[:, head],
            sk,
            sv,
            dcross[:, head],
            lse[0, 2 * heads + h : 2 * heads + h + 1],
            row_dot(dcross[:, head], cross[:, head]),
        )
        aux[:, head] = (jnp.transpose(dq) * SCALE).astype(BF16)
        dkv[:, cols[0]] = dk
        dkv[:, cols[1]] = dv

    @pl.when(step > 0)
    def _():
        partner_copy(send, recv, sems, before).wait()
        absorb(before, state_next)

    grad_state = dstate[...]
    change = jnp.sum(grad_state * (state[...] - state_next[...]), 0, keepdims=True)
    sums[...] += jnp.broadcast_to(change * gate_f, sums.shape)
    dupd[...] = ((1.0 - gate_f) * grad_state).astype(BF16)
    for h in range(heads):
        cols = [slice(p * local_w + h * HD, p * local_w + (h + 1) * HD) for p in range(4)]
        head = cols[0]
        sk, sv = sproj[:, cols[2]], sproj[:, cols[3]]
        dself = dot_nn(dupd[...], w_out[:, cols[0]]).astype(BF16)
        dext = dot_nn(dupd[...], w_out[:, cols[1]]).astype(BF16)
        sq = sproj[:, cols[0]]
        dq, dk, dv, _ = back_unit(
            dot_nt(sk, sq) * SCALE2,
            sq,
            sk,
            sv,
            dself,
            lse[0, h : h + 1],
            row_dot(dself, satt[:, cols[0]]),
        )
        dsproj[:, cols[0]] = (jnp.transpose(dq) * SCALE).astype(BF16)
        dsproj[:, cols[2]] = (dk + dkv[:, cols[0]]).astype(BF16)
        dsproj[:, cols[3]] = (dv + dkv[:, cols[1]]).astype(BF16)
        sx = sproj[:, cols[1]]
        dq, dk, dv, _ = back_unit(
            dot_nt(kc[:, head], sx) * SCALE2,
            sx,
            kc[:, head],
            vc[:, head],
            dext,
            lse[0, heads + h : heads + h + 1],
            row_dot(dext, satt[:, cols[1]]),
        )
        dsproj[:, cols[1]] = (jnp.transpose(dq) * SCALE).astype(BF16)
        aux[:, cols[1]] = dk.astype(BF16)
        aux[:, cols[2]] = dv.astype(BF16)

    def pass_on():
        send[slot] = dot_nt(dsproj[...], w_in[...]).astype(BF16)
        partner_copy(send, recv, sems, slot).start()

    if finish:
        pl.when(step < steps - 1)(pass_on)

        @pl.when(step == steps - 1)
        def _():
            leave[...] = jnp.zeros_like(leave)
    else:
        pass_on()

        @pl.when(step == steps - 1)
        def _():
            partner_copy(send, recv, sems, slot).wait()
            absorb(slot, state)
            leave[...] = dstate[...]


def chain_backward(
    top, steps, later, states, gain, gate, w_in, w_out, proj, grad_att, att, sproj, satt, lse, kept
):
    seq_len, width = proj.shape
    local_w = width // 4
    heads = local_w // HD
    blocks = seq_len // W
    local_blocks = blocks // 2
    model = states.shape[1]
    start = later is None

    def phys(part):
        return pl.BlockSpec((W, local_w), lambda i: rotated(top - i, blocks, local_blocks, part))

    def full(arr):
        return pl.BlockSpec(arr.shape, lambda i: (0,) * arr.ndim, pipeline_mode=pl.Buffered(1))

    def row_block(cols):
        return pl.BlockSpec((S, cols), lambda i: (top - i, 0))

    operands = [] if start else [later]
    in_specs = [full(arr) for arr in operands]
    operands += [states, states, gain, gate, w_in, w_out]
    in_specs += [
        row_block(model),
        pl.BlockSpec((S, model), lambda i: (jnp.minimum(top - i + 1, blocks - 1), 0)),
    ]
    in_specs += [full(arr) for arr in operands[-4:]]
    operands += [proj, proj, proj, grad_att, att, sproj, satt, lse]
    in_specs += [phys(1), phys(2), phys(3), phys(1), phys(1)]
    in_specs += [row_block(width), row_block(2 * local_w)]
    in_specs += [pl.BlockSpec((1, 3 * heads, S), lambda i: (top - i, 0, 0))]
    aliases = {}
    if not start:
        for place, arr in enumerate(kept):
            aliases[len(operands)] = place
            operands.append(arr)
            in_specs.append(pl.BlockSpec(memory_space=pl.ANY))
    return pl.pallas_call(
        functools.partial(chain_backward_kernel, top, steps, start),
        grid=(steps,),
        in_specs=in_specs,
        out_specs=[
            row_block(model),
            row_block(width),
            pl.BlockSpec((W, 3 * local_w), lambda i: rotated(top - i, blocks, local_blocks, 0)),
            pl.BlockSpec((8, model), lambda i: (0, 0)),
            pl.BlockSpec((S, model), lambda i: (0, 0)),
        ],
        out_shape=[
            jax.ShapeDtypeStruct((blocks * S, model), BF16),
            jax.ShapeDtypeStruct((blocks * S, width), BF16),
            jax.ShapeDtypeStruct((seq_len, 3 * local_w), BF16),
            jax.ShapeDtypeStruct((8, model), F32),
            jax.ShapeDtypeStruct((S, model), F32),
        ],
        scratch_shapes=[
            pltpu.VMEM((S, model), F32),
            pltpu.VMEM((S, 2 * local_w), F32),
            pltpu.VMEM((2, S, model), BF16),
            pltpu.VMEM((2, S, model), BF16),
            pltpu.SemaphoreType.DMA((2, 2)),
        ],
        input_output_aliases=aliases,
        compiler_params=pltpu.CompilerParams(
            vmem_limit_bytes=VMEM_BYTES,
            collective_id=1 if start else 2,
            has_side_effects=True,
        ),
        cost_estimate=pl.CostEstimate(
            flops=steps * (S * model * local_w * 12 + 3 * S * W * local_w * 12),
            bytes_accessed=steps * S * model * 24,
            transcendentals=steps * 3 * S * W * heads,
        ),
        name="chain_backward_first" if start else "chain_backward_second",
    )(*operands)


def up_kernel(rows, weight, act, slope):
    step = min(512, weight.shape[1])
    root = 0.7978845608028654
    for start in range(0, weight.shape[1], step):
        cols = slice(start, start + step)
        pre = dot_nn(rows[...], weight[:, cols])
        square = pre * pre
        half = 0.5 * jnp.tanh(pre * (root + (root * 0.044715) * square)) + 0.5
        value = pre * half
        act[:, cols] = value.astype(BF16)
        rise = 2.0 * root + (6.0 * root * 0.044715) * square
        slope[:, cols] = (half + value * (1.0 - half) * rise).astype(BF16)


def up_project(rows, weight, units):
    count, model = rows.shape
    out = jax.ShapeDtypeStruct((count, units), BF16)
    return pl.pallas_call(
        up_kernel,
        grid=(count // W,),
        in_specs=[
            pl.BlockSpec((W, model), lambda i: (i, 0)),
            pl.BlockSpec((model, units), lambda i: (0, 0)),
        ],
        out_specs=[pl.BlockSpec((W, units), lambda i: (i, 0))] * 2,
        out_shape=[out, out],
        compiler_params=pltpu.CompilerParams(vmem_limit_bytes=VMEM_BYTES),
        cost_estimate=pl.CostEstimate(
            flops=2 * count * model * units,
            bytes_accessed=count * (model + 2 * units) * 2 + model * units * 2,
            transcendentals=count * units,
        ),
        name="up_project",
    )(rows, weight)


def after(value, *others):
    return lax.optimization_barrier((value, *others))


def hold(value, *others):
    for arr in others:
        value = value + (arr[0, 0] * 0).astype(value.dtype)
    return value


def gather_weight(shard):
    if lax.axis_size(("mph", "mpl")) == 2:
        whole = lax.all_gather(shard, ("mph", "mpl") + ORIG_DP, axis=0, tiled=True)
        model = whole.shape[0] // 2
        first = lax.axis_index(GRP) * model
    else:
        whole = regroup(lax.all_gather(shard, ORIG_DP, axis=0, tiled=True), True)
        model, first = whole.shape[0], 0

    def take(start, stop):
        return lax.dynamic_slice(whole, (first, start), (model, stop - start))

    return whole, take


def scatter_moved(moved):
    return lax.psum_scatter(moved, ORIG_DP, scatter_dimension=0, tiled=True)


def local(
    tokens,
    prefix,
    init_state,
    cotangent,
    norm_gains,
    gate_bias,
    rel_table,
    tok_in_proj,
    tok_out_proj,
    st_in_proj,
    st_out_proj,
    mlp_up,
    mlp_down,
):
    rows = tokens.shape[1]
    model = tokens.shape[2]
    size = lax.axis_size(GRP)
    rank = lax.axis_index(GRP)
    seq_len = rows * size
    blocks = seq_len // W
    shard = tok_in_proj.shape[0]
    local_w = tok_in_proj.shape[2]
    heads = rel_table.shape[1]
    units = mlp_up.shape[1]

    small = jnp.concatenate([norm_gains, gate_bias[None]], 0).T
    entries = rel_table.shape[0]
    extra = jnp.zeros((shard, EXTRA), BF16)
    extra = lax.dynamic_update_slice(extra, small, (0, 0))
    extra = lax.dynamic_update_slice(extra, rel_table, (0, 4))
    digits = jnp.stack([prefix // 64, prefix % 64], 1).astype(BF16)
    extra = lax.dynamic_update_slice(extra, digits, (0, 4 + heads))
    tok_rows = regroup(tokens[0], True)
    wide = 4 * local_w
    shard_tin = tok_in_proj.reshape(shard, wide)
    shard_sin = st_in_proj.reshape(shard, wide)
    first, take_first = gather_weight(jnp.concatenate([shard_tin, extra], 1))
    second = jnp.concatenate([shard_sin, st_out_proj.reshape(2 * local_w, shard).T], 1)
    third = jnp.concatenate([mlp_up, tok_out_proj.reshape(2 * local_w, shard).T], 1)
    second, take_second = gather_weight(hold(second, first, tok_rows))
    extra = take_first(wide, wide + EXTRA)
    w_tin = take_first(0, wide)
    small = extra[:, :4].T.astype(F32)
    by_seq = extra.reshape(-1, shard, EXTRA)
    table = by_seq[:, :entries, 4 : 4 + heads].reshape(-1, heads).astype(F32)
    seq = lax.axis_index(("dph", "mph"))
    digits = lax.dynamic_index_in_dim(by_seq[:, 0, 4 + heads : 6 + heads], seq, 0, False)
    digits = digits.astype(jnp.int32)
    prefix_len = digits[0] * 64 + digits[1]
    start = regroup(hold(init_state[0], tok_rows), True)
    if size == 2:
        other = shift(start, 1)
        state0 = jnp.where(
            rank == 0,
            jnp.concatenate([start, other], 0),
            jnp.concatenate([other, start], 0),
        )
    else:
        state0 = lax.all_gather(start, GRP, axis=0, tiled=True)

    gain1, gain2, gain3 = small[0:1], small[1:2], small[2:3]
    gate = jax.nn.sigmoid(small[3:4])
    near = near_bias(table * LOG2E)
    base = jnp.stack([rank.astype(jnp.int32) * (rows // W), prefix_len])

    def where_at(block):
        return jnp.concatenate([base, jnp.full((1,), block, jnp.int32)])

    tok_f = tok_rows.astype(F32)
    unit1, inv1 = normalize(tok_f)
    normed = gather_rot((unit1 * gain1).astype(BF16))
    normed, near, state0 = lax.optimization_barrier((normed, near, state0))
    proj = dot_nn(normed, w_tin).astype(BF16)
    att, lse_tok = self_forward(where_at(0), proj, near)
    third, take_third = gather_weight(hold(third, second, att))
    w_sin, w_sout = take_second(0, wide), take_second(wide, wide + 2 * local_w)
    if size == 2:
        w_sout, cot_rows = after(w_sout, cotangent[0])
        cot_rows = regroup(cot_rows, True)
        outs = chain_forward(state0, gain3, gate, w_sin, w_sout, proj, att)
        states, norm_st, sproj, satt, att, lse_st, final = outs
        att, cot_rows = after(att, cot_rows)
    else:
        cot_rows = regroup(cotangent[0], True)
        states, ups = [], []
        prev, mine, theirs, kept = state0, None, None, None
        for block in range(blocks):
            outs = state_forward(
                where_at(block),
                block,
                prev,
                mine,
                theirs,
                gain3,
                gate,
                w_sin,
                w_sout,
                proj,
                kept,
                att,
            )
            prev, norm_st, sproj, satt, att, lse_st, mine = outs
            kept = (norm_st, sproj, satt, lse_st)
            theirs = lax.psum(mine.astype(F32), GRP) - mine.astype(F32)
            theirs = theirs.astype(BF16)
            states.append(prev)
            ups.append((mine, theirs))
        final = gate * prev + (1.0 - gate) * (mine.astype(F32) + theirs.astype(F32))
    fourth, take_fourth = gather_weight(hold(mlp_down.T, third, att))
    w_up, w_tout = take_third(0, units), take_third(units, units + 2 * local_w)
    w_down = take_fourth(0, units)
    final_rows = lax.dynamic_slice_in_dim(final, rank * (S // size), S // size, 0)
    final_rows = regroup(final_rows, False)

    def attn_term(first, count):
        return dot_nt(lax.slice_in_dim(att, first, first + count, axis=0), w_tout)

    resid = tok_f + sum_rot(attn_term, rows)
    unit2, inv2 = normalize(resid)
    normed2 = gather_rot((unit2 * gain2).astype(BF16))
    act, slope = up_project(normed2, w_up, units)

    def mlp_term(first, count):
        return dot_nt(lax.slice_in_dim(act, first, first + count, axis=0), w_down)

    mixed = (resid + sum_rot(mlp_term, rows)).astype(BF16)

    cot_all = gather_rot(cot_rows)
    grad_pre = (dot_nn(cot_all, w_down) * slope.astype(F32)).astype(BF16)
    grad_down = regroup(dot_tn(cot_all, act).astype(BF16), False)

    def up_term(first, count):
        return dot_nt(lax.slice_in_dim(grad_pre, first, first + count, axis=0), w_up)

    grad_norm2 = sum_rot(up_term, rows)
    grad_up = regroup(dot_tn(normed2, grad_pre).astype(BF16), False)
    grad_resid = cot_rows.astype(F32) + norm_back(grad_norm2, gain2, unit2, inv2)
    grad_attn = gather_rot(grad_resid.astype(BF16))
    grad_att = dot_nn(grad_attn, w_tout).astype(BF16)
    grad_tout = regroup(dot_tn(grad_attn, att).astype(BF16), False)
    grad_att, grad_down, final_rows = after(grad_att, grad_down, final_rows)
    grad_down = scatter_moved(grad_down)

    if size == 2:
        half = blocks // 2
        shared = (states, gain3, gate, w_sin, w_sout, proj, grad_att, att, sproj, satt, lse_st)
        dupd, dsproj, aux, sums, later = chain_backward(blocks - 1, half, None, *shared, None)
        later, grad_up, grad_down = after(later, grad_up, grad_down)
        grad_up = scatter_moved(grad_up)
        dupd, dsproj, aux, more, _ = chain_backward(
            half - 1, half, later, *shared, (dupd, dsproj, aux)
        )
        gate_grad = sums[0] + more[0]
        aux, grad_tout = after(aux, grad_tout)
        grad_tout = scatter_moved(grad_tout)
    else:
        grad_up, grad_tout = scatter_moved(grad_up), scatter_moved(grad_tout)
        chain, kept_b, sums = None, None, []
        for block in reversed(range(blocks)):
            outs = state_backward(
                where_at(block),
                block,
                chain,
                states[block],
                gain3,
                gate,
                w_sin,
                w_sout,
                proj,
                grad_att,
                att,
                sproj,
                satt,
                lse_st,
                kept_b,
            )
            later, dupd, dsproj, aux, sum_b, part = outs
            kept_b = (dupd, dsproj, aux)
            sums.append(sum_b)
            if block > 0:
                other = (lax.psum(part.astype(F32), GRP) - part.astype(F32)).astype(BF16)
                chain = (later, part, other, states[block]) + ups[block - 1]
        gate_grad = functools.reduce(jnp.add, sums)[0]
    grad_sout = dot_tn(dupd, satt).astype(BF16)
    grad_sout = regroup(grad_sout, False)
    grad_sin = dot_tn(norm_st, dsproj).astype(BF16)
    aux, grad_sin, grad_sout, grad_up = after(aux, grad_sin, grad_sout, grad_up)
    grad_sout = scatter_moved(grad_sout)
    grad_sin = regroup(grad_sin, False)

    half = blocks // 2
    shared = (where_at(0), proj, near, grad_att, lse_tok, aux)
    grad_proj, cells, carry = self_backward(blocks - 1, half, *shared)
    carry, grad_tout, grad_sin = after(carry, grad_tout, grad_sin)
    grad_sin = scatter_moved(grad_sin)
    grad_proj, cells, _ = self_backward(half - 1, half, *shared, grad_proj, cells, carry)
    grad_proj, grad_sout = after(grad_proj, grad_sout)

    def tok_term(first, count):
        return dot_nt(lax.slice_in_dim(grad_proj, first, first + count, axis=0), w_tin)

    grad_table = table_grad(cells, table.shape[0]).reshape(-1, entries, heads)
    grad_table = jnp.pad(grad_table, ((0, 0), (0, shard - entries), (0, 0)))
    packed = jnp.concatenate([gate_grad[:, None], grad_table.reshape(model, heads)], 1)
    packed = jnp.pad(packed, ((0, 0), (0, EXTRA - 1 - heads))).astype(BF16)
    grad_tin = jnp.concatenate([dot_tn(normed, grad_proj).astype(BF16), packed], 1)
    grad_proj, grad_tin = after(grad_proj, grad_tin)
    grad_tin, mixed = after(regroup(grad_tin, False), mixed)
    mixed = regroup(mixed, False)
    if size == 2:
        sent = shift(tok_term(rows, rows).astype(BF16), 1)
        sent, grad_tin = after(sent, grad_tin)
        grad_norm1 = tok_term(0, rows) + sent.astype(F32)
    else:
        grad_norm1 = sum_rot(tok_term, rows)
    grad_tin = scatter_moved(grad_tin)
    grad_tin, packed = grad_tin[:, :wide], grad_tin[:, wide:].astype(F32)
    input_grad = grad_resid + norm_back(grad_norm1, gain1, unit1, inv1)

    def gain_sum(shard_in, grad):
        return jnp.sum(shard_in.astype(F32) * grad.astype(F32), 1)

    ranks = lax.axis_size(("mph", "mpl"))
    vectors = jnp.stack(
        [
            gain_sum(shard_tin, grad_tin),
            gain_sum(mlp_up, grad_up),
            gain_sum(shard_sin, grad_sin),
            packed[:, 0] / ranks,
        ]
    )
    if ranks == 2:
        vectors = vectors + lax.ppermute(vectors, ("mph", "mpl"), [(0, 1), (1, 0)])
    else:
        vectors = lax.psum(vectors, ("mph", "mpl"))
    gains = vectors[:3] / norm_gains.astype(F32)
    grad_table = packed[:entries, 1 : 1 + heads]

    return (
        mixed[None],
        final_rows[None],
        regroup(input_grad.astype(BF16), False).astype(F32)[None],
        gains,
        vectors[3],
        grad_table,
        grad_tin.astype(F32).reshape(shard, 4, local_w),
        grad_tout.T.astype(F32).reshape(2, local_w, shard),
        grad_sin.astype(F32).reshape(shard, 4, local_w),
        grad_sout.T.astype(F32).reshape(2, local_w, shard),
        grad_up.astype(F32),
        grad_down.T.astype(F32),
    )


def solution(mesh):
    devs = mesh.devices
    dp_n, mp_n = devs.shape
    fine = jax.sharding.Mesh(
        devs.reshape(dp_n // 2, 2, 2, mp_n // 2), ("dph", "core", "mph", "mpl")
    )
    dp, mp = ("dph", "core"), ("mph", "mpl")
    weights = (
        P(None, dp),
        P(dp),
        P(dp, mp),
        P(dp, None, mp),
        P(None, mp, dp),
        P(dp, None, mp),
        P(None, mp, dp),
        P(dp, mp),
        P(mp, dp),
    )
    rows = P(dp, mp, None)
    return jax.shard_map(
        local,
        mesh=fine,
        in_specs=(rows, P(dp), rows, rows) + weights,
        out_specs=(rows, rows, rows) + weights,
        check_vma=False,
    )
```

```python
import functools

import jax
import jax.numpy as jnp
from jax import lax
from jax.experimental import pallas as pl
from jax.experimental.pallas import tpu as pltpu
from jax.sharding import PartitionSpec as P

HD = 128
S = 512
W = 512
TILE = 128
EXTRA = 128

EPS = 1e-06
NEG = -1e30
THRESH = (12, 16, 23, 32, 46, 64, 91)
LOG2E = 1.4426950408889634
SCALE = HD ** (-0.5)
SCALE2 = SCALE * LOG2E
VMEM_BYTES = 60 * 1024 * 1024

GRP = ("mpl", "core")
ORIG_DP = ("dph", "core")
SWAP = ("core", "mph", "mpl")

F32 = jnp.float32
BF16 = jnp.bfloat16


def regroup(arr, forward):
    ranks = lax.axis_size(("mph", "mpl"))
    half = ranks // 2
    pairs = []
    for seq in range(2):
        for rank in range(ranks):
            here = seq * ranks + rank
            there = (rank % 2) * ranks + seq * half + rank // 2
            if here != there:
                pairs.append((here, there) if forward else (there, here))
    moved = lax.ppermute(arr, SWAP, pairs)
    seq, rank = lax.axis_index("core"), lax.axis_index(("mph", "mpl"))
    stays = (rank % 2 == seq) & (rank == seq * half + rank // 2)
    return jnp.where(stays, arr, moved)


def shift(arr, step):
    half = lax.axis_size("mpl")
    size = 2 * half

    def place(rank):
        return (rank % 2) * half + rank // 2

    pairs = [(place(i), place((i + step) % size)) for i in range(size)]
    return lax.ppermute(arr, ("core", "mpl"), pairs)


def gather_rot(rows):
    size = lax.axis_size(GRP)
    return jnp.concatenate([rows] + [shift(rows, -k) for k in range(1, size)], 0)


def sum_rot(term, count):
    size = lax.axis_size(GRP)
    sent = [shift(term(k * count, count).astype(BF16), k) for k in range(1, size)]
    total = term(0, count)
    for piece in sent:
        total = total + piece.astype(F32)
    return total


def dot_nn(left, right):
    return lax.dot_general(left, right, (((1,), (0,)), ((), ())), preferred_element_type=F32)


def dot_tn(left, right):
    return lax.dot_general(left, right, (((0,), (0,)), ((), ())), preferred_element_type=F32)


def dot_nt(left, right):
    return lax.dot_general(left, right, (((1,), (1,)), ((), ())), preferred_element_type=F32)


def normalize(values):
    center = values - jnp.mean(values, -1, keepdims=True)
    spread = jnp.mean(center * center, -1, keepdims=True)
    inv = lax.rsqrt(spread + EPS)
    return center * inv, inv


def norm_back(grad, gain, unit, inv):
    scaled = grad * gain
    mean_g = jnp.mean(scaled, -1, keepdims=True)
    mean_x = jnp.mean(scaled * unit, -1, keepdims=True)
    return inv * (scaled - mean_g - unit * mean_x)


def bucket_of(offset, half):
    distance = jnp.abs(offset)
    far_part = jnp.full(offset.shape, 8, jnp.int32)
    for limit in THRESH:
        far_part = far_part + (distance >= limit).astype(jnp.int32)
    magnitude = jnp.where(distance < 8, distance, far_part)
    return magnitude + half * (offset > 0).astype(jnp.int32)


def near_bias(table):
    entries, heads = table.shape
    diag = lax.broadcasted_iota(jnp.int32, (3, TILE, TILE), 0) - 1
    key_pos = lax.broadcasted_iota(jnp.int32, (3, TILE, TILE), 1)
    query_pos = lax.broadcasted_iota(jnp.int32, (3, TILE, TILE), 2)
    which = bucket_of(diag * TILE + key_pos - query_pos, entries // 2)
    near = jnp.zeros((heads, 3, TILE, TILE), F32)
    for entry in range(entries):
        near = jnp.where((which == entry)[None], table[entry][:, None, None, None], near)
    far = jnp.stack([table[entries // 2 - 1], table[entries - 1]], 1)
    far = jnp.broadcast_to(far[:, :, None, None], (heads, 2, TILE, TILE))
    return jnp.concatenate([near, far], 1)


def tile_slot(kt, qt):
    diag = kt - W // TILE - qt
    return diag + 1 if -1 <= diag <= 1 else (3 if diag < 0 else 4)


def fill_bias(near, bias):
    for h in range(near.shape[0]):
        for kt in range(2 * W // TILE):
            for qt in range(W // TILE):
                bias[h, kt * TILE : (kt + 1) * TILE, qt * TILE : (qt + 1) * TILE] = near[
                    h, tile_slot(kt, qt)
                ]


def table_grad(cells, entries):
    heads = cells.shape[0]
    diag = lax.broadcasted_iota(jnp.int32, (3, TILE, TILE), 0) - 1
    key_pos = lax.broadcasted_iota(jnp.int32, (3, TILE, TILE), 1)
    query_pos = lax.broadcasted_iota(jnp.int32, (3, TILE, TILE), 2)
    which = bucket_of(diag * TILE + key_pos - query_pos, entries // 2)
    rows = lax.broadcasted_iota(jnp.int32, (entries, 1, 1, 1), 0)
    hot = (which[None] == rows).astype(F32)
    near = jnp.stack(
        [jnp.sum(hot * cells[h, :3][None], (1, 2, 3)) for h in range(heads)], 1
    )
    far = jnp.sum(cells[:, 3:], (2, 3))
    entry = lax.broadcasted_iota(jnp.int32, (entries, heads), 0)
    left = jnp.where(entry == entries // 2 - 1, far[:, 0][None], 0.0)
    right = jnp.where(entry == entries - 1, far[:, 1][None], 0.0)
    return near + left + right


def reach_of(block, prefix):
    query = block * W + lax.broadcasted_iota(jnp.int32, (1, W), 1)
    return jnp.where(query < prefix, jnp.maximum(query, prefix - 1), query)


def allowed_keys(block, prefix):
    key = block * W + lax.broadcasted_iota(jnp.int32, (W, W), 0)
    return key <= reach_of(block, prefix)


def soft_unit(logits, values):
    top = jnp.max(logits[0], 0, keepdims=True)
    for part in logits[1:]:
        top = jnp.maximum(top, jnp.max(part, 0, keepdims=True))
    total = None
    acc = None
    for part, vals in zip(logits, values):
        expo = jnp.exp2(part - top)
        summed = jnp.sum(expo, 0, keepdims=True)
        mixed = dot_tn(vals, expo.astype(BF16))
        total = summed if total is None else total + summed
        acc = mixed if acc is None else acc + mixed
    return jnp.transpose(acc / total).astype(BF16), top + jnp.log2(total)


def row_dot(grad_out, out):
    prod = grad_out.astype(F32) * out.astype(F32)
    return jnp.sum(jnp.transpose(prod), 0, keepdims=True)


def back_unit(logits, queries, keys, values, grad_out, lse, delta):
    probs = jnp.exp2(logits - lse)
    grad_probs = dot_nt(values, grad_out)
    grad_values = dot_nn(probs.astype(BF16), grad_out)
    grad_scores = probs * (grad_probs - delta)
    low = grad_scores.astype(BF16)
    grad_keys = dot_nn(low, queries) * SCALE
    grad_queries = dot_tn(keys, low)
    return grad_queries, grad_keys, grad_values, grad_scores


def self_forward_kernel(where, q, kp, kc, vp, vc, near, out, lse, bias):
    block = pl.program_id(0)

    @pl.when(block == 0)
    def _():
        fill_bias(near, bias)

    edge = jnp.where(block == 0, NEG, 0.0)
    allowed = allowed_keys(block, where[1])
    for h in range(bias.shape[0]):
        cols = slice(h * HD, (h + 1) * HD)
        before = dot_nt(kp[:, cols], q[:, cols]) * SCALE2 + (bias[h, :W] + edge)
        here = jnp.where(allowed, dot_nt(kc[:, cols], q[:, cols]) * SCALE2 + bias[h, W:], NEG)
        out[:, cols], lse[0, h : h + 1] = soft_unit(
            (before, here), (vp[:, cols], vc[:, cols])
        )


def self_specs(blocks, local_w, order):
    def at(part, delta):
        def index(i, where):
            block = jnp.maximum(order(i) + delta, 0)
            return ((block + blocks - where[0]) % blocks, part)

        return pl.BlockSpec((W, local_w), index)

    return at


def self_forward(where, proj, near):
    seq_len, width = proj.shape
    local_w = width // 4
    heads = near.shape[0]
    blocks = seq_len // W
    at = self_specs(blocks, local_w, lambda i: i)
    return pl.pallas_call(
        self_forward_kernel,
        grid_spec=pltpu.PrefetchScalarGridSpec(
            num_scalar_prefetch=1,
            grid=(blocks,),
            in_specs=[
                at(0, 0),
                at(2, -1),
                at(2, 0),
                at(3, -1),
                at(3, 0),
                pl.BlockSpec(near.shape, lambda i, where: (0, 0, 0, 0)),
            ],
            out_specs=[
                at(0, 0),
                pl.BlockSpec((1, heads, W), lambda i, where: (i, 0, 0)),
            ],
            scratch_shapes=[pltpu.VMEM((heads, 2 * W, W), F32)],
        ),
        out_shape=[
            jax.ShapeDtypeStruct((seq_len, 2 * local_w), BF16),
            jax.ShapeDtypeStruct((blocks, heads, W), F32),
        ],
        compiler_params=pltpu.CompilerParams(vmem_limit_bytes=VMEM_BYTES),
        cost_estimate=pl.CostEstimate(
            flops=seq_len * 2 * W * local_w * 4,
            bytes_accessed=seq_len * local_w * 12,
            transcendentals=seq_len * 2 * W * heads,
        ),
        name="self_forward",
    )(where, proj, proj, proj, proj, proj, near)


def self_backward_kernel(top, where, q, kp, kc, vp, vc, near, dout, lse, aux, *refs):
    grad_proj, cells, carry, bias = refs[-4:]
    step = pl.program_id(0)
    block = top - step
    edge = jnp.where(block == 0, NEG, 0.0)
    allowed = allowed_keys(block, where[1])
    heads = bias.shape[0]
    local_w = heads * HD
    tiles = W // TILE

    @pl.when(step == 0)
    def _():
        fill_bias(near, bias)
        if len(refs) > 4:
            cells[...] = refs[1][...]
            carry[...] = refs[2][...]
        else:
            carry[...] = jnp.zeros_like(carry)
            cells[...] = jnp.zeros_like(cells)

    for h in range(heads):
        cols = slice(h * HD, (h + 1) * HD)
        vcols = slice(local_w + h * HD, local_w + (h + 1) * HD)
        row_lse = lse[0, h : h + 1]
        before = dot_nt(kp[:, cols], q[:, cols]) * SCALE2 + (bias[h, :W] + edge)
        here = jnp.where(allowed, dot_nt(kc[:, cols], q[:, cols]) * SCALE2 + bias[h, W:], NEG)
        probs0, probs1 = jnp.exp2(before - row_lse), jnp.exp2(here - row_lse)
        prod0 = probs0 * dot_nt(vp[:, cols], dout[:, cols])
        prod1 = probs1 * dot_nt(vc[:, cols], dout[:, cols])
        delta = jnp.sum(prod0, 0, keepdims=True) + jnp.sum(prod1, 0, keepdims=True)
        ds0 = (prod0 - probs0 * delta).astype(BF16)
        ds1 = (prod1 - probs1 * delta).astype(BF16)
        dv0 = dot_nn(probs0.astype(BF16), dout[:, cols])
        dv1 = dot_nn(probs1.astype(BF16), dout[:, cols])
        dk0 = dot_nn(ds0, q[:, cols]) * SCALE
        dk1 = dot_nn(ds1, q[:, cols]) * SCALE
        dq = dot_tn(kp[:, cols], ds0) + dot_tn(kc[:, cols], ds1)
        parts = {0: [], 1: [], 2: [], 3: [], 4: []}
        for kt in range(2 * tiles):
            for qt in range(tiles):
                source, row = (ds0, kt) if kt < tiles else (ds1, kt - tiles)
                cell = source[row * TILE : (row + 1) * TILE, qt * TILE : (qt + 1) * TILE]
                cell = cell.astype(F32)
                parts[tile_slot(kt, qt)].append(cell)
        for slot, group in parts.items():
            cells[h, slot] += functools.reduce(jnp.add, group)
        grad_proj[:, cols] = (jnp.transpose(dq) * SCALE).astype(BF16)
        grad_proj[:, local_w + h * HD : local_w + (h + 1) * HD] = aux[:, cols]
        grad_proj[:, 2 * local_w + h * HD : 2 * local_w + (h + 1) * HD] = (
            dk1 + carry[:, cols] + aux[:, vcols].astype(F32)
        ).astype(BF16)
        grad_proj[:, 3 * local_w + h * HD : 3 * local_w + (h + 1) * HD] = (
            dv1
            + carry[:, vcols]
            + aux[:, 2 * local_w + h * HD : 2 * local_w + (h + 1) * HD].astype(F32)
        ).astype(BF16)
        carry[:, cols] = dk0
        carry[:, vcols] = dv0


def self_backward(top, steps, where, proj, near, grad_att, lse, aux, *kept):
    seq_len, width = proj.shape
    local_w = width // 4
    heads = near.shape[0]
    blocks = seq_len // W

    def order(i):
        return top - i

    at = self_specs(blocks, local_w, order)

    def whole(i, where):
        return ((order(i) + blocks - where[0]) % blocks, 0)

    cell_spec = pl.BlockSpec((heads, 5, TILE, TILE), lambda i, where: (0, 0, 0, 0))
    carry_spec = pl.BlockSpec((W, 2 * local_w), lambda i, where: (0, 0))
    return pl.pallas_call(
        functools.partial(self_backward_kernel, top),
        grid_spec=pltpu.PrefetchScalarGridSpec(
            num_scalar_prefetch=1,
            grid=(steps,),
            in_specs=[
                at(0, 0),
                at(2, -1),
                at(2, 0),
                at(3, -1),
                at(3, 0),
                pl.BlockSpec(near.shape, lambda i, where: (0, 0, 0, 0)),
                at(0, 0),
                pl.BlockSpec((1, heads, W), lambda i, where: (order(i), 0, 0)),
                pl.BlockSpec((W, 3 * local_w), whole),
            ]
            + ([pl.BlockSpec(memory_space=pl.ANY), cell_spec, carry_spec] if kept else []),
            out_specs=[pl.BlockSpec((W, width), whole), cell_spec, carry_spec],
            scratch_shapes=[pltpu.VMEM((heads, 2 * W, W), F32)],
        ),
        out_shape=[
            jax.ShapeDtypeStruct((seq_len, width), BF16),
            jax.ShapeDtypeStruct((heads, 5, TILE, TILE), F32),
            jax.ShapeDtypeStruct((W, 2 * local_w), F32),
        ],
        input_output_aliases={10: 0} if kept else {},
        compiler_params=pltpu.CompilerParams(vmem_limit_bytes=VMEM_BYTES),
        cost_estimate=pl.CostEstimate(
            flops=steps * W * 2 * W * local_w * 20,
            bytes_accessed=steps * W * local_w * 30,
            transcendentals=steps * W * 2 * W * heads,
        ),
        name="self_backward_second" if kept else "self_backward_first",
    )(where, proj, proj, proj, proj, proj, near, grad_att, lse, aux, *kept)


def state_forward_kernel(first, where, *refs):
    refs = list(refs)
    prev = refs.pop(0)
    if not first:
        mine, theirs = refs.pop(0), refs.pop(0)
    gain, gate, w_in, w_out, cq, kc, vc = refs[:7]
    state, norm, sproj, satt, att, lse, part = refs[-7:]
    local_w = cq.shape[1]
    heads = local_w // HD
    if first:
        fresh = prev[...]
    else:
        update = mine[...].astype(F32) + theirs[...].astype(F32)
        fresh = gate[...] * prev[...] + (1.0 - gate[...]) * update
    state[...] = fresh
    unit, _ = normalize(fresh)
    normed = (unit * gain[...]).astype(BF16)
    norm[...] = normed
    for p in range(4):
        cols = slice(p * local_w, (p + 1) * local_w)
        sproj[:, cols] = dot_nn(normed, w_in[:, cols]).astype(BF16)
    for h in range(heads):
        cols = [slice(p * local_w + h * HD, p * local_w + (h + 1) * HD) for p in range(4)]
        sk, sv = sproj[:, cols[2]], sproj[:, cols[3]]
        satt[:, cols[0]], lse[0, h : h + 1] = soft_unit(
            (dot_nt(sk, sproj[:, cols[0]]) * SCALE2,), (sv,)
        )
        satt[:, cols[1]], lse[0, heads + h : heads + h + 1] = soft_unit(
            (dot_nt(kc[:, cols[0]], sproj[:, cols[1]]) * SCALE2,), (vc[:, cols[0]],)
        )
        att[:, cols[0]], lse[0, 2 * heads + h : 2 * heads + h + 1] = soft_unit(
            (dot_nt(sk, cq[:, cols[0]]) * SCALE2,), (sv,)
        )
    part[...] = dot_nt(satt[...], w_out[...]).astype(BF16)


def state_forward(where, block, prev, mine, theirs, gain, gate, w_in, w_out, proj, kept, att):
    first = block == 0
    seq_len, width = proj.shape
    local_w = width // 4
    heads = local_w // HD
    blocks = seq_len // W
    model = prev.shape[1]

    def phys(part):
        return pl.BlockSpec(
            (W, local_w), lambda i, where: ((where[2] + blocks - where[0]) % blocks, part)
        )

    def full(arr):
        return pl.BlockSpec(arr.shape, lambda i, where: (0,) * arr.ndim)

    def row_block(cols):
        return pl.BlockSpec((S, cols), lambda i, where: (where[2], 0))

    anywhere = pl.BlockSpec(memory_space=pl.ANY)
    operands = [prev] + ([] if first else [mine, theirs]) + [gain, gate, w_in, w_out]
    in_specs = [full(arr) for arr in operands] + [phys(1), phys(2), phys(3)]
    operands += [proj, proj, proj]
    aliases = {}
    held = [] if first else list(kept[:3])
    for slot, arr in enumerate(held):
        aliases[1 + len(operands)] = 1 + slot
        operands.append(arr)
        in_specs.append(anywhere)
    aliases[1 + len(operands)] = 4
    operands.append(att)
    in_specs.append(anywhere)
    if not first:
        aliases[1 + len(operands)] = 5
        operands.append(kept[3])
        in_specs.append(anywhere)
    return pl.pallas_call(
        functools.partial(state_forward_kernel, first),
        grid_spec=pltpu.PrefetchScalarGridSpec(
            num_scalar_prefetch=1,
            grid=(1,),
            in_specs=in_specs,
            out_specs=[
                full(prev),
                row_block(model),
                row_block(width),
                row_block(2 * local_w),
                phys(1),
                pl.BlockSpec((1, 3 * heads, S), lambda i, where: (where[2], 0, 0)),
                full(prev),
            ],
        ),
        out_shape=[
            jax.ShapeDtypeStruct(prev.shape, F32),
            jax.ShapeDtypeStruct((blocks * S, model), BF16),
            jax.ShapeDtypeStruct((blocks * S, width), BF16),
            jax.ShapeDtypeStruct((blocks * S, 2 * local_w), BF16),
            jax.ShapeDtypeStruct(att.shape, BF16),
            jax.ShapeDtypeStruct((blocks, 3 * heads, S), F32),
            jax.ShapeDtypeStruct(prev.shape, BF16),
        ],
        input_output_aliases=aliases,
        compiler_params=pltpu.CompilerParams(vmem_limit_bytes=VMEM_BYTES),
        cost_estimate=pl.CostEstimate(
            flops=S * model * local_w * 12 + 3 * S * W * local_w * 4,
            bytes_accessed=(w_in.size + w_out.size) * 2 + S * model * 20,
            transcendentals=3 * S * W * heads,
        ),
        name="state_forward",
    )(where, *operands)


def state_backward_kernel(last, where, *refs):
    refs = list(refs)
    if not last:
        later, mine, theirs, state_next, upd_mine, upd_theirs = refs[:6]
        refs = refs[6:]
    state, gain, gate, w_in, w_out, cq, kc, vc, dcross, cross, sproj, satt, lse = refs[:13]
    dstate, dupd, dsproj, aux, sums, part = refs[-6:]
    local_w = cq.shape[1]
    heads = local_w // HD
    model = state.shape[1]
    gate_f = gate[...]
    if last:
        dstate[...] = jnp.zeros_like(dstate)
        dupd[...] = jnp.zeros_like(dupd)
        gate_sum = jnp.zeros((1, model), F32)
    else:
        unit, inv = normalize(state_next[...])
        grad_norm = mine[...].astype(F32) + theirs[...].astype(F32)
        grad_state = gate_f * later[...] + norm_back(grad_norm, gain[...], unit, inv)
        dstate[...] = grad_state
        update = upd_mine[...].astype(F32) + upd_theirs[...].astype(F32)
        gate_sum = jnp.sum(grad_state * (state[...] - update), 0, keepdims=True)
        gate_sum = gate_sum * gate_f * (1.0 - gate_f)
        dupd[...] = ((1.0 - gate_f) * grad_state).astype(BF16)
    for h in range(heads):
        cols = [slice(p * local_w + h * HD, p * local_w + (h + 1) * HD) for p in range(4)]
        head = cols[0]
        sk, sv = sproj[:, cols[2]], sproj[:, cols[3]]
        delta = row_dot(dcross[:, head], cross[:, head])
        dq, dk, dv, _ = back_unit(
            dot_nt(sk, cq[:, head]) * SCALE2,
            cq[:, head],
            sk,
            sv,
            dcross[:, head],
            lse[0, 2 * heads + h : 2 * heads + h + 1],
            delta,
        )
        aux[:, cols[0]] = (jnp.transpose(dq) * SCALE).astype(BF16)
        if last:
            aux[:, cols[1]] = jnp.zeros((S, HD), BF16)
            aux[:, cols[2]] = jnp.zeros((S, HD), BF16)
            dsproj[:, cols[0]] = jnp.zeros((S, HD), BF16)
            dsproj[:, cols[1]] = jnp.zeros((S, HD), BF16)
        else:
            dself = dot_nn(dupd[...], w_out[:, cols[0]]).astype(BF16)
            dext = dot_nn(dupd[...], w_out[:, cols[1]]).astype(BF16)
            sq = sproj[:, cols[0]]
            dq, dk_s, dv_s, _ = back_unit(
                dot_nt(sk, sq) * SCALE2,
                sq,
                sk,
                sv,
                dself,
                lse[0, h : h + 1],
                row_dot(dself, satt[:, cols[0]]),
            )
            dsproj[:, cols[0]] = (jnp.transpose(dq) * SCALE).astype(BF16)
            dk = dk + dk_s
            dv = dv + dv_s
            sx = sproj[:, cols[1]]
            dq, dk_x, dv_x, _ = back_unit(
                dot_nt(kc[:, head], sx) * SCALE2,
                sx,
                kc[:, head],
                vc[:, head],
                dext,
                lse[0, heads + h : heads + h + 1],
                row_dot(dext, satt[:, cols[1]]),
            )
            dsproj[:, cols[1]] = (jnp.transpose(dq) * SCALE).astype(BF16)
            aux[:, cols[1]] = dk_x.astype(BF16)
            aux[:, cols[2]] = dv_x.astype(BF16)
        dsproj[:, cols[2]] = dk.astype(BF16)
        dsproj[:, cols[3]] = dv.astype(BF16)
    part[...] = dot_nt(dsproj[...], w_in[...]).astype(BF16)
    sums[...] = jnp.broadcast_to(gate_sum, sums.shape)


def state_backward(
    where, block, chain, state, gain, gate, w_in, w_out, proj, grad_att, att, sproj, satt, lse, kept
):
    seq_len, width = proj.shape
    local_w = width // 4
    heads = local_w // HD
    blocks = seq_len // W
    last = block == blocks - 1
    model = state.shape[1]

    def phys(part):
        return pl.BlockSpec(
            (W, local_w), lambda i, where: ((where[2] + blocks - where[0]) % blocks, part)
        )

    def full(arr):
        return pl.BlockSpec(arr.shape, lambda i, where: (0,) * arr.ndim)

    def row_block(cols):
        return pl.BlockSpec((S, cols), lambda i, where: (where[2], 0))

    anywhere = pl.BlockSpec(memory_space=pl.ANY)
    operands = ([] if last else list(chain)) + [state, gain, gate, w_in, w_out]
    in_specs = [full(arr) for arr in operands]
    operands += [proj, proj, proj, grad_att, att, sproj, satt, lse]
    in_specs += [phys(1), phys(2), phys(3), phys(1), phys(1)]
    in_specs += [row_block(width), row_block(2 * local_w)]
    in_specs += [pl.BlockSpec((1, 3 * heads, S), lambda i, where: (where[2], 0, 0))]
    aliases = {}
    if not last:
        for slot, arr in enumerate(kept):
            aliases[1 + len(operands)] = 1 + slot
            operands.append(arr)
            in_specs.append(anywhere)
    return pl.pallas_call(
        functools.partial(state_backward_kernel, last),
        grid_spec=pltpu.PrefetchScalarGridSpec(
            num_scalar_prefetch=1,
            grid=(1,),
            in_specs=in_specs,
            out_specs=[
                full(state),
                row_block(model),
                row_block(width),
                pl.BlockSpec(
                    (W, 3 * local_w),
                    lambda i, where: ((where[2] + blocks - where[0]) % blocks, 0),
                ),
                pl.BlockSpec((8, model), lambda i, where: (0, 0)),
                full(state),
            ],
        ),
        out_shape=[
            jax.ShapeDtypeStruct(state.shape, F32),
            jax.ShapeDtypeStruct((blocks * S, model), BF16),
            jax.ShapeDtypeStruct((blocks * S, width), BF16),
            jax.ShapeDtypeStruct((seq_len, 3 * local_w), BF16),
            jax.ShapeDtypeStruct((8, model), F32),
            jax.ShapeDtypeStruct(state.shape, BF16),
        ],
        input_output_aliases=aliases,
        compiler_params=pltpu.CompilerParams(vmem_limit_bytes=VMEM_BYTES),
        cost_estimate=pl.CostEstimate(
            flops=S * model * local_w * 12 + 3 * S * W * local_w * 10,
            bytes_accessed=(w_in.size + w_out.size) * 2 + S * model * 40,
            transcendentals=3 * S * W * heads,
        ),
        name="state_backward",
    )(where, *operands)


def partner_copy(send, recv, sems, slot):
    other = {"core": 1 - lax.axis_index("core")}
    return pltpu.make_async_remote_copy(
        src_ref=send.at[slot],
        dst_ref=recv.at[slot],
        send_sem=sems.at[0, slot],
        recv_sem=sems.at[1, slot],
        device_id=other,
        device_id_type=pl.DeviceIdType.MESH,
    )


def greet():
    barrier = pltpu.get_barrier_semaphore()
    other = {"core": 1 - lax.axis_index("core")}
    pl.semaphore_signal(barrier, inc=1, device_id=other, device_id_type=pl.DeviceIdType.MESH)
    pl.semaphore_wait(barrier, 1)


def chain_forward_kernel(
    state0,
    gain,
    gate,
    w_in,
    w_out,
    cq,
    kc,
    vc,
    held,
    states,
    norm,
    sproj,
    satt,
    att,
    lse,
    final,
    state,
    send,
    recv,
    sems,
):
    step = pl.program_id(0)
    steps = pl.num_programs(0)
    slot = lax.rem(step, 2)
    before = lax.rem(step + 1, 2)
    local_w = cq.shape[1]
    heads = local_w // HD

    @pl.when(step == 0)
    def _():
        greet()
        state[...] = state0[...]

    @pl.when(step > 0)
    def _():
        partner_copy(send, recv, sems, before).wait()
        update = send[before].astype(F32) + recv[before].astype(F32)
        state[...] = gate[...] * state[...] + (1.0 - gate[...]) * update

    fresh = state[...]
    states[...] = fresh
    unit, _ = normalize(fresh)
    normed = (unit * gain[...]).astype(BF16)
    norm[...] = normed
    for p in range(4):
        cols = slice(p * local_w, (p + 1) * local_w)
        sproj[:, cols] = dot_nn(normed, w_in[:, cols]).astype(BF16)
    for h in range(heads):
        cols = [slice(p * local_w + h * HD, p * local_w + (h + 1) * HD) for p in range(4)]
        sk, sv = sproj[:, cols[2]], sproj[:, cols[3]]
        satt[:, cols[0]], lse[0, h : h + 1] = soft_unit(
            (dot_nt(sk, sproj[:, cols[0]]) * SCALE2,), (sv,)
        )
        satt[:, cols[1]], lse[0, heads + h : heads + h + 1] = soft_unit(
            (dot_nt(kc[:, cols[0]], sproj[:, cols[1]]) * SCALE2,), (vc[:, cols[0]],)
        )
    send[slot] = dot_nt(satt[...], w_out[...]).astype(BF16)
    copy = partner_copy(send, recv, sems, slot)
    copy.start()
    for h in range(heads):
        cols = [slice(p * local_w + h * HD, p * local_w + (h + 1) * HD) for p in range(4)]
        sk, sv = sproj[:, cols[2]], sproj[:, cols[3]]
        att[:, cols[0]], lse[0, 2 * heads + h : 2 * heads + h + 1] = soft_unit(
            (dot_nt(sk, cq[:, cols[0]]) * SCALE2,), (sv,)
        )

    @pl.when(step == steps - 1)
    def _():
        copy.wait()
        update = send[slot].astype(F32) + recv[slot].astype(F32)
        final[...] = gate[...] * state[...] + (1.0 - gate[...]) * update


def rotated(block, blocks, local_blocks, part):
    return (lax.rem(block + blocks - lax.axis_index("core") * local_blocks, blocks), part)


def chain_forward(state0, gain, gate, w_in, w_out, proj, att):
    seq_len, width = proj.shape
    local_w = width // 4
    heads = local_w // HD
    blocks = seq_len // W
    local_blocks = blocks // 2
    model = state0.shape[1]

    def phys(part):
        return pl.BlockSpec((W, local_w), lambda i: rotated(i, blocks, local_blocks, part))

    def full(arr):
        return pl.BlockSpec(arr.shape, lambda i: (0,) * arr.ndim, pipeline_mode=pl.Buffered(1))

    def row_block(cols):
        return pl.BlockSpec((S, cols), lambda i: (i, 0))

    return pl.pallas_call(
        chain_forward_kernel,
        grid=(blocks,),
        in_specs=[full(arr) for arr in (state0, gain, gate, w_in, w_out)]
        + [phys(1), phys(2), phys(3), pl.BlockSpec(memory_space=pl.ANY)],
        out_specs=[
            row_block(model),
            row_block(model),
            row_block(width),
            row_block(2 * local_w),
            phys(1),
            pl.BlockSpec((1, 3 * heads, S), lambda i: (i, 0, 0)),
            pl.BlockSpec((S, model), lambda i: (0, 0)),
        ],
        out_shape=[
            jax.ShapeDtypeStruct((blocks * S, model), F32),
            jax.ShapeDtypeStruct((blocks * S, model), BF16),
            jax.ShapeDtypeStruct((blocks * S, width), BF16),
            jax.ShapeDtypeStruct((blocks * S, 2 * local_w), BF16),
            jax.ShapeDtypeStruct(att.shape, BF16),
            jax.ShapeDtypeStruct((blocks, 3 * heads, S), F32),
            jax.ShapeDtypeStruct((S, model), F32),
        ],
        scratch_shapes=[
            pltpu.VMEM((S, model), F32),
            pltpu.VMEM((2, S, model), BF16),
            pltpu.VMEM((2, S, model), BF16),
            pltpu.SemaphoreType.DMA((2, 2)),
        ],
        input_output_aliases={8: 4},
        compiler_params=pltpu.CompilerParams(
            vmem_limit_bytes=VMEM_BYTES, collective_id=0, has_side_effects=True
        ),
        cost_estimate=pl.CostEstimate(
            flops=blocks * (S * model * local_w * 12 + 3 * S * W * local_w * 8),
            bytes_accessed=blocks * S * model * 12,
            transcendentals=blocks * 3 * S * W * heads,
        ),
        name="chain_forward",
    )(state0, gain, gate, w_in, w_out, proj, proj, proj, att)


def chain_backward_kernel(top, steps, start, *refs):
    refs = list(refs)
    later = None if start else refs.pop(0)
    state, state_next, gain, gate, w_in, w_out, cq, kc, vc, dcross, cross, sproj, satt, lse = refs[
        :14
    ]
    refs = refs[14:] if start else refs[17:]
    dupd, dsproj, aux, sums, leave, dstate, dkv, send, recv, sems = refs
    step = pl.program_id(0)
    slot = lax.rem(step, 2)
    before = lax.rem(step + 1, 2)
    local_w = cq.shape[1]
    heads = local_w // HD
    gate_f = gate[...]
    finish = top - steps + 1 == 0

    def absorb(where, at):
        grad_norm = send[where].astype(F32) + recv[where].astype(F32)
        unit, inv = normalize(at[...])
        dstate[...] = gate_f * dstate[...] + norm_back(grad_norm, gain[...], unit, inv)

    @pl.when(step == 0)
    def _():
        greet()
        sums[...] = jnp.zeros_like(sums)
        dstate[...] = jnp.zeros_like(dstate) if start else later[...]

    for h in range(heads):
        cols = [slice(p * local_w + h * HD, p * local_w + (h + 1) * HD) for p in range(4)]
        head = cols[0]
        sk, sv = sproj[:, cols[2]], sproj[:, cols[3]]
        dq, dk, dv, _ = back_unit(
            dot_nt(sk, cq[:, head]) * SCALE2,
            cq[:, head],
            sk,
            sv,
            dcross[:, head],
            lse[0, 2 * heads + h : 2 * heads + h + 1],
            row_dot(dcross[:, head], cross[:, head]),
        )
        aux[:, head] = (jnp.transpose(dq) * SCALE).astype(BF16)
        dkv[:, cols[0]] = dk
        dkv[:, cols[1]] = dv

    @pl.when(step > 0)
    def _():
        partner_copy(send, recv, sems, before).wait()
        absorb(before, state_next)

    grad_state = dstate[...]
    change = jnp.sum(grad_state * (state[...] - state_next[...]), 0, keepdims=True)
    sums[...] += jnp.broadcast_to(change * gate_f, sums.shape)
    dupd[...] = ((1.0 - gate_f) * grad_state).astype(BF16)
    for h in range(heads):
        cols = [slice(p * local_w + h * HD, p * local_w + (h + 1) * HD) for p in range(4)]
        head = cols[0]
        sk, sv = sproj[:, cols[2]], sproj[:, cols[3]]
        dself = dot_nn(dupd[...], w_out[:, cols[0]]).astype(BF16)
        dext = dot_nn(dupd[...], w_out[:, cols[1]]).astype(BF16)
        sq = sproj[:, cols[0]]
        dq, dk, dv, _ = back_unit(
            dot_nt(sk, sq) * SCALE2,
            sq,
            sk,
            sv,
            dself,
            lse[0, h : h + 1],
            row_dot(dself, satt[:, cols[0]]),
        )
        dsproj[:, cols[0]] = (jnp.transpose(dq) * SCALE).astype(BF16)
        dsproj[:, cols[2]] = (dk + dkv[:, cols[0]]).astype(BF16)
        dsproj[:, cols[3]] = (dv + dkv[:, cols[1]]).astype(BF16)
        sx = sproj[:, cols[1]]
        dq, dk, dv, _ = back_unit(
            dot_nt(kc[:, head], sx) * SCALE2,
            sx,
            kc[:, head],
            vc[:, head],
            dext,
            lse[0, heads + h : heads + h + 1],
            row_dot(dext, satt[:, cols[1]]),
        )
        dsproj[:, cols[1]] = (jnp.transpose(dq) * SCALE).astype(BF16)
        aux[:, cols[1]] = dk.astype(BF16)
        aux[:, cols[2]] = dv.astype(BF16)

    def pass_on():
        send[slot] = dot_nt(dsproj[...], w_in[...]).astype(BF16)
        partner_copy(send, recv, sems, slot).start()

    if finish:
        pl.when(step < steps - 1)(pass_on)

        @pl.when(step == steps - 1)
        def _():
            leave[...] = jnp.zeros_like(leave)
    else:
        pass_on()

        @pl.when(step == steps - 1)
        def _():
            partner_copy(send, recv, sems, slot).wait()
            absorb(slot, state)
            leave[...] = dstate[...]


def chain_backward(
    top, steps, later, states, gain, gate, w_in, w_out, proj, grad_att, att, sproj, satt, lse, kept
):
    seq_len, width = proj.shape
    local_w = width // 4
    heads = local_w // HD
    blocks = seq_len // W
    local_blocks = blocks // 2
    model = states.shape[1]
    start = later is None

    def phys(part):
        return pl.BlockSpec((W, local_w), lambda i: rotated(top - i, blocks, local_blocks, part))

    def full(arr):
        return pl.BlockSpec(arr.shape, lambda i: (0,) * arr.ndim, pipeline_mode=pl.Buffered(1))

    def row_block(cols):
        return pl.BlockSpec((S, cols), lambda i: (top - i, 0))

    operands = [] if start else [later]
    in_specs = [full(arr) for arr in operands]
    operands += [states, states, gain, gate, w_in, w_out]
    in_specs += [
        row_block(model),
        pl.BlockSpec((S, model), lambda i: (jnp.minimum(top - i + 1, blocks - 1), 0)),
    ]
    in_specs += [full(arr) for arr in operands[-4:]]
    operands += [proj, proj, proj, grad_att, att, sproj, satt, lse]
    in_specs += [phys(1), phys(2), phys(3), phys(1), phys(1)]
    in_specs += [row_block(width), row_block(2 * local_w)]
    in_specs += [pl.BlockSpec((1, 3 * heads, S), lambda i: (top - i, 0, 0))]
    aliases = {}
    if not start:
        for place, arr in enumerate(kept):
            aliases[len(operands)] = place
            operands.append(arr)
            in_specs.append(pl.BlockSpec(memory_space=pl.ANY))
    return pl.pallas_call(
        functools.partial(chain_backward_kernel, top, steps, start),
        grid=(steps,),
        in_specs=in_specs,
        out_specs=[
            row_block(model),
            row_block(width),
            pl.BlockSpec((W, 3 * local_w), lambda i: rotated(top - i, blocks, local_blocks, 0)),
            pl.BlockSpec((8, model), lambda i: (0, 0)),
            pl.BlockSpec((S, model), lambda i: (0, 0)),
        ],
        out_shape=[
            jax.ShapeDtypeStruct((blocks * S, model), BF16),
            jax.ShapeDtypeStruct((blocks * S, width), BF16),
            jax.ShapeDtypeStruct((seq_len, 3 * local_w), BF16),
            jax.ShapeDtypeStruct((8, model), F32),
            jax.ShapeDtypeStruct((S, model), F32),
        ],
        scratch_shapes=[
            pltpu.VMEM((S, model), F32),
            pltpu.VMEM((S, 2 * local_w), F32),
            pltpu.VMEM((2, S, model), BF16),
            pltpu.VMEM((2, S, model), BF16),
            pltpu.SemaphoreType.DMA((2, 2)),
        ],
        input_output_aliases=aliases,
        compiler_params=pltpu.CompilerParams(
            vmem_limit_bytes=VMEM_BYTES,
            collective_id=1 if start else 2,
            has_side_effects=True,
        ),
        cost_estimate=pl.CostEstimate(
            flops=steps * (S * model * local_w * 12 + 3 * S * W * local_w * 12),
            bytes_accessed=steps * S * model * 24,
            transcendentals=steps * 3 * S * W * heads,
        ),
        name="chain_backward_first" if start else "chain_backward_second",
    )(*operands)


def up_kernel(rows, weight, act, slope):
    step = min(512, weight.shape[1])
    root = 0.7978845608028654
    for start in range(0, weight.shape[1], step):
        cols = slice(start, start + step)
        pre = dot_nn(rows[...], weight[:, cols])
        square = pre * pre
        half = 0.5 * jnp.tanh(pre * (root + (root * 0.044715) * square)) + 0.5
        value = pre * half
        act[:, cols] = value.astype(BF16)
        rise = 2.0 * root + (6.0 * root * 0.044715) * square
        slope[:, cols] = (half + value * (1.0 - half) * rise).astype(BF16)


def up_project(rows, weight, units):
    count, model = rows.shape
    out = jax.ShapeDtypeStruct((count, units), BF16)
    return pl.pallas_call(
        up_kernel,
        grid=(count // W,),
        in_specs=[
            pl.BlockSpec((W, model), lambda i: (i, 0)),
            pl.BlockSpec((model, units), lambda i: (0, 0)),
        ],
        out_specs=[pl.BlockSpec((W, units), lambda i: (i, 0))] * 2,
        out_shape=[out, out],
        compiler_params=pltpu.CompilerParams(vmem_limit_bytes=VMEM_BYTES),
        cost_estimate=pl.CostEstimate(
            flops=2 * count * model * units,
            bytes_accessed=count * (model + 2 * units) * 2 + model * units * 2,
            transcendentals=count * units,
        ),
        name="up_project",
    )(rows, weight)


def after(value, *others):
    return lax.optimization_barrier((value, *others))


def hold(value, *others):
    for arr in others:
        value = value + (arr[0, 0] * 0).astype(value.dtype)
    return value


def gather_weight(shard):
    if lax.axis_size(("mph", "mpl")) == 2:
        whole = lax.all_gather(shard, ("mph", "mpl") + ORIG_DP, axis=0, tiled=True)
        model = whole.shape[0] // 2
        first = lax.axis_index(GRP) * model
    else:
        whole = regroup(lax.all_gather(shard, ORIG_DP, axis=0, tiled=True), True)
        model, first = whole.shape[0], 0

    def take(start, stop):
        return lax.dynamic_slice(whole, (first, start), (model, stop - start))

    return whole, take


def scatter_moved(moved):
    return lax.psum_scatter(moved, ORIG_DP, scatter_dimension=0, tiled=True)


def local(
    tokens,
    prefix,
    init_state,
    cotangent,
    norm_gains,
    gate_bias,
    rel_table,
    tok_in_proj,
    tok_out_proj,
    st_in_proj,
    st_out_proj,
    mlp_up,
    mlp_down,
):
    rows = tokens.shape[1]
    model = tokens.shape[2]
    size = lax.axis_size(GRP)
    rank = lax.axis_index(GRP)
    seq_len = rows * size
    blocks = seq_len // W
    shard = tok_in_proj.shape[0]
    local_w = tok_in_proj.shape[2]
    heads = rel_table.shape[1]
    units = mlp_up.shape[1]

    small = jnp.concatenate([norm_gains, gate_bias[None]], 0).T
    entries = rel_table.shape[0]
    extra = jnp.zeros((shard, EXTRA), BF16)
    extra = lax.dynamic_update_slice(extra, small, (0, 0))
    extra = lax.dynamic_update_slice(extra, rel_table, (0, 4))
    digits = jnp.stack([prefix // 64, prefix % 64], 1).astype(BF16)
    extra = lax.dynamic_update_slice(extra, digits, (0, 4 + heads))
    tok_rows = regroup(tokens[0], True)
    wide = 4 * local_w
    shard_tin = tok_in_proj.reshape(shard, wide)
    shard_sin = st_in_proj.reshape(shard, wide)
    first, take_first = gather_weight(jnp.concatenate([shard_tin, extra], 1))
    second = jnp.concatenate([shard_sin, st_out_proj.reshape(2 * local_w, shard).T], 1)
    third = jnp.concatenate([mlp_up, tok_out_proj.reshape(2 * local_w, shard).T], 1)
    second, take_second = gather_weight(hold(second, first, tok_rows))
    extra = take_first(wide, wide + EXTRA)
    w_tin = take_first(0, wide)
    small = extra[:, :4].T.astype(F32)
    by_seq = extra.reshape(-1, shard, EXTRA)
    table = by_seq[:, :entries, 4 : 4 + heads].reshape(-1, heads).astype(F32)
    seq = lax.axis_index(("dph", "mph"))
    digits = lax.dynamic_index_in_dim(by_seq[:, 0, 4 + heads : 6 + heads], seq, 0, False)
    digits = digits.astype(jnp.int32)
    prefix_len = digits[0] * 64 + digits[1]
    start = regroup(hold(init_state[0], tok_rows), True)
    if size == 2:
        other = shift(start, 1)
        state0 = jnp.where(
            rank == 0,
            jnp.concatenate([start, other], 0),
            jnp.concatenate([other, start], 0),
        )
    else:
        state0 = lax.all_gather(start, GRP, axis=0, tiled=True)

    gain1, gain2, gain3 = small[0:1], small[1:2], small[2:3]
    gate = jax.nn.sigmoid(small[3:4])
    near = near_bias(table * LOG2E)
    base = jnp.stack([rank.astype(jnp.int32) * (rows // W), prefix_len])

    def where_at(block):
        return jnp.concatenate([base, jnp.full((1,), block, jnp.int32)])

    tok_f = tok_rows.astype(F32)
    unit1, inv1 = normalize(tok_f)
    normed = gather_rot((unit1 * gain1).astype(BF16))
    normed, near, state0 = lax.optimization_barrier((normed, near, state0))
    proj = dot_nn(normed, w_tin).astype(BF16)
    att, lse_tok = self_forward(where_at(0), proj, near)
    third, take_third = gather_weight(hold(third, second, att))
    w_sin, w_sout = take_second(0, wide), take_second(wide, wide + 2 * local_w)
    if size == 2:
        w_sout, cot_rows = after(w_sout, cotangent[0])
        cot_rows = regroup(cot_rows, True)
        outs = chain_forward(state0, gain3, gate, w_sin, w_sout, proj, att)
        states, norm_st, sproj, satt, att, lse_st, final = outs
        att, cot_rows = after(att, cot_rows)
    else:
        cot_rows = regroup(cotangent[0], True)
        states, ups = [], []
        prev, mine, theirs, kept = state0, None, None, None
        for block in range(blocks):
            outs = state_forward(
                where_at(block),
                block,
                prev,
                mine,
                theirs,
                gain3,
                gate,
                w_sin,
                w_sout,
                proj,
                kept,
                att,
            )
            prev, norm_st, sproj, satt, att, lse_st, mine = outs
            kept = (norm_st, sproj, satt, lse_st)
            theirs = lax.psum(mine.astype(F32), GRP) - mine.astype(F32)
            theirs = theirs.astype(BF16)
            states.append(prev)
            ups.append((mine, theirs))
        final = gate * prev + (1.0 - gate) * (mine.astype(F32) + theirs.astype(F32))
    fourth, take_fourth = gather_weight(hold(mlp_down.T, third, att))
    w_up, w_tout = take_third(0, units), take_third(units, units + 2 * local_w)
    w_down = take_fourth(0, units)
    final_rows = lax.dynamic_slice_in_dim(final, rank * (S // size), S // size, 0)
    final_rows = regroup(final_rows, False)

    def attn_term(first, count):
        return dot_nt(lax.slice_in_dim(att, first, first + count, axis=0), w_tout)

    resid = tok_f + sum_rot(attn_term, rows)
    unit2, inv2 = normalize(resid)
    normed2 = gather_rot((unit2 * gain2).astype(BF16))
    act, slope = up_project(normed2, w_up, units)
    act, final_rows = after(act, final_rows)

    def mlp_term(first, count):
        return dot_nt(lax.slice_in_dim(act, first, first + count, axis=0), w_down)

    mixed = (resid + sum_rot(mlp_term, rows)).astype(BF16)

    cot_all = gather_rot(cot_rows)
    grad_pre = (dot_nn(cot_all, w_down) * slope.astype(F32)).astype(BF16)
    grad_down = regroup(dot_tn(cot_all, act).astype(BF16), False)

    def up_term(first, count):
        return dot_nt(lax.slice_in_dim(grad_pre, first, first + count, axis=0), w_up)

    grad_norm2 = sum_rot(up_term, rows)
    grad_up = regroup(dot_tn(normed2, grad_pre).astype(BF16), False)
    grad_resid = cot_rows.astype(F32) + norm_back(grad_norm2, gain2, unit2, inv2)
    grad_attn = gather_rot(grad_resid.astype(BF16))
    grad_att = dot_nn(grad_attn, w_tout).astype(BF16)
    grad_tout = regroup(dot_tn(grad_attn, att).astype(BF16), False)
    grad_att, grad_down = after(grad_att, grad_down)
    grad_down = scatter_moved(grad_down)

    if size == 2:
        half = blocks // 2
        shared = (states, gain3, gate, w_sin, w_sout, proj, grad_att, att, sproj, satt, lse_st)
        dupd, dsproj, aux, sums, later = chain_backward(blocks - 1, half, None, *shared, None)
        later, grad_up, grad_down = after(later, grad_up, grad_down)
        grad_up = scatter_moved(grad_up)
        dupd, dsproj, aux, more, _ = chain_backward(
            half - 1, half, later, *shared, (dupd, dsproj, aux)
        )
        gate_grad = sums[0] + more[0]
        aux, grad_tout = after(aux, grad_tout)
        grad_tout = scatter_moved(grad_tout)
    else:
        grad_up, grad_tout = scatter_moved(grad_up), scatter_moved(grad_tout)
        chain, kept_b, sums = None, None, []
        for block in reversed(range(blocks)):
            outs = state_backward(
                where_at(block),
                block,
                chain,
                states[block],
                gain3,
                gate,
                w_sin,
                w_sout,
                proj,
                grad_att,
                att,
                sproj,
                satt,
                lse_st,
                kept_b,
            )
            later, dupd, dsproj, aux, sum_b, part = outs
            kept_b = (dupd, dsproj, aux)
            sums.append(sum_b)
            if block > 0:
                other = (lax.psum(part.astype(F32), GRP) - part.astype(F32)).astype(BF16)
                chain = (later, part, other, states[block]) + ups[block - 1]
        gate_grad = functools.reduce(jnp.add, sums)[0]
    grad_sout = dot_tn(dupd, satt).astype(BF16)
    grad_sout = regroup(grad_sout, False)
    grad_sin = dot_tn(norm_st, dsproj).astype(BF16)
    aux, grad_sin, grad_sout, grad_up = after(aux, grad_sin, grad_sout, grad_up)
    grad_sout = scatter_moved(grad_sout)
    grad_sin = regroup(grad_sin, False)

    half = blocks // 2
    shared = (where_at(0), proj, near, grad_att, lse_tok, aux)
    grad_proj, cells, carry = self_backward(blocks - 1, half, *shared)
    carry, grad_tout, grad_sin = after(carry, grad_tout, grad_sin)
    grad_sin = scatter_moved(grad_sin)
    grad_proj, cells, _ = self_backward(half - 1, half, *shared, grad_proj, cells, carry)
    grad_proj, grad_sout = after(grad_proj, grad_sout)

    def tok_term(first, count):
        return dot_nt(lax.slice_in_dim(grad_proj, first, first + count, axis=0), w_tin)

    grad_table = table_grad(cells, table.shape[0]).reshape(-1, entries, heads)
    grad_table = jnp.pad(grad_table, ((0, 0), (0, shard - entries), (0, 0)))
    packed = jnp.concatenate([gate_grad[:, None], grad_table.reshape(model, heads)], 1)
    packed = jnp.pad(packed, ((0, 0), (0, EXTRA - 1 - heads))).astype(BF16)
    grad_tin = jnp.concatenate([dot_tn(normed, grad_proj).astype(BF16), packed], 1)
    grad_proj, grad_tin = after(grad_proj, grad_tin)
    grad_tin, mixed = after(regroup(grad_tin, False), mixed)
    mixed = regroup(mixed, False)
    if size == 2:
        sent = shift(tok_term(rows, rows).astype(BF16), 1)
        sent, grad_tin = after(sent, grad_tin)
        grad_norm1 = tok_term(0, rows) + sent.astype(F32)
    else:
        grad_norm1 = sum_rot(tok_term, rows)
    grad_tin = scatter_moved(grad_tin)
    grad_tin, packed = grad_tin[:, :wide], grad_tin[:, wide:].astype(F32)
    input_grad = grad_resid + norm_back(grad_norm1, gain1, unit1, inv1)

    def gain_sum(shard_in, grad):
        return jnp.sum(shard_in.astype(F32) * grad.astype(F32), 1)

    ranks = lax.axis_size(("mph", "mpl"))
    vectors = jnp.stack(
        [
            gain_sum(shard_tin, grad_tin),
            gain_sum(mlp_up, grad_up),
            gain_sum(shard_sin, grad_sin),
            packed[:, 0] / ranks,
        ]
    )
    if ranks == 2:
        vectors = vectors + lax.ppermute(vectors, ("mph", "mpl"), [(0, 1), (1, 0)])
    else:
        vectors = lax.psum(vectors, ("mph", "mpl"))
    gains = vectors[:3] / norm_gains.astype(F32)
    grad_table = packed[:entries, 1 : 1 + heads]

    return (
        mixed[None],
        final_rows[None],
        regroup(input_grad.astype(BF16), False).astype(F32)[None],
        gains,
        vectors[3],
        grad_table,
        grad_tin.astype(F32).reshape(shard, 4, local_w),
        grad_tout.T.astype(F32).reshape(2, local_w, shard),
        grad_sin.astype(F32).reshape(shard, 4, local_w),
        grad_sout.T.astype(F32).reshape(2, local_w, shard),
        grad_up.astype(F32),
        grad_down.T.astype(F32),
    )


def solution(mesh):
    devs = mesh.devices
    dp_n, mp_n = devs.shape
    fine = jax.sharding.Mesh(
        devs.reshape(dp_n // 2, 2, 2, mp_n // 2), ("dph", "core", "mph", "mpl")
    )
    dp, mp = ("dph", "core"), ("mph", "mpl")
    weights = (
        P(None, dp),
        P(dp),
        P(dp, mp),
        P(dp, None, mp),
        P(None, mp, dp),
        P(dp, None, mp),
        P(None, mp, dp),
        P(dp, mp),
        P(mp, dp),
    )
    rows = P(dp, mp, None)
    return jax.shard_map(
        local,
        mesh=fine,
        in_specs=(rows, P(dp), rows, rows) + weights,
        out_specs=(rows, rows, rows) + weights,
        check_vma=False,
    )
```
